32 devices in a mesh: dp: 8 (over z, core), tensor: 4 (over y, x).
Axes of the slice: x: 2, y: 2, z: 4, core: 2. Of those that a mesh axis runs over, the one named last changes fastest.
Arguments:
- tokens: bfloat16 [24576, 1024], P('dp'), may hold values from -6 to 6
- lengths: int32 [24], P('dp'), may hold values from 512 to 1024, as said below
- routes: int32 [24576, 1], P('dp'), may hold values from 0 to 7
- fill_order: int32 [8, 3072], P('dp'), may hold values from 0 to 3071, each once within a row
- norm_gain: float32 [1024], replicated, may hold values from 0.1 to 1.9
- norm_bias: float32 [1024], replicated, may hold values from -3 to 3
- qkv_weight: bfloat16 [1024, 16, 192], P(None, 'tensor'), may hold values from -0.1875 to 0.1875
- out_weight: bfloat16 [16, 64, 1024], P('tensor'), may hold values from -0.75 to 0.75
- centroids: bfloat16 [8, 1024], P('dp'), may hold values from -0.125 to 0.125
- expert_in: bfloat16 [8, 2, 1024, 4096], P('dp', None, None, 'tensor'), may hold values from -0.1875 to 0.1875
- expert_out: bfloat16 [8, 2, 4096, 1024], P('dp', None, 'tensor'), may hold values from -0.09375 to 0.09375
- cotangent: bfloat16 [24576, 1024], P('dp'), may hold values from -6 to 6
Outputs:
- output: bfloat16 [24576, 1024], P('dp')
- grad_tokens: bfloat16 [24576, 1024], P('dp')
- grad_norm_gain: float32 [1024], P('tensor')
- grad_norm_bias: float32 [1024], P('tensor')
- grad_qkv_weight: float32 [1024, 16, 192], P(None, 'tensor')
- grad_out_weight: float32 [16, 64, 1024], P('tensor')
- grad_centroids: float32 [8, 1024], P('dp')
- grad_expert_in: float32 [8, 2, 1024, 4096], P('dp', None, None, 'tensor')
- grad_expert_out: float32 [8, 2, 4096, 1024], P('dp', None, 'tensor')
The draws below stay inside these ranges and needn't reach their ends.
Inputs may be any that keep to these rules, and one draw needn't show every extreme that they name: `lengths`: valid tokens of each sequence; one sequence has exactly 1024 and one exactly 512.
All inputs are finite; a program needn't handle non-finite values.
Results may differ from the reference program's by a relative error of at most 0.015.
Values may be sent and summed in bfloat16 or wider, within the bound.
A program may use at most 448 MiB of HBM per device.

```python
from functools import partial
import jax
import jax.numpy as jnp
from jax import lax

D = 1024
H = 16
HD = 64
FF = 4096
SEQ_DEV = 3
LEN = 1024
TOK_DEV = 3072
SEQS = 24
TOKENS = 24576
GROUPS = 8
EXPERTS = 8
CAP = 432
N_DP = 8


def draw_lengths(key, part):
    first, second, third = jax.random.split(key, 3)
    picked = jax.random.randint(first, (SEQS,), LEN // 2, LEN + 1)
    longest = jax.random.randint(second, (), 0, SEQS)
    shortest = (longest + 1 + jax.random.randint(third, (), 0, SEQS - 1)) % SEQS
    places = jnp.arange(SEQS)
    picked = jnp.where(places == longest, LEN, picked)
    picked = jnp.where(places == shortest, LEN // 2, picked)
    return picked.astype(jnp.int32)


def shard_levels(key, shape, cuts, smallest, high):
    def one(dim, parts):
        draws = jax.random.uniform(jax.random.fold_in(jax.random.fold_in(key, 6), dim), (parts,), jnp.float32, smallest / len(cuts), high / len(cuts))
        return jnp.repeat(jnp.exp(draws), shape[dim] // parts).reshape((-1,) + (1,) * (len(shape) - dim - 1))

    factor_of = one(*cuts[0])
    for cut in cuts[1:]:
        factor_of = factor_of * one(*cut)
    return factor_of


def distinct(stream_key, rows, amount, top, lift):
    order = jax.random.permutation(jax.random.fold_in(stream_key, 1), amount)
    pull = order
    for power in range(3):
        pull = pull * pull // amount
    pull = pull * lift // amount
    tickets = jax.random.randint(jax.random.fold_in(stream_key, 2), (rows, amount), 0, 4096) + pull
    sure = jax.random.permutation(jax.random.fold_in(stream_key, 3), rows)[jnp.arange(amount) % rows]
    tickets = jnp.where(jnp.arange(rows)[:, None] == sure[None, :], 1 << 14, tickets)
    priority = tickets * amount + jnp.arange(amount)
    return lax.top_k(priority.astype(jnp.int32), top)[1].astype(jnp.int32)


def noise(rng, dims, width, bound, cuts=(), kind=jnp.bfloat16):
    gain = shard_levels(rng, dims, cuts, -0.22, 0.18) if cuts else 1.0
    drawn = jax.random.normal(rng, dims, jnp.float32) * width * gain
    return jnp.minimum(jnp.maximum(drawn, -bound), bound).astype(kind)


def setup_inputs(seed: int = 0) -> dict:
    keys = jax.random.split(jax.random.key(seed), 13)
    return {
        "tokens": noise(keys[0], (TOKENS, D), 1.0, 6.0, ((0, 8),)),
        "lengths": draw_lengths(jax.random.fold_in(keys[12], 71), 0),
        "routes": distinct(keys[2], TOKENS, EXPERTS, 1, 2048),
        "fill_order": jax.vmap(lambda own: jax.random.permutation(own, TOK_DEV))(jax.random.split(keys[3], GROUPS)).reshape((GROUPS, TOK_DEV)).astype(jnp.int32),
        "norm_gain": jnp.clip(1.0 + 0.18 * jax.random.normal(keys[4], (D,), jnp.float32), 0.1, 1.9),
        "norm_bias": noise(keys[5], (D,), 0.5, 3.0, (), jnp.float32),
        "qkv_weight": noise(keys[6], (D, H, 3 * HD), D ** -0.5, 0.1875, ((1, 4),)),
        "out_weight": noise(keys[7], (H, HD, D), HD ** -0.5, 0.75, ((0, 4),)),
        "centroids": noise(keys[8], (EXPERTS, D), 0.02, 0.125, ((0, 8),)),
        "expert_in": noise(keys[9], (EXPERTS, 2, D, FF), D ** -0.5, 0.1875, ((0, 8), (3, 4))),
        "expert_out": noise(keys[10], (EXPERTS, 2, FF, D), FF ** -0.5, 0.09375, ((0, 8), (2, 4))),
        "cotangent": noise(keys[11], (TOKENS, D), 1.0, 6.0, ((0, 8),)),
    }


EPSILON = 1e-05
HIGHEST = lax.Precision.HIGHEST

@jax.custom_vjp
def low(v):
    return lax.optimization_barrier(v.astype(jnp.bfloat16)).astype(jnp.float32)

@jax.custom_vjp
def low_back(v):
    return v

def low_keep(v):
    return (low(v), None)

def low_pass(kept, grad):
    return (grad,)

def back_keep(v):
    return (v, None)

def back_low(kept, grad):
    return (low(grad),)
low.defvjp(low_keep, low_pass)
low_back.defvjp(back_keep, back_low)

def plan_slots(routes, order, lengths, seq_len, experts, capacity):
    count = routes.shape[0]
    seq_count = lengths.shape[0]
    places = jnp.arange(count, dtype=jnp.int32)
    limits = jnp.broadcast_to(lengths[:, None], (seq_count, seq_len)).reshape(count)
    is_valid = places % seq_len < limits
    order_row = order.reshape(count).astype(jnp.int32)
    route_sorted = routes.reshape(count)[order_row]
    valid_sorted = is_valid[order_row]
    matches = ((route_sorted[:, None] == jnp.arange(experts, dtype=jnp.int32)[None, :]) & valid_sorted[:, None]).astype(jnp.int32)
    before = (jnp.cumsum(matches, axis=0).astype(jnp.int32) - matches).astype(jnp.int32)
    rank_sorted = lax.optimization_barrier(jnp.sum(before * matches, axis=1)).astype(jnp.int32)
    kept_sorted = valid_sorted & (rank_sorted < capacity)
    slot_sorted = jnp.where(kept_sorted, route_sorted * capacity + rank_sorted, experts * capacity).astype(jnp.int32)
    slot_token = jnp.full((experts * capacity + 1,), count, jnp.int32).at[slot_sorted].set(order_row)[:experts * capacity]
    token_slot = jnp.zeros((count,), jnp.int32).at[order_row].set(slot_sorted)
    return (slot_token, token_slot)

def attend_sequence(weights, sequence, limit):
    norm_gain, norm_bias, qkv_weight, out_weight = weights
    centre = sequence - lax.optimization_barrier(jnp.mean(sequence, axis=1, keepdims=True))
    normed = centre * lax.rsqrt(lax.optimization_barrier(jnp.mean(centre * centre, axis=1, keepdims=True)) + EPSILON)
    ln_in = low(normed * norm_gain + norm_bias)
    projected = low_back(low(jnp.einsum('td,dhe->the', ln_in, qkv_weight, precision=HIGHEST)))
    queries = projected[:, :, :HD]
    key_vectors = projected[:, :, HD:2 * HD]
    values = projected[:, :, 2 * HD:]
    scores = low_back(jnp.einsum('qhd,khd->hqk', queries, key_vectors, precision=HIGHEST) * HD ** (-0.5))
    positions = jnp.arange(LEN, dtype=jnp.int32)
    allowed = (positions[None, :] <= positions[:, None]) & (positions[None, :] < limit)
    masked = jnp.where(allowed[None], scores, -1e+30)
    row_max = lax.optimization_barrier(jnp.max(masked, axis=-1, keepdims=True))
    raised = jnp.exp(masked - row_max)
    attention_weights = raised / lax.optimization_barrier(jnp.sum(raised, axis=-1, keepdims=True))
    attended = low_back(low(jnp.einsum('hqk,khd->qhd', low(attention_weights), values, precision=HIGHEST)))
    mixed = jnp.einsum('qhd,hde->qe', attended, out_weight, precision=HIGHEST)
    return sequence + low_back(mixed)

def expert_block(inputs):
    rows, centroid, expert_in, expert_out = inputs
    gate_values = jax.nn.sigmoid(jnp.dot(rows, centroid, precision=HIGHEST))
    current = rows
    for sublayer in range(2):
        hidden_pre = low_back(jnp.dot(low(current), expert_in[sublayer], precision=HIGHEST))
        hidden_act = low(jax.nn.gelu(hidden_pre, approximate=False))
        current = current + low_back(jnp.dot(hidden_act, expert_out[sublayer], precision=HIGHEST))
    return low_back(low(gate_values[:, None] * current))

def take_rows(block, table):
    return block[table]

def forward(tokens, norm_gain, norm_bias, qkv_weight, out_weight, centroids, expert_in, expert_out, lengths, slot_token, token_slot):
    sequences = tokens.reshape(SEQS, LEN, D)
    attend = jax.checkpoint(partial(attend_sequence, (norm_gain, norm_bias, qkv_weight, out_weight)))

    def attend_pair(pair):
        return attend(pair[0], pair[1])
    mixed = lax.map(attend_pair, (sequences, lengths)).reshape(TOKENS, D)
    sent = low_back(low(mixed)).reshape(N_DP, TOK_DEV, D)
    padded = jnp.concatenate([sent, jnp.zeros((N_DP, 1, D), jnp.float32)], axis=1)
    slotted = jax.vmap(take_rows)(padded, slot_token)
    per_expert = slotted.reshape(N_DP, EXPERTS, CAP, D).transpose(1, 0, 2, 3).reshape(EXPERTS, N_DP * CAP, D)
    returned = lax.map(jax.checkpoint(expert_block), (per_expert, centroids, expert_in, expert_out))
    back = returned.reshape(EXPERTS, N_DP, CAP, D).transpose(1, 0, 2, 3).reshape(N_DP, EXPERTS * CAP, D)
    back = jnp.concatenate([back, jnp.zeros((N_DP, 1, D), jnp.float32)], axis=1)
    gathered = jax.vmap(take_rows)(back, token_slot)
    return mixed + gathered.reshape(TOKENS, D)

def reference(tokens, lengths, routes, fill_order, norm_gain, norm_bias, qkv_weight, out_weight, centroids, expert_in, expert_out, cotangent):
    planner = partial(plan_slots, seq_len=LEN, experts=EXPERTS, capacity=CAP)
    slot_token, token_slot = jax.vmap(planner)(routes.reshape(N_DP, TOK_DEV, 1), fill_order.reshape(N_DP, 1, TOK_DEV), lengths.reshape(N_DP, SEQ_DEV))
    primals = (tokens.astype(jnp.float32), norm_gain.astype(jnp.float32), norm_bias.astype(jnp.float32), qkv_weight.astype(jnp.float32), out_weight.astype(jnp.float32), centroids.astype(jnp.float32), expert_in.astype(jnp.float32), expert_out.astype(jnp.float32))

    def apply_block(*weights):
        return forward(*weights, lengths, slot_token, token_slot)
    result, pullback = jax.vjp(apply_block, *primals)
    grads = pullback(cotangent.astype(jnp.float32))
    return (result.astype(jnp.bfloat16), grads[0].astype(jnp.bfloat16), grads[1], grads[2], grads[3], grads[4], grads[5], grads[6], grads[7])
```

```python
import math

import jax
import jax.numpy as jnp
from jax import lax
from jax.sharding import PartitionSpec as P

EPSILON = 1e-05
HIGHEST = lax.Precision.HIGHEST
F32 = jnp.float32
BF16 = jnp.bfloat16


class Grid:
    def __init__(self, size):
        inner = int(math.isqrt(size))
        while size % inner:
            inner -= 1
        self.size = size
        self.parts = {"x": inner, "y": size // inner}

    def _pairs(self, axis, shift):
        wide, tall = self.parts["x"], self.parts["y"]
        pairs = []
        for row in range(tall):
            for col in range(wide):
                if axis == "x":
                    other = row * wide + (col + shift) % wide
                else:
                    other = ((row + shift) % tall) * wide + col
                pairs.append((other, row * wide + col))
        return pairs

    def fetch(self, value, axis, shift=1):
        return lax.ppermute(value, "tensor", self._pairs(axis, shift))

    def gather_list(self, value, axis):
        return [value] + [self.fetch(value, axis, s) for s in range(1, self.parts[axis])]

    def scatter_list(self, parts, axis):
        total = parts[0]
        for s in range(1, self.parts[axis]):
            total = total + self.fetch(parts[s].astype(BF16), axis, -s).astype(F32)
        return total


def gather_rows(grid, value):
    if grid.size != 4:
        return lax.all_gather(value, "tensor", axis=0, tiled=False)
    half = value.shape[0] // 2
    me = lax.axis_index("tensor")
    first, second = value[:half], value[half:]
    first_x = grid.fetch(first, "x")
    second_y = grid.fetch(second, "y")
    first_y = grid.fetch(first, "y")
    second_x = grid.fetch(second, "x")
    first_xy = grid.fetch(first_x, "y")
    second_xy = grid.fetch(second_y, "x")
    out = jnp.zeros((4,) + value.shape, value.dtype)
    out = lax.dynamic_update_slice(out, value[None], (me, 0, 0))
    for other, top, bottom in ((1, first_x, second_x), (2, first_y, second_y), (3, first_xy, second_xy)):
        place = jnp.bitwise_xor(me, other)
        out = lax.dynamic_update_slice(out, top[None], (place, 0, 0))
        out = lax.dynamic_update_slice(out, bottom[None], (place, half, 0))
    return out


def scatter_rows(grid, term):
    size, rows, width = term.shape
    if size != 4:
        return lax.psum_scatter(term.astype(BF16), "tensor", scatter_dimension=0, tiled=False).astype(F32)
    me = lax.axis_index("tensor")
    half = width // 2

    def pick(other, low):
        place = jnp.bitwise_xor(me, other)
        return lax.dynamic_slice(term, (place, 0, low), (1, rows, half))[0]

    totals = []
    for low, near, far, near_axis, far_axis in ((0, 1, 2, "x", "y"), (half, 2, 1, "y", "x")):
        got_far = grid.fetch(pick(3, low).astype(BF16), near_axis)
        got_own = grid.fetch(pick(near, low).astype(BF16), near_axis)
        onward = pick(far, low).astype(F32) + got_far.astype(F32)
        got = grid.fetch(onward.astype(BF16), far_axis)
        totals.append(pick(0, low).astype(F32) + got_own.astype(F32) + got.astype(F32))
    return jnp.concatenate(totals, axis=1)


def gelu_pair(pre):
    cdf = 0.5 * (1.0 + lax.erf(pre * (2.0**-0.5)))
    density = jnp.exp(-0.5 * pre * pre) * ((2.0 * math.pi) ** -0.5)
    return (pre * cdf).astype(BF16), (cdf + pre * density).astype(BF16)


def plan_slots(routes, order, lengths, seq_len, experts, capacity, padded):
    count = routes.shape[0]
    seq_count = lengths.shape[0]
    places = jnp.arange(count, dtype=jnp.int32)
    limits = jnp.broadcast_to(lengths[:, None], (seq_count, seq_len)).reshape(count)
    is_valid = places % seq_len < limits
    order_row = order.reshape(count)
    route_sorted = routes.reshape(count)[order_row]
    valid_sorted = is_valid[order_row]
    matches = (
        (route_sorted[:, None] == jnp.arange(experts, dtype=jnp.int32)[None, :])
        & valid_sorted[:, None]
    ).astype(jnp.int32)
    before = jnp.cumsum(matches, axis=0) - matches
    rank_sorted = jnp.sum(before * matches, axis=1)
    kept_sorted = valid_sorted & (rank_sorted < capacity)
    slot_sorted = jnp.where(kept_sorted, route_sorted * padded + rank_sorted, experts * padded)
    slot_token = (
        jnp.full((experts * padded + 1,), count, jnp.int32)
        .at[slot_sorted]
        .set(order_row)[: experts * padded]
    )
    token_slot = jnp.zeros((count,), jnp.int32).at[order_row].set(slot_sorted)
    return (slot_token, token_slot)


def dot(a, b, contract):
    return lax.dot_general(a, b, (contract, ((), ())), preferred_element_type=F32)


def body(
    tokens,
    lengths,
    routes,
    fill_order,
    norm_gain,
    norm_bias,
    qkv_weight,
    out_weight,
    centroids,
    expert_in,
    expert_out,
    cotangent,
):
    tok_count, model_width = tokens.shape
    seq_count = lengths.shape[0]
    seq_len = tok_count // seq_count
    heads_here = qkv_weight.shape[1]
    head_size = out_weight.shape[1]
    experts = lax.axis_size("dp")
    shards = lax.axis_size("tensor")
    grid = Grid(shards)
    me = lax.axis_index("tensor")
    capacity = (9 * tok_count + 8 * experts - 1) // (8 * experts)
    share = 16 * -(-capacity // (16 * shards))
    padded = share * shards
    own_rows = experts * share
    tok_rows = tok_count // shards
    score_scale = head_size ** (-0.5)

    row_axis = ("y", "x")
    weight_axis = ("x", "y")
    win = [grid.gather_list(expert_in[0, k], weight_axis[k]) for k in range(2)]
    wout = [grid.gather_list(expert_out[0, k], weight_axis[k]) for k in range(2)]
    out_flat = out_weight.reshape(heads_here * head_size, model_width)
    out_all = lax.all_gather(out_flat, "tensor", axis=0, tiled=True)

    slot_token, token_slot = plan_slots(
        routes, fill_order, lengths, seq_len, experts, capacity, padded
    )
    own_slot = lax.dynamic_slice_in_dim(
        slot_token.reshape(experts, padded), me * share, share, 1
    ).reshape(own_rows)
    own_filled = (own_slot < tok_count)[:, None]
    own_index = jnp.minimum(own_slot, tok_count - 1)
    kept = (token_slot < experts * padded)[:, None]
    tok_expert = jnp.minimum(token_slot // padded, experts - 1)
    tok_rank = token_slot % padded
    tok_place = ((tok_rank // share) * experts + tok_expert) * share + tok_rank % share

    def to_experts(rows):
        picked = jnp.where(own_filled, rows[own_index], jnp.zeros((), rows.dtype))
        moved = lax.all_to_all(
            picked.reshape(experts, share, model_width), "dp", split_axis=0, concat_axis=0, tiled=True
        )
        return moved.reshape(own_rows, model_width)

    def from_experts(rows):
        moved = lax.all_to_all(
            rows.reshape(experts, share, model_width), "dp", split_axis=0, concat_axis=0, tiled=True
        )
        every = gather_rows(grid, moved.reshape(own_rows, model_width))
        picked = every.reshape(shards * own_rows, model_width)[tok_place]
        return jnp.where(kept, picked, jnp.zeros((), rows.dtype)).astype(F32)

    grad_ret = to_experts(cotangent).astype(F32)

    input_rows = tokens.astype(F32)
    centre = input_rows - jnp.mean(input_rows, axis=1, keepdims=True)
    inverse_scale = lax.rsqrt(jnp.mean(centre * centre, axis=1, keepdims=True) + EPSILON)
    normed = centre * inverse_scale
    ln_in = (normed * norm_gain + norm_bias).astype(BF16)
    projected = jnp.einsum(
        "td,dhe->the", ln_in, qkv_weight, preferred_element_type=F32
    ).astype(BF16)
    projected = projected.reshape(seq_count, seq_len, heads_here, 3 * head_size)
    queries = projected[..., :head_size]
    key_vectors = projected[..., head_size : 2 * head_size]
    values = projected[..., 2 * head_size :]
    positions = jnp.arange(seq_len, dtype=jnp.int32)
    allowed = (positions[None, None, :] <= positions[None, :, None]) & (
        positions[None, None, :] < lengths[:, None, None]
    )

    def attention_probs(log_total):
        scores = (
            jnp.einsum("sqhd,skhd->shqk", queries, key_vectors, preferred_element_type=F32)
            * score_scale
        )
        scores = jnp.where(allowed[:, None], scores, -1e30)
        if log_total is None:
            row_max = jnp.max(scores, axis=-1, keepdims=True)
            log_total = row_max + jnp.log(
                jnp.sum(jnp.exp(scores - row_max), axis=-1, keepdims=True)
            )
        return (jnp.exp(scores - log_total), log_total)

    attention_weights, log_total = attention_probs(None)
    attended = jnp.einsum(
        "shqk,skhd->sqhd",
        attention_weights.astype(BF16),
        values,
        preferred_element_type=F32,
    ).astype(BF16)
    attended = attended.reshape(tok_count, heads_here * head_size)
    every_attended = gather_rows(grid, attended)
    attended_all = jnp.swapaxes(every_attended, 0, 1).reshape(tok_count, -1)
    mixed = input_rows + dot(attended_all, out_all, ((1,), (0,)))
    sent = mixed.astype(BF16)

    expert_rows = to_experts(sent)
    centroid = centroids[0]
    gate = jax.nn.sigmoid(jnp.dot(expert_rows, centroid, preferred_element_type=F32))[:, None]
    current = expert_rows.astype(F32)
    saved = []
    for k in range(2):
        rows_in = jnp.concatenate(grid.gather_list(current.astype(BF16), row_axis[k]), axis=0)
        acts, slopes = [], []
        total = None
        for w_in, w_out in zip(win[k], wout[k]):
            act, slope = gelu_pair(dot(rows_in, w_in, ((1,), (0,))))
            term = dot(act, w_out, ((1,), (0,)))
            total = term if total is None else total + term
            acts.append(act)
            slopes.append(slope)
        parts = jnp.split(total, grid.parts[row_axis[k]], axis=0)
        current = current + grid.scatter_list(parts, row_axis[k])
        saved.append((rows_in, acts, slopes))
    output = (mixed + from_experts((gate * current).astype(BF16))).astype(BF16)

    grad_gate = jnp.sum(grad_ret * current, axis=1, keepdims=True)
    grad_logit = grad_gate * gate * (1.0 - gate)
    grad_current = gate * grad_ret
    grads_in = [None, None]
    grads_back = [None, None]
    for k in (1, 0):
        rows_in, acts, slopes = saved[k]
        branch = jnp.concatenate(grid.gather_list(grad_current.astype(BF16), row_axis[k]), axis=0)
        total = None
        in_parts, out_parts = [], []
        for w_in, w_out, act, slope in zip(win[k], wout[k], acts, slopes):
            grad_pre = (dot(branch, w_out, ((1,), (1,))) * slope.astype(F32)).astype(BF16)
            term = dot(grad_pre, w_in, ((1,), (1,)))
            total = term if total is None else total + term
            out_parts.append(dot(act, branch, ((0,), (0,))))
            in_parts.append(dot(rows_in, grad_pre, ((0,), (0,))))
        parts = jnp.split(total, grid.parts[row_axis[k]], axis=0)
        grad_current = grad_current + grid.scatter_list(parts, row_axis[k])
        grads_in[k] = grid.scatter_list(in_parts, weight_axis[k])
        grads_back[k] = grid.scatter_list(out_parts, weight_axis[k])
    grad_rows = (grad_current + grad_logit * centroid.astype(F32)[None, :]).astype(BF16)
    grad_centroid = lax.psum(
        jnp.sum(grad_logit * expert_rows.astype(F32), axis=0, keepdims=True), "tensor"
    )
    grad_mixed = cotangent.astype(F32) + from_experts(grad_rows)

    grad_attn = grad_mixed.astype(BF16)
    grad_out_local = dot(attended, grad_attn, ((0,), (0,))).reshape(
        heads_here, head_size, model_width
    )
    grad_attended = dot(grad_attn, out_flat, ((1,), (1,))).astype(BF16)
    grad_attended = grad_attended.reshape(seq_count, seq_len, heads_here, head_size)
    attention_weights, unused_total = attention_probs(log_total)
    grad_probs = jnp.einsum(
        "sqhd,skhd->shqk", grad_attended, values, preferred_element_type=F32
    )
    row_delta = jnp.sum(attention_weights * grad_probs, axis=-1, keepdims=True)
    grad_scores = (attention_weights * (grad_probs - row_delta)).astype(BF16)
    grad_query = (
        jnp.einsum("shqk,skhd->sqhd", grad_scores, key_vectors, preferred_element_type=F32)
        * score_scale
    ).astype(BF16)
    grad_key = (
        jnp.einsum("shqk,sqhd->skhd", grad_scores, queries, preferred_element_type=F32)
        * score_scale
    ).astype(BF16)
    grad_value = jnp.einsum(
        "shqk,sqhd->skhd",
        attention_weights.astype(BF16),
        grad_attended,
        preferred_element_type=F32,
    ).astype(BF16)
    grad_projected = jnp.concatenate([grad_query, grad_key, grad_value], axis=-1).reshape(
        tok_count, heads_here, 3 * head_size
    )
    grad_qkv_local = jnp.einsum(
        "td,the->dhe", ln_in, grad_projected, preferred_element_type=F32
    )
    grad_ln_part = jnp.einsum(
        "the,dhe->td", grad_projected, qkv_weight, preferred_element_type=F32
    )
    grad_ln = scatter_rows(grid, grad_ln_part.astype(BF16).reshape(shards, tok_rows, model_width))

    def own(rows):
        return lax.dynamic_slice_in_dim(rows, me * tok_rows, tok_rows, 0)

    own_scale = own(inverse_scale)
    own_normed = own(centre) * own_scale
    grad_normed = grad_ln * norm_gain
    mean_plain = jnp.mean(grad_normed, axis=1, keepdims=True)
    mean_cross = jnp.mean(grad_normed * own_normed, axis=1, keepdims=True)
    grad_input = own(grad_mixed) + own_scale * (grad_normed - mean_plain - own_normed * mean_cross)
    grad_tokens = gather_rows(grid, grad_input.astype(BF16)).reshape(tok_count, model_width)
    norm_parts = jnp.stack([jnp.sum(grad_ln * own_normed, axis=0), jnp.sum(grad_ln, axis=0)])
    norm_total = lax.dynamic_slice_in_dim(
        lax.psum(norm_parts, ("dp", "tensor")), me * (model_width // shards), model_width // shards, 1
    )
    grad_qkv_weight, grad_out_weight = lax.psum((grad_qkv_local, grad_out_local), "dp")
    return (
        output,
        grad_tokens,
        norm_total[0],
        norm_total[1],
        grad_qkv_weight,
        grad_out_weight,
        grad_centroid,
        jnp.stack(grads_in)[None],
        jnp.stack(grads_back)[None],
    )


def solution(mesh):
    return jax.shard_map(
        body,
        mesh=mesh,
        in_specs=(
            P("dp", None),
            P("dp"),
            P("dp", None),
            P("dp", None),
            P(),
            P(),
            P(None, "tensor", None),
            P("tensor", None, None),
            P("dp", None),
            P("dp", None, None, "tensor"),
            P("dp", None, "tensor", None),
            P("dp", None),
        ),
        out_specs=(
            P("dp", None),
            P("dp", None),
            P("tensor"),
            P("tensor"),
            P(None, "tensor", None),
            P("tensor", None, None),
            P("dp", None),
            P("dp", None, None, "tensor"),
            P("dp", None, "tensor", None),
        ),
        check_vma=False,
    )
```

```python
import math

import jax
import jax.numpy as jnp
from jax import lax
from jax.sharding import PartitionSpec as P

EPSILON = 1e-05
HIGHEST = lax.Precision.HIGHEST
F32 = jnp.float32
BF16 = jnp.bfloat16


CORES = 2


class Grid:
    def __init__(self, shards, experts):
        self.size = shards
        self.experts = experts
        self.depth = experts // CORES

    def over_core(self, value):
        return lax.ppermute(value, "dp", [(d, d ^ 1) for d in range(self.experts)])

    def over_tensor(self, value, other):
        return lax.ppermute(value, "tensor", [(t, t ^ other) for t in range(self.size)])

    def exchange_depth(self, value):
        groups = [[CORES * z + c for z in range(self.depth)] for c in range(CORES)]
        return lax.all_to_all(
            value, "dp", split_axis=0, concat_axis=0, axis_index_groups=groups, tiled=True
        )


def slice_half(value, half, axis):
    width = value.shape[axis] // 2
    return lax.dynamic_slice_in_dim(value, half * width, width, axis)


def owner_pairs(grid, flip, back=False):
    pairs = []
    for z in range(grid.depth):
        for core in range(CORES):
            for y in range(2):
                for x in range(2):
                    here = (CORES * z + core) * 4 + 2 * y + x
                    there = (CORES * z + (x ^ flip)) * 4 + 2 * y + core
                    pairs.append((there, here) if back else (here, there))
    return pairs


def fetch_halves(grid, weight, axis):
    core = lax.axis_index("dp") % CORES
    me = lax.axis_index("tensor")
    if grid.size == 4:
        near = [
            lax.ppermute(
                slice_half(weight, jnp.bitwise_xor(me % 2, flip), axis),
                ("dp", "tensor"),
                owner_pairs(grid, flip),
            )
            for flip in range(2)
        ]
        return near + [grid.over_tensor(piece, 2) for piece in near]
    every = lax.all_gather(weight, "tensor", axis=0, tiled=False)
    chosen = jnp.where(me % 2 == core, every, grid.over_core(every))
    return [slice_half(chosen[t], core, axis) for t in range(grid.size)]


def return_halves(grid, pieces, axis):
    core = lax.axis_index("dp") % CORES
    me = lax.axis_index("tensor")
    if grid.size == 4:
        halves = []
        for flip in range(2):
            far = grid.over_tensor(pieces[2 + flip].astype(BF16), 2)
            total = pieces[flip] + far.astype(F32)
            halves.append(
                lax.ppermute(total.astype(BF16), ("dp", "tensor"), owner_pairs(grid, flip, True))
            )
        swapped = me % 2 == 1
    else:
        stacked = jnp.stack(pieces).astype(BF16)
        wide = jnp.stack([jnp.where(me % 2 == p, stacked, jnp.zeros_like(stacked)) for p in range(2)])
        mine = lax.psum_scatter(wide, "tensor", scatter_dimension=1, tiled=False)
        halves = [
            jnp.where(core == 0, mine[0], mine[1]),
            grid.over_core(jnp.where(core == 0, mine[1], mine[0])),
        ]
        swapped = core == 1
    halves = [half.astype(F32) for half in halves]
    return jnp.where(swapped, jnp.concatenate(halves[::-1], axis), jnp.concatenate(halves, axis))


def gather_rows(grid, value, balanced=True):
    if grid.size != 4:
        return lax.all_gather(value, "tensor", axis=0, tiled=False)
    me = lax.axis_index("tensor")
    out = jnp.zeros((4,) + value.shape, value.dtype)
    out = lax.dynamic_update_slice(out, value[None], (me, 0, 0))
    if not balanced:
        from_y = grid.over_tensor(value, 2)
        from_x = grid.over_tensor(value, 1)
        from_xy = grid.over_tensor(from_y, 1)
        for other, piece in ((1, from_x), (2, from_y), (3, from_xy)):
            out = lax.dynamic_update_slice(out, piece[None], (jnp.bitwise_xor(me, other), 0, 0))
        return out
    half = value.shape[0] // 2
    first, second = value[:half], value[half:]
    first_x = grid.over_tensor(first, 1)
    second_y = grid.over_tensor(second, 2)
    first_y = grid.over_tensor(first, 2)
    second_x = grid.over_tensor(second, 1)
    first_xy = grid.over_tensor(first_x, 2)
    second_xy = grid.over_tensor(second_y, 1)
    for other, top, bottom in ((1, first_x, second_x), (2, first_y, second_y), (3, first_xy, second_xy)):
        place = jnp.bitwise_xor(me, other)
        out = lax.dynamic_update_slice(out, top[None], (place, 0, 0))
        out = lax.dynamic_update_slice(out, bottom[None], (place, half, 0))
    return out


def scatter_rows(grid, term):
    size, rows, width = term.shape
    if size != 4:
        return lax.psum_scatter(term.astype(BF16), "tensor", scatter_dimension=0, tiled=False).astype(F32)
    me = lax.axis_index("tensor")
    half = width // 2

    def pick(other, low):
        place = jnp.bitwise_xor(me, other)
        return lax.dynamic_slice(term, (place, 0, low), (1, rows, half))[0]

    totals = []
    for low, near, far in ((0, 1, 2), (half, 2, 1)):
        got_far = grid.over_tensor(pick(3, low).astype(BF16), near)
        got_own = grid.over_tensor(pick(near, low).astype(BF16), near)
        onward = pick(far, low).astype(F32) + got_far.astype(F32)
        got = grid.over_tensor(onward.astype(BF16), far)
        totals.append(pick(0, low).astype(F32) + got_own.astype(F32) + got.astype(F32))
    return jnp.concatenate(totals, axis=1)


def gelu_pair(pre):
    cdf = 0.5 * (1.0 + lax.erf(pre * (2.0**-0.5)))
    density = jnp.exp(-0.5 * pre * pre) * ((2.0 * math.pi) ** -0.5)
    return (pre * cdf).astype(BF16), (cdf + pre * density).astype(BF16)


def plan_slots(routes, order, lengths, seq_len, experts, capacity, padded):
    count = routes.shape[0]
    seq_count = lengths.shape[0]
    places = jnp.arange(count, dtype=jnp.int32)
    limits = jnp.broadcast_to(lengths[:, None], (seq_count, seq_len)).reshape(count)
    is_valid = places % seq_len < limits
    order_row = order.reshape(count)
    route_sorted = routes.reshape(count)[order_row]
    valid_sorted = is_valid[order_row]
    matches = (
        (route_sorted[:, None] == jnp.arange(experts, dtype=jnp.int32)[None, :])
        & valid_sorted[:, None]
    ).astype(jnp.int32)
    before = jnp.cumsum(matches, axis=0) - matches
    rank_sorted = jnp.sum(before * matches, axis=1)
    kept_sorted = valid_sorted & (rank_sorted < capacity)
    slot_sorted = jnp.where(kept_sorted, route_sorted * padded + rank_sorted, experts * padded)
    slot_token = (
        jnp.full((experts * padded + 1,), count, jnp.int32)
        .at[slot_sorted]
        .set(order_row)[: experts * padded]
    )
    token_slot = jnp.zeros((count,), jnp.int32).at[order_row].set(slot_sorted)
    return (slot_token, token_slot)


def dot(a, b, contract):
    return lax.dot_general(a, b, (contract, ((), ())), preferred_element_type=F32)


def body(
    tokens,
    lengths,
    routes,
    fill_order,
    norm_gain,
    norm_bias,
    qkv_weight,
    out_weight,
    centroids,
    expert_in,
    expert_out,
    cotangent,
):
    tok_count, model_width = tokens.shape
    seq_count = lengths.shape[0]
    seq_len = tok_count // seq_count
    heads_here = qkv_weight.shape[1]
    head_size = out_weight.shape[1]
    experts = lax.axis_size("dp")
    shards = lax.axis_size("tensor")
    grid = Grid(shards, experts)
    me = lax.axis_index("tensor")
    parity, part = me % 2, me // 2
    core = lax.axis_index("dp") % CORES
    depth = experts // CORES
    row_parts = shards // 2
    capacity = (9 * tok_count + 8 * experts - 1) // (8 * experts)
    share = 16 * -(-capacity // (16 * row_parts))
    padded = share * row_parts
    own_rows = depth * share
    tok_rows = tok_count // shards
    score_scale = head_size ** (-0.5)

    win, wout = [], []
    for k in range(2):
        win.append(fetch_halves(grid, expert_in[0, k], 1))
        wout.append(fetch_halves(grid, expert_out[0, k], 0))
    out_flat = out_weight.reshape(heads_here * head_size, model_width)
    out_all = gather_rows(grid, out_flat, False).reshape(shards * heads_here * head_size, model_width)
    centroid = jnp.where(parity == core, centroids[0], grid.over_core(centroids[0]))

    slot_token, token_slot = plan_slots(
        routes, fill_order, lengths, seq_len, experts, capacity, padded
    )
    own_slot = lax.dynamic_slice(
        slot_token.reshape(depth, CORES, row_parts, share), (0, parity, part, 0), (depth, 1, 1, share)
    ).reshape(own_rows)
    own_filled = (own_slot < tok_count)[:, None]
    own_index = jnp.minimum(own_slot, tok_count - 1)
    kept = (token_slot < experts * padded)[:, None]
    tok_expert = jnp.minimum(token_slot // padded, experts - 1)
    tok_rank = token_slot % padded
    tok_device = (tok_rank // share) * 2 + tok_expert % 2
    tok_place = (tok_device * depth + tok_expert // 2) * share + tok_rank % share

    def to_experts(rows):
        picked = jnp.where(own_filled, rows[own_index], jnp.zeros((), rows.dtype))
        return grid.exchange_depth(picked.reshape(depth, share, model_width)).reshape(own_rows, model_width)

    def from_experts(rows, balanced):
        moved = grid.exchange_depth(rows.reshape(depth, share, model_width))
        every = gather_rows(grid, moved.reshape(own_rows, model_width), balanced)
        picked = every.reshape(shards * own_rows, model_width)[tok_place]
        return jnp.where(kept, picked, jnp.zeros((), rows.dtype)).astype(F32)

    grad_ret = to_experts(cotangent).astype(F32)

    input_rows = tokens.astype(F32)
    centre = input_rows - jnp.mean(input_rows, axis=1, keepdims=True)
    inverse_scale = lax.rsqrt(jnp.mean(centre * centre, axis=1, keepdims=True) + EPSILON)
    normed = centre * inverse_scale
    ln_in = (normed * norm_gain + norm_bias).astype(BF16)
    projected = jnp.einsum(
        "td,dhe->the", ln_in, qkv_weight, preferred_element_type=F32
    ).astype(BF16)
    projected = projected.reshape(seq_count, seq_len, heads_here, 3 * head_size)
    queries = projected[..., :head_size]
    key_vectors = projected[..., head_size : 2 * head_size]
    values = projected[..., 2 * head_size :]
    positions = jnp.arange(seq_len, dtype=jnp.int32)
    allowed = (positions[None, None, :] <= positions[None, :, None]) & (
        positions[None, None, :] < lengths[:, None, None]
    )

    def attention_probs(log_total):
        scores = (
            jnp.einsum("sqhd,skhd->shqk", queries, key_vectors, preferred_element_type=F32)
            * score_scale
        )
        scores = jnp.where(allowed[:, None], scores, -1e30)
        if log_total is None:
            row_max = jnp.max(scores, axis=-1, keepdims=True)
            log_total = row_max + jnp.log(
                jnp.sum(jnp.exp(scores - row_max), axis=-1, keepdims=True)
            )
        return (jnp.exp(scores - log_total), log_total)

    attention_weights, log_total = attention_probs(None)
    attended = jnp.einsum(
        "shqk,skhd->sqhd",
        attention_weights.astype(BF16),
        values,
        preferred_element_type=F32,
    ).astype(BF16)
    attended = attended.reshape(tok_count, heads_here * head_size)
    every_attended = gather_rows(grid, attended, False)
    attended_all = jnp.swapaxes(every_attended, 0, 1).reshape(tok_count, -1)
    mixed = input_rows + dot(attended_all, out_all, ((1,), (0,)))
    sent = mixed.astype(BF16)

    def both_cores(value):
        return jnp.concatenate([value, grid.over_core(value)], axis=0)

    def sum_cores(total):
        return total[:own_rows] + grid.over_core(total[own_rows:].astype(BF16)).astype(F32)

    expert_rows = to_experts(sent)
    gate = jax.nn.sigmoid(jnp.dot(expert_rows, centroid, preferred_element_type=F32))[:, None]
    current = expert_rows.astype(F32)
    saved = []
    for k in range(2):
        rows_in = both_cores(current.astype(BF16))
        acts, slopes = [], []
        total = None
        for w_in, w_out in zip(win[k], wout[k]):
            act, slope = gelu_pair(dot(rows_in, w_in, ((1,), (0,))))
            term = dot(act, w_out, ((1,), (0,)))
            total = term if total is None else total + term
            acts.append(act)
            slopes.append(slope)
        current = current + sum_cores(total)
        saved.append((rows_in, acts, slopes))
    output = (mixed + from_experts((gate * current).astype(BF16), False)).astype(BF16)

    grad_gate = jnp.sum(grad_ret * current, axis=1, keepdims=True)
    grad_logit = grad_gate * gate * (1.0 - gate)
    grad_current = gate * grad_ret
    grads_in = [None, None]
    grads_back = [None, None]
    for k in (1, 0):
        rows_in, acts, slopes = saved[k]
        branch = both_cores(grad_current.astype(BF16))
        total = None
        in_parts, out_parts = [], []
        for w_in, w_out, act, slope in zip(win[k], wout[k], acts, slopes):
            grad_pre = (dot(branch, w_out, ((1,), (1,))) * slope.astype(F32)).astype(BF16)
            term = dot(grad_pre, w_in, ((1,), (1,)))
            total = term if total is None else total + term
            out_parts.append(dot(act, branch, ((0,), (0,))))
            in_parts.append(dot(rows_in, grad_pre, ((0,), (0,))))
        grad_current = grad_current + sum_cores(total)
        grads_in[k] = return_halves(grid, in_parts, 1)
        grads_back[k] = return_halves(grid, out_parts, 0)
    grad_rows = (grad_current + grad_logit * centroid.astype(F32)[None, :]).astype(BF16)
    centroid_part = jnp.sum(grad_logit * expert_rows.astype(F32), axis=0, keepdims=True)
    centroid_parts = lax.psum(
        jnp.concatenate([jnp.where(parity == p, centroid_part, 0.0) for p in range(2)], axis=0), "tensor"
    )
    centroid_parts = centroid_parts + grid.over_core(centroid_parts)
    grad_centroid = lax.dynamic_slice_in_dim(centroid_parts, core, 1, 0)
    grad_mixed = cotangent.astype(F32) + from_experts(grad_rows, True)

    grad_attn = grad_mixed.astype(BF16)
    grad_out_local = dot(attended, grad_attn, ((0,), (0,))).reshape(
        heads_here, head_size, model_width
    )
    grad_attended = dot(grad_attn, out_flat, ((1,), (1,))).astype(BF16)
    grad_attended = grad_attended.reshape(seq_count, seq_len, heads_here, head_size)
    attention_weights, unused_total = attention_probs(log_total)
    grad_probs = jnp.einsum(
        "sqhd,skhd->shqk", grad_attended, values, preferred_element_type=F32
    )
    row_delta = jnp.sum(attention_weights * grad_probs, axis=-1, keepdims=True)
    grad_scores = (attention_weights * (grad_probs - row_delta)).astype(BF16)
    grad_query = (
        jnp.einsum("shqk,skhd->sqhd", grad_scores, key_vectors, preferred_element_type=F32)
        * score_scale
    ).astype(BF16)
    grad_key = (
        jnp.einsum("shqk,sqhd->skhd", grad_scores, queries, preferred_element_type=F32)
        * score_scale
    ).astype(BF16)
    grad_value = jnp.einsum(
        "shqk,sqhd->skhd",
        attention_weights.astype(BF16),
        grad_attended,
        preferred_element_type=F32,
    ).astype(BF16)
    grad_projected = jnp.concatenate([grad_query, grad_key, grad_value], axis=-1).reshape(
        tok_count, heads_here, 3 * head_size
    )
    grad_qkv_local = jnp.einsum(
        "td,the->dhe", ln_in, grad_projected, preferred_element_type=F32
    )
    grad_ln_part = jnp.einsum(
        "the,dhe->td", grad_projected, qkv_weight, preferred_element_type=F32
    )
    grad_ln = scatter_rows(grid, grad_ln_part.astype(BF16).reshape(shards, tok_rows, model_width))

    def own(rows):
        return lax.dynamic_slice_in_dim(rows, me * tok_rows, tok_rows, 0)

    own_scale = own(inverse_scale)
    own_normed = own(centre) * own_scale
    grad_normed = grad_ln * norm_gain
    mean_plain = jnp.mean(grad_normed, axis=1, keepdims=True)
    mean_cross = jnp.mean(grad_normed * own_normed, axis=1, keepdims=True)
    grad_input = own(grad_mixed) + own_scale * (grad_normed - mean_plain - own_normed * mean_cross)
    grad_tokens = gather_rows(grid, grad_input.astype(BF16)).reshape(tok_count, model_width)
    norm_parts = jnp.stack([jnp.sum(grad_ln * own_normed, axis=0), jnp.sum(grad_ln, axis=0)])
    norm_total = lax.dynamic_slice_in_dim(
        lax.psum(norm_parts, ("dp", "tensor")), me * (model_width // shards), model_width // shards, 1
    )
    grad_qkv_weight, grad_out_weight = lax.psum((grad_qkv_local, grad_out_local), "dp")
    return (
        output,
        grad_tokens,
        norm_total[0],
        norm_total[1],
        grad_qkv_weight,
        grad_out_weight,
        grad_centroid,
        jnp.stack(grads_in)[None],
        jnp.stack(grads_back)[None],
    )


def solution(mesh):
    return jax.shard_map(
        body,
        mesh=mesh,
        in_specs=(
            P("dp", None),
            P("dp"),
            P("dp", None),
            P("dp", None),
            P(),
            P(),
            P(None, "tensor", None),
            P("tensor", None, None),
            P("dp", None),
            P("dp", None, None, "tensor"),
            P("dp", None, "tensor", None),
            P("dp", None),
        ),
        out_specs=(
            P("dp", None),
            P("dp", None),
            P("tensor"),
            P("tensor"),
            P(None, "tensor", None),
            P("tensor", None, None),
            P("dp", None),
            P("dp", None, None, "tensor"),
            P("dp", None, "tensor", None),
        ),
        check_vma=False,
    )
```

```python
import functools
import math

import jax
import jax.numpy as jnp
from jax import lax
from jax.experimental import pallas as pl
from jax.experimental.pallas import tpu as pltpu
from jax.sharding import PartitionSpec as P

EPSILON = 1e-05
MASKED = -1e30
F32 = jnp.float32
BF16 = jnp.bfloat16
CORES = 2


def dot(a, b, contract):
    return lax.dot_general(a, b, (contract, ((), ())), preferred_element_type=F32)


def norm_project_kernel(x_ref, gain_ref, bias_ref, w_ref, ln_ref, out_ref):
    x = x_ref[...].astype(F32)
    centre = x - jnp.mean(x, axis=1, keepdims=True)
    scale = lax.rsqrt(jnp.mean(centre * centre, axis=1, keepdims=True) + EPSILON)
    ln = (centre * scale * gain_ref[...] + bias_ref[...]).astype(BF16)
    ln_ref[...] = ln
    out_ref[...] = dot(ln, w_ref[...], ((1,), (0,))).astype(BF16)


def norm_project(tokens, gain, bias, weight):
    rows, width = tokens.shape
    columns = weight.shape[1]
    tile = 512
    return pl.pallas_call(
        norm_project_kernel,
        grid=(rows // tile,),
        in_specs=[
            pl.BlockSpec((tile, width), lambda i: (i, 0)),
            pl.BlockSpec((1, width), lambda i: (0, 0)),
            pl.BlockSpec((1, width), lambda i: (0, 0)),
            pl.BlockSpec((width, columns), lambda i: (0, 0)),
        ],
        out_specs=[
            pl.BlockSpec((tile, width), lambda i: (i, 0)),
            pl.BlockSpec((tile, columns), lambda i: (i, 0)),
        ],
        out_shape=[
            jax.ShapeDtypeStruct((rows, width), BF16),
            jax.ShapeDtypeStruct((rows, columns), BF16),
        ],
        compiler_params=pltpu.CompilerParams(vmem_limit_bytes=40 << 20),
        cost_estimate=pl.CostEstimate(
            flops=2 * rows * width * columns,
            bytes_accessed=2 * (2 * rows * width + rows * columns + width * columns),
            transcendentals=rows,
        ),
    )(tokens, gain[None], bias[None], weight)


def attend_kernel(head_size, group, tile, len_ref, q_ref, k_ref, v_ref, o_ref, lse_ref):
    seq_len, lanes = q_ref.shape
    scale = head_size**-0.5
    limit = len_ref[pl.program_id(0)]
    keys = k_ref[...]
    values = v_ref[...]
    key_place = lax.broadcasted_iota(jnp.int32, (seq_len, lanes), 0)
    lane = lax.broadcasted_iota(jnp.int32, (seq_len, lanes), 1)
    causal = lax.broadcasted_iota(jnp.int32, (tile, tile), 0) <= lax.broadcasted_iota(
        jnp.int32, (tile, tile), 1
    )
    tall = lax.broadcasted_iota(jnp.int32, (lanes, tile), 0)
    lane_q = lax.broadcasted_iota(jnp.int32, (tile, lanes), 1)
    heads = []
    for a in range(group):
        mine = (lane >= a * head_size) & (lane < (a + 1) * head_size)
        spare = ((a + 1) % group) * head_size
        extra = jnp.where((lane == spare) & (key_place >= limit), MASKED, 0.0).astype(BF16)
        k_a = jnp.where(mine, keys, extra)
        v_a = jnp.where(mine, values, jnp.ones((), BF16))
        heads.append((k_a, v_a, spare))
    for i in range(seq_len // tile):
        end = (i + 1) * tile
        q = (q_ref[i * tile : end, :].astype(F32) * scale).astype(BF16)
        out = None
        for a in range(group):
            k_a, v_a, spare = heads[a]
            mine_q = (lane_q >= a * head_size) & (lane_q < (a + 1) * head_size)
            q_a = jnp.where(mine_q, q, jnp.where(lane_q == spare, 1.0, 0.0).astype(BF16))
            scores = dot(k_a[:end], q_a, ((1,), (1,)))
            last = jnp.where(causal, scores[i * tile :], MASKED)
            scores = jnp.concatenate([scores[: i * tile], last], axis=0) if i else last
            top = jnp.max(scores, axis=0, keepdims=True)
            probs = jnp.exp(scores - top).astype(BF16)
            result = dot(v_a[:end], probs, ((0,), (0,)))
            total = result[spare : spare + 1, :]
            lse_ref[0, 0, a : a + 1, i * tile : end] = top + jnp.log(total)
            result = result / total
            if out is None:
                out = result
            else:
                out = jnp.where((tall >= a * head_size) & (tall < (a + 1) * head_size), result, out)
        o_ref[i * tile : end, :] = out.T.astype(BF16)


def attend(projected, lengths, seqs, heads, head_size):
    rows = projected.shape[0]
    seq_len = rows // seqs
    group = 2
    lanes = group * head_size
    groups = heads // group
    tile = 256
    return pl.pallas_call(
        functools.partial(attend_kernel, head_size, group, tile),
        grid_spec=pltpu.PrefetchScalarGridSpec(
            num_scalar_prefetch=1,
            grid=(seqs, groups),
            in_specs=[
                pl.BlockSpec((seq_len, lanes), lambda s, g, n: (s, g)),
                pl.BlockSpec((seq_len, lanes), lambda s, g, n: (s, groups + g)),
                pl.BlockSpec((seq_len, lanes), lambda s, g, n: (s, 2 * groups + g)),
            ],
            out_specs=[
                pl.BlockSpec((seq_len, lanes), lambda s, g, n: (s, g)),
                pl.BlockSpec((1, 1, group, seq_len), lambda s, g, n: (s, g, 0, 0)),
            ],
        ),
        out_shape=[
            jax.ShapeDtypeStruct((rows, heads * head_size), BF16),
            jax.ShapeDtypeStruct((seqs, groups, group, seq_len), F32),
        ],
        compiler_params=pltpu.CompilerParams(vmem_limit_bytes=40 << 20),
        cost_estimate=pl.CostEstimate(
            flops=4 * rows * seq_len * heads * head_size,
            bytes_accessed=8 * rows * heads * head_size,
            transcendentals=rows * seq_len * heads // 2,
        ),
    )(lengths, projected, projected, projected)


def attend_back_kernel(head_size, group, tile, len_ref, q_ref, k_ref, v_ref, o_ref, do_ref, lse_ref, out_ref, dk_acc, dv_acc):
    seq_len, lanes = q_ref.shape
    scale = head_size**-0.5
    limit = len_ref[pl.program_id(0)]
    keys = k_ref[...]
    values = v_ref[...]
    zero = jnp.zeros((), BF16)

    def place(kind):
        block = kind * pl.num_programs(1) + pl.program_id(1)
        return pl.ds(pl.multiple_of(block * lanes, lanes), lanes)

    key_place = lax.broadcasted_iota(jnp.int32, (seq_len, lanes), 0)
    lane = lax.broadcasted_iota(jnp.int32, (seq_len, lanes), 1)
    causal = lax.broadcasted_iota(jnp.int32, (tile, tile), 0) <= lax.broadcasted_iota(
        jnp.int32, (tile, tile), 1
    )
    lane_q = lax.broadcasted_iota(jnp.int32, (tile, lanes), 1)
    heads = []
    for a in range(group):
        mine = (lane >= a * head_size) & (lane < (a + 1) * head_size)
        spare = ((a + 1) % group) * head_size
        extra = jnp.where((lane == spare) & (key_place >= limit), MASKED, 0.0).astype(BF16)
        k_a = jnp.where(mine, keys, extra)
        ones = jnp.where((lane == spare) | (lane == spare + 1), 1.0, 0.0).astype(BF16)
        v_a = jnp.where(mine, values, ones)
        heads.append((k_a, v_a, spare))
    steps = seq_len // tile
    for i in reversed(range(steps)):
        end = (i + 1) * tile
        q = (q_ref[i * tile : end, :].astype(F32) * scale).astype(BF16)
        do = do_ref[i * tile : end, :]
        product = do.astype(F32) * o_ref[i * tile : end, :].astype(F32)
        dq = None
        dk = None
        dv = None
        for a in range(group):
            k_a, v_a, spare = heads[a]
            mine_q = (lane_q >= a * head_size) & (lane_q < (a + 1) * head_size)
            q_m = jnp.where(mine_q, q, zero)
            q_a = jnp.where(mine_q, q, jnp.where(lane_q == spare, 1.0, 0.0).astype(BF16))
            delta = -jnp.sum(jnp.where(mine_q, product, 0.0), axis=1, keepdims=True)
            high = delta.astype(BF16)
            low = (delta - high.astype(F32)).astype(BF16)
            do_m = jnp.where(mine_q, do, zero)
            do_a = jnp.where(lane_q == spare, high, jnp.where(lane_q == spare + 1, low, do_m))
            scores = dot(k_a[:end], q_a, ((1,), (1,)))
            last = jnp.where(causal, scores[i * tile :], MASKED)
            scores = jnp.concatenate([scores[: i * tile], last], axis=0) if i else last
            probs = jnp.exp(scores - lse_ref[0, 0, a : a + 1, i * tile : end])
            grad = dot(v_a[:end], do_a, ((1,), (1,)))
            grad = (probs * grad).astype(BF16)
            term_v = dot(probs.astype(BF16), do_m, ((1,), (0,)))
            term_k = dot(grad, q_m, ((1,), (0,)))
            term_q = dot(k_a[:end], grad, ((0,), (0,)))
            dv = term_v if dv is None else dv + term_v
            dk = term_k if dk is None else dk + term_k
            if dq is None:
                dq = term_q
            else:
                tall = lax.broadcasted_iota(jnp.int32, (lanes, tile), 0)
                dq = jnp.where((tall >= a * head_size) & (tall < (a + 1) * head_size), term_q, dq)
        out_ref[i * tile : end, place(0)] = (dq.T * scale).astype(BF16)
        if i == steps - 1:
            dk_acc[...] = dk
            dv_acc[...] = dv
        else:
            dk_acc[:end, :] += dk
            dv_acc[:end, :] += dv
    out_ref[:, place(1)] = dk_acc[...].astype(BF16)
    out_ref[:, place(2)] = dv_acc[...].astype(BF16)


def attend_back(projected, attended, grad_attended, lse, lengths, seqs, heads, head_size):
    rows = projected.shape[0]
    seq_len = rows // seqs
    group = 2
    lanes = group * head_size
    groups = heads // group
    tile = 256
    spec = pl.BlockSpec((seq_len, lanes), lambda s, g, n: (s, g))
    return pl.pallas_call(
        functools.partial(attend_back_kernel, head_size, group, tile),
        grid_spec=pltpu.PrefetchScalarGridSpec(
            num_scalar_prefetch=1,
            grid=(seqs, groups),
            in_specs=[
                spec,
                pl.BlockSpec((seq_len, lanes), lambda s, g, n: (s, groups + g)),
                pl.BlockSpec((seq_len, lanes), lambda s, g, n: (s, 2 * groups + g)),
                spec,
                spec,
                pl.BlockSpec((1, 1, group, seq_len), lambda s, g, n: (s, g, 0, 0)),
            ],
            out_specs=pl.BlockSpec((seq_len, 3 * groups * lanes), lambda s, g, n: (s, 0)),
            scratch_shapes=[pltpu.VMEM((seq_len, lanes), F32), pltpu.VMEM((seq_len, lanes), F32)],
        ),
        out_shape=jax.ShapeDtypeStruct((rows, 3 * heads * head_size), BF16),
        compiler_params=pltpu.CompilerParams(vmem_limit_bytes=48 << 20),
        cost_estimate=pl.CostEstimate(
            flops=10 * rows * seq_len * heads * head_size,
            bytes_accessed=16 * rows * heads * head_size,
            transcendentals=rows * seq_len * heads // 2,
        ),
    )(lengths, projected, projected, projected, attended, grad_attended, lse)


def place_kernel(order_ref, out_ref):
    count = out_ref.shape[1]
    tile = order_ref.shape[0]
    step = pl.program_id(0)
    token = lax.broadcasted_iota(jnp.int32, (tile, count), 1)
    index = lax.broadcasted_iota(jnp.int32, (tile, 1), 0) + step * tile
    hit = jnp.sum(jnp.where(order_ref[...] == token, index, 0), axis=0, keepdims=True)

    @pl.when(step == 0)
    def _():
        out_ref[...] = hit

    @pl.when(step > 0)
    def _():
        out_ref[...] += hit


def rank_kernel(key_ref, keys_ref, out_ref):
    step = pl.program_id(0)
    keys = keys_ref[...]
    base = jnp.bitwise_and(keys, -4096)
    key = key_ref[...]
    hit = jnp.sum(jnp.where((key < keys) & (key >= base), 1, 0), axis=0, keepdims=True)

    @pl.when(step == 0)
    def _():
        out_ref[...] = hit

    @pl.when(step > 0)
    def _():
        out_ref[...] += hit


def tall_reduce(kernel, column, rows, count):
    tile = 512
    specs = [pl.BlockSpec((tile, 1), lambda i: (i, 0))]
    specs += [pl.BlockSpec((1, count), lambda i: (0, 0)) for _ in rows]
    return pl.pallas_call(
        kernel,
        grid=(count // tile,),
        in_specs=specs,
        out_specs=pl.BlockSpec((1, count), lambda i: (0, 0)),
        out_shape=jax.ShapeDtypeStruct((1, count), jnp.int32),
        cost_estimate=pl.CostEstimate(
            flops=4 * count * count, bytes_accessed=600 * count, transcendentals=0
        ),
    )(column, *rows)


def token_slots(routes, order, lengths, seq_len, capacity, padded, none):
    count = routes.shape[0]
    places = jnp.arange(count, dtype=jnp.int32)[None]
    limits = jnp.repeat(lengths, seq_len, total_repeat_length=count)[None]
    valid = places % seq_len < limits
    turn = tall_reduce(place_kernel, order.reshape(count, 1), [], count)
    route = routes.reshape(1, count)
    keys = jnp.where(valid, route * 4096 + turn, 1 << 20)
    rank = tall_reduce(rank_kernel, keys.reshape(count, 1), [keys], count)
    return jnp.where(valid & (rank < capacity), route * padded + rank, none)


def pick_kernel(share, experts_step, padded, first_ref, slots_ref, rows_ref, out_ref):
    step = pl.program_id(0)
    start = first_ref[0] + step * experts_step * padded
    count = rows_ref.shape[0]
    slot = lax.broadcasted_iota(jnp.int32, (share, count), 0) + start
    chosen = jnp.where(slots_ref[...] == slot, 1.0, 0.0).astype(BF16)
    out_ref[...] = dot(chosen, rows_ref[...], ((1,), (0,))).astype(BF16)


def pick_rows(rows, slots, first, blocks, share, step, padded):
    count, width = rows.shape
    return pl.pallas_call(
        functools.partial(pick_kernel, share, step, padded),
        grid_spec=pltpu.PrefetchScalarGridSpec(
            num_scalar_prefetch=1,
            grid=(blocks,),
            in_specs=[
                pl.BlockSpec((1, count), lambda i, n: (0, 0)),
                pl.BlockSpec((count, width), lambda i, n: (0, 0)),
            ],
            out_specs=pl.BlockSpec((share, width), lambda i, n: (i, 0)),
        ),
        out_shape=jax.ShapeDtypeStruct((blocks * share, width), BF16),
        compiler_params=pltpu.CompilerParams(vmem_limit_bytes=40 << 20),
        cost_estimate=pl.CostEstimate(
            flops=2 * blocks * share * count * width,
            bytes_accessed=2 * (count + blocks * share) * width,
            transcendentals=0,
        ),
    )(first, slots, rows)


def out_project_kernel(count, first_ref, *refs):
    piece_refs, w_ref, x_ref, out_ref, wide = refs[:count], *refs[count:]
    for i, piece in enumerate(piece_refs):
        width = piece.shape[1]
        start = pl.multiple_of(first_ref[i] * width, width)
        wide[:, pl.ds(start, width)] = piece[...]
    out_ref[...] = (x_ref[...].astype(F32) + dot(wide[...], w_ref[...], ((1,), (0,)))).astype(BF16)


def out_project(pieces, first, weight, tokens):
    rows, width = tokens.shape
    inner = weight.shape[0]
    count = len(pieces)
    tile = 512
    return pl.pallas_call(
        functools.partial(out_project_kernel, count),
        grid_spec=pltpu.PrefetchScalarGridSpec(
            num_scalar_prefetch=1,
            grid=(rows // tile,),
            in_specs=[pl.BlockSpec((tile, p.shape[1]), lambda i, n: (i, 0)) for p in pieces]
            + [
                pl.BlockSpec((inner, width), lambda i, n: (0, 0)),
                pl.BlockSpec((tile, width), lambda i, n: (i, 0)),
            ],
            out_specs=pl.BlockSpec((tile, width), lambda i, n: (i, 0)),
            scratch_shapes=[pltpu.VMEM((tile, inner), BF16)],
        ),
        out_shape=jax.ShapeDtypeStruct((rows, width), BF16),
        compiler_params=pltpu.CompilerParams(vmem_limit_bytes=40 << 20),
        cost_estimate=pl.CostEstimate(
            flops=2 * rows * width * inner,
            bytes_accessed=2 * (3 * rows * width + inner * width),
            transcendentals=0,
        ),
    )(first, *pieces, weight, tokens)


def spread(count, first_ref, place_ref, piece_refs):
    place = place_ref[...]
    total = None
    for i in range(count):
        rows = piece_refs[i].shape[0]
        index = lax.broadcasted_iota(jnp.int32, (place.shape[0], rows), 1) + first_ref[i]
        chosen = jnp.where(place == index, 1.0, 0.0).astype(BF16)
        term = dot(chosen, piece_refs[i][...], ((1,), (0,)))
        total = term if total is None else total + term
    return total


def combine_kernel(count, first_ref, place_ref, base_ref, *refs):
    total = spread(count, first_ref, place_ref, refs[:count])
    refs[count][...] = (base_ref[...].astype(F32) + total).astype(BF16)


def combine_project_kernel(count, first_ref, place_ref, base_ref, *refs):
    total = spread(count, first_ref, place_ref, refs[:count])
    w_ref, out_ref, back_ref = refs[count:]
    out = (base_ref[...].astype(F32) + total).astype(BF16)
    out_ref[...] = out
    back_ref[...] = dot(out, w_ref[...], ((1,), (1,))).astype(BF16)


def combine(pieces, first, place, base, weight=None):
    rows, width = base.shape
    count = len(pieces)
    tile = 256
    block = pl.BlockSpec((tile, width), lambda i, n: (i, 0))
    in_specs = [pl.BlockSpec((tile, 1), lambda i, n: (i, 0)), block]
    in_specs += [pl.BlockSpec(p.shape, lambda i, n: (0, 0), pipeline_mode=pl.Buffered(1)) for p in pieces]
    args = [place, base, *pieces]
    out_specs, out_shape = [block], [jax.ShapeDtypeStruct((rows, width), BF16)]
    kernel = combine_kernel
    table = sum(p.shape[0] for p in pieces)
    flops = 2 * rows * width * table
    if weight is not None:
        inner = weight.shape[0]
        in_specs.append(pl.BlockSpec((inner, width), lambda i, n: (0, 0)))
        args.append(weight)
        out_specs.append(pl.BlockSpec((tile, inner), lambda i, n: (i, 0)))
        out_shape.append(jax.ShapeDtypeStruct((rows, inner), BF16))
        kernel = combine_project_kernel
        flops += 2 * rows * width * inner
    return pl.pallas_call(
        functools.partial(kernel, count),
        grid_spec=pltpu.PrefetchScalarGridSpec(
            num_scalar_prefetch=1, grid=(rows // tile,), in_specs=in_specs, out_specs=out_specs
        ),
        out_shape=out_shape,
        compiler_params=pltpu.CompilerParams(vmem_limit_bytes=48 << 20),
        cost_estimate=pl.CostEstimate(
            flops=flops, bytes_accessed=2 * (2 * rows + table) * width, transcendentals=0
        ),
    )(first, *args)


class Grid:
    def __init__(self, shards, experts):
        self.size = shards
        self.experts = experts
        self.depth = experts // CORES

    def over_core(self, value):
        return lax.ppermute(value, "dp", [(d, d ^ 1) for d in range(self.experts)])

    def over_tensor(self, value, other):
        return lax.ppermute(value, "tensor", [(t, t ^ other) for t in range(self.size)])

    def sum_all(self, value):
        step = 1
        while step < self.size:
            value = value + self.over_tensor(value, step)
            step *= 2
        step = 1
        while step < self.experts:
            pairs = [(d, d ^ step) for d in range(self.experts)]
            value = value + lax.ppermute(value, "dp", pairs)
            step *= 2
        return value

    def exchange_depth(self, value):
        groups = [[CORES * z + c for z in range(self.depth)] for c in range(CORES)]
        return lax.all_to_all(
            value, "dp", split_axis=0, concat_axis=0, axis_index_groups=groups, tiled=True
        )


def slice_half(value, half, axis):
    width = value.shape[axis] // 2
    return lax.dynamic_slice_in_dim(value, half * width, width, axis)


def owner_pairs(grid, flip, back=False):
    pairs = []
    for z in range(grid.depth):
        for core in range(CORES):
            for y in range(2):
                for x in range(2):
                    here = (CORES * z + core) * 4 + 2 * y + x
                    there = (CORES * z + (x ^ flip)) * 4 + 2 * y + core
                    pairs.append((there, here) if back else (here, there))
    return pairs


def fetch_halves(grid, weight, axis):
    core = lax.axis_index("dp") % CORES
    me = lax.axis_index("tensor")
    if grid.size == 4:
        near = [
            lax.ppermute(
                slice_half(weight, jnp.bitwise_xor(me % 2, flip), axis),
                ("dp", "tensor"),
                owner_pairs(grid, flip),
            )
            for flip in range(2)
        ]
        return near + [grid.over_tensor(piece, 2) for piece in near]
    every = lax.all_gather(weight, "tensor", axis=0, tiled=False)
    chosen = jnp.where(me % 2 == core, every, grid.over_core(every))
    return [slice_half(chosen[t], core, axis) for t in range(grid.size)]


def return_halves(grid, pieces, axis):
    core = lax.axis_index("dp") % CORES
    me = lax.axis_index("tensor")
    if grid.size == 4:
        halves = []
        for flip in range(2):
            far = grid.over_tensor(pieces[2 + flip].astype(BF16), 2)
            total = pieces[flip] + far.astype(F32)
            halves.append(
                lax.ppermute(total.astype(BF16), ("dp", "tensor"), owner_pairs(grid, flip, True))
            )
        swapped = me % 2 == 1
    else:
        stacked = jnp.stack(pieces).astype(BF16)
        wide = jnp.stack([jnp.where(me % 2 == p, stacked, jnp.zeros_like(stacked)) for p in range(2)])
        mine = lax.psum_scatter(wide, "tensor", scatter_dimension=1, tiled=False)
        halves = [
            jnp.where(core == 0, mine[0], mine[1]),
            grid.over_core(jnp.where(core == 0, mine[1], mine[0])),
        ]
        swapped = core == 1
    halves = [half.astype(F32) for half in halves]
    return jnp.where(swapped, jnp.concatenate(halves[::-1], axis), jnp.concatenate(halves, axis))


def gather_pieces(grid, value, balanced):
    if grid.size != 4:
        every = lax.all_gather(value, "tensor", axis=0, tiled=True)
        return [every], [jnp.int32(0)], [0]
    me = lax.axis_index("tensor")
    if not balanced:
        from_y = grid.over_tensor(value, 2)
        from_x = grid.over_tensor(value, 1)
        from_xy = grid.over_tensor(from_y, 1)
        return [value, from_x, from_y, from_xy], [jnp.bitwise_xor(me, o) for o in range(4)], [0] * 4
    half = value.shape[0] // 2
    first, second = value[:half], value[half:]
    first_x = grid.over_tensor(first, 1)
    second_y = grid.over_tensor(second, 2)
    first_y = grid.over_tensor(first, 2)
    second_x = grid.over_tensor(second, 1)
    first_xy = grid.over_tensor(first_x, 2)
    second_xy = grid.over_tensor(second_y, 1)
    pieces = [value, first_x, second_x, first_y, second_y, first_xy, second_xy]
    devices = [jnp.bitwise_xor(me, o) for o in (0, 1, 1, 2, 2, 3, 3)]
    return pieces, devices, [0, 0, half, 0, half, 0, half]


def gather_rows(grid, value, balanced=True):
    pieces, devices, starts = gather_pieces(grid, value, balanced)
    if len(pieces) == 1:
        return pieces[0]
    rows, width = value.shape
    out = jnp.zeros((grid.size * rows, width), value.dtype)
    for piece, device, start in zip(pieces, devices, starts):
        out = lax.dynamic_update_slice(out, piece, (device * rows + start, 0))
    return out


def scatter_rows(grid, term):
    size, rows, width = term.shape
    if size != 4:
        return lax.psum_scatter(term.astype(BF16), "tensor", scatter_dimension=0, tiled=False).astype(F32)
    me = lax.axis_index("tensor")
    half = width // 2

    def pick(other, low):
        place = jnp.bitwise_xor(me, other)
        return lax.dynamic_slice(term, (place, 0, low), (1, rows, half))[0]

    totals = []
    for low, near, far in ((0, 1, 2), (half, 2, 1)):
        got_far = grid.over_tensor(pick(3, low).astype(BF16), near)
        got_own = grid.over_tensor(pick(near, low).astype(BF16), near)
        onward = pick(far, low).astype(F32) + got_far.astype(F32)
        got = grid.over_tensor(onward.astype(BF16), far)
        totals.append(pick(0, low).astype(F32) + got_own.astype(F32) + got.astype(F32))
    return jnp.concatenate(totals, axis=1)


def gelu_pair(pre):
    cdf = 0.5 * (1.0 + lax.erf(pre * (2.0**-0.5)))
    density = jnp.exp(-0.5 * pre * pre) * ((2.0 * math.pi) ** -0.5)
    return (pre * cdf).astype(BF16), (cdf + pre * density).astype(BF16)


def body(
    tokens,
    lengths,
    routes,
    fill_order,
    norm_gain,
    norm_bias,
    qkv_weight,
    out_weight,
    centroids,
    expert_in,
    expert_out,
    cotangent,
):
    tok_count, model_width = tokens.shape
    seq_count = lengths.shape[0]
    seq_len = tok_count // seq_count
    heads_here = qkv_weight.shape[1]
    head_size = out_weight.shape[1]
    experts = lax.axis_size("dp")
    shards = lax.axis_size("tensor")
    grid = Grid(shards, experts)
    me = lax.axis_index("tensor")
    parity, part = me % 2, me // 2
    core = lax.axis_index("dp") % CORES
    depth = experts // CORES
    row_parts = shards // 2
    capacity = (9 * tok_count + 8 * experts - 1) // (8 * experts)
    share = 16 * -(-capacity // (16 * row_parts))
    padded = share * row_parts
    own_rows = depth * share
    tok_rows = tok_count // shards

    win, wout = [], []
    for k in range(2):
        win.append(fetch_halves(grid, expert_in[0, k], 1))
        wout.append(fetch_halves(grid, expert_out[0, k], 0))
    out_flat = out_weight.reshape(heads_here * head_size, model_width)
    out_all = gather_rows(grid, out_flat, False)
    centroid = jnp.where(parity == core, centroids[0], grid.over_core(centroids[0]))

    slots = token_slots(
        routes, fill_order, lengths, seq_len, capacity, padded, experts * padded
    )
    slot = slots.reshape(tok_count, 1)
    rank = slot % padded
    slot_device = (rank // share) * 2 + (slot // padded) % 2
    slot_place = (slot_device * depth + slot // (2 * padded)) * share + rank % share
    place = jnp.where(slot < experts * padded, slot_place, -1)
    own_first = (parity * padded + part * share).astype(jnp.int32).reshape(1)

    def to_experts(rows):
        picked = pick_rows(rows, slots, own_first, depth, share, CORES, padded)
        return grid.exchange_depth(picked.reshape(depth, share, model_width)).reshape(own_rows, model_width)

    def from_experts(rows, balanced):
        moved = grid.exchange_depth(rows.reshape(depth, share, model_width))
        pieces, devices, starts = gather_pieces(grid, moved.reshape(own_rows, model_width), balanced)
        first = [device * own_rows + start for device, start in zip(devices, starts)]
        return pieces, jnp.stack(first).astype(jnp.int32)

    grad_ret = to_experts(cotangent).astype(F32)
    heads = heads_here + heads_here % 2
    fused = qkv_weight.reshape(model_width, heads_here, 3, head_size)
    fused = jnp.swapaxes(fused, 1, 2)
    fused = jnp.pad(fused, ((0, 0), (0, 0), (0, heads - heads_here), (0, 0)))
    fused = fused.reshape(model_width, 3 * heads * head_size)
    inner = heads_here * head_size
    ln_in, projected = norm_project(tokens, norm_gain, norm_bias, fused)
    attended, log_total = attend(projected, lengths, seq_count, heads, head_size)
    if shards == 4:
        pieces, devices, unused = gather_pieces(grid, attended, False)
        first = jnp.stack(devices).astype(jnp.int32)
    else:
        every = lax.all_gather(attended[:, :inner], "tensor", axis=1, tiled=True)
        pieces, first = [every], jnp.zeros((1,), jnp.int32)
    sent = out_project(pieces, first, out_all, tokens)

    def both_cores(value):
        return jnp.concatenate([value, grid.over_core(value)], axis=0)

    def sum_cores(total):
        return total[:own_rows] + grid.over_core(total[own_rows:].astype(BF16)).astype(F32)

    expert_rows = to_experts(sent)
    gate = jax.nn.sigmoid(jnp.dot(expert_rows, centroid, preferred_element_type=F32))[:, None]
    current = expert_rows.astype(F32)
    saved = []
    for k in range(2):
        rows_in = both_cores(current.astype(BF16))
        acts, slopes = [], []
        total = None
        for w_in, w_out in zip(win[k], wout[k]):
            act, slope = gelu_pair(dot(rows_in, w_in, ((1,), (0,))))
            term = dot(act, w_out, ((1,), (0,)))
            total = term if total is None else total + term
            acts.append(act)
            slopes.append(slope)
        current = current + sum_cores(total)
        saved.append((rows_in, acts, slopes))
    pieces, first = from_experts((gate * current).astype(BF16), False)
    output = combine(pieces, first, place, sent)[0]

    grad_gate = jnp.sum(grad_ret * current, axis=1, keepdims=True)
    grad_logit = grad_gate * gate * (1.0 - gate)
    grad_current = gate * grad_ret
    grads_in = [None, None]
    grads_back = [None, None]
    for k in (1, 0):
        rows_in, acts, slopes = saved[k]
        branch = both_cores(grad_current.astype(BF16))
        total = None
        in_parts, out_parts = [], []
        for w_in, w_out, act, slope in zip(win[k], wout[k], acts, slopes):
            grad_pre = (dot(branch, w_out, ((1,), (1,))) * slope.astype(F32)).astype(BF16)
            term = dot(grad_pre, w_in, ((1,), (1,)))
            total = term if total is None else total + term
            out_parts.append(dot(act, branch, ((0,), (0,))))
            in_parts.append(dot(rows_in, grad_pre, ((0,), (0,))))
        grad_current = grad_current + sum_cores(total)
        grads_in[k] = return_halves(grid, in_parts, 1)
        grads_back[k] = return_halves(grid, out_parts, 0)
    grad_rows = (grad_current + grad_logit * centroid.astype(F32)[None, :]).astype(BF16)
    centroid_part = jnp.sum(grad_logit * expert_rows.astype(F32), axis=0, keepdims=True)
    centroid_parts = lax.psum(
        jnp.concatenate([jnp.where(parity == p, centroid_part, 0.0) for p in range(2)], axis=0), "tensor"
    )
    centroid_parts = centroid_parts + grid.over_core(centroid_parts)
    grad_centroid = lax.dynamic_slice_in_dim(centroid_parts, core, 1, 0)
    pieces, first = from_experts(grad_rows, True)
    out_padded = jnp.pad(out_flat, ((0, heads * head_size - inner), (0, 0)))
    grad_mixed, grad_attended = combine(pieces, first, place, cotangent, out_padded)
    grad_out_local = dot(attended[:, :inner], grad_mixed, ((0,), (0,))).reshape(
        heads_here, head_size, model_width
    )
    grad_projected = attend_back(
        projected, attended, grad_attended, log_total, lengths, seq_count, heads, head_size
    )
    grad_qkv_local = dot(ln_in, grad_projected, ((0,), (0,)))
    grad_ln_part = dot(grad_projected, fused, ((1,), (1,))).astype(BF16)
    grad_ln = scatter_rows(grid, grad_ln_part.reshape(shards, tok_rows, model_width))

    def own(rows):
        return lax.dynamic_slice_in_dim(rows, me * tok_rows, tok_rows, 0)

    own_tokens = own(tokens).astype(F32)
    centre = own_tokens - jnp.mean(own_tokens, axis=1, keepdims=True)
    own_scale = lax.rsqrt(jnp.mean(centre * centre, axis=1, keepdims=True) + EPSILON)
    own_normed = centre * own_scale
    grad_normed = grad_ln * norm_gain
    mean_plain = jnp.mean(grad_normed, axis=1, keepdims=True)
    mean_cross = jnp.mean(grad_normed * own_normed, axis=1, keepdims=True)
    grad_input = own(grad_mixed).astype(F32) + own_scale * (
        grad_normed - mean_plain - own_normed * mean_cross
    )
    grad_tokens = gather_rows(grid, grad_input.astype(BF16))
    norm_total = jnp.stack([jnp.sum(grad_ln * own_normed, axis=0), jnp.sum(grad_ln, axis=0)])
    norm_total = grid.sum_all(norm_total)
    norm_total = lax.dynamic_slice_in_dim(
        norm_total, me * (model_width // shards), model_width // shards, 1
    )
    grad_qkv, grad_out_weight = lax.psum(
        (grad_qkv_local.astype(BF16), grad_out_local.astype(BF16)), "dp"
    )
    grad_qkv = grad_qkv.astype(F32).reshape(model_width, 3, heads, head_size)[:, :, :heads_here]
    grad_qkv_weight = jnp.swapaxes(grad_qkv, 1, 2).reshape(model_width, heads_here, 3 * head_size)
    return (
        output,
        grad_tokens,
        norm_total[0],
        norm_total[1],
        grad_qkv_weight,
        grad_out_weight.astype(F32),
        grad_centroid,
        jnp.stack(grads_in)[None],
        jnp.stack(grads_back)[None],
    )


def solution(mesh):
    return jax.shard_map(
        body,
        mesh=mesh,
        in_specs=(
            P("dp", None),
            P("dp"),
            P("dp", None),
            P("dp", None),
            P(),
            P(),
            P(None, "tensor", None),
            P("tensor", None, None),
            P("dp", None),
            P("dp", None, None, "tensor"),
            P("dp", None, "tensor", None),
            P("dp", None),
        ),
        out_specs=(
            P("dp", None),
            P("dp", None),
            P("tensor"),
            P("tensor"),
            P(None, "tensor", None),
            P("tensor", None, None),
            P("dp", None),
            P("dp", None, None, "tensor"),
            P("dp", None, "tensor", None),
        ),
        check_vma=False,
    )
```

```python
import functools
import math

import jax
import jax.numpy as jnp
from jax import lax
from jax.experimental import pallas as pl
from jax.experimental.pallas import tpu as pltpu
from jax.sharding import PartitionSpec as P

EPSILON = 1e-05
MASKED = -1e30
F32 = jnp.float32
BF16 = jnp.bfloat16
CORES = 2


def dot(a, b, contract):
    return lax.dot_general(a, b, (contract, ((), ())), preferred_element_type=F32)


def norm_project_kernel(x_ref, gain_ref, bias_ref, w_ref, ln_ref, out_ref):
    x = x_ref[...].astype(F32)
    centre = x - jnp.mean(x, axis=1, keepdims=True)
    scale = lax.rsqrt(jnp.mean(centre * centre, axis=1, keepdims=True) + EPSILON)
    ln = (centre * scale * gain_ref[...] + bias_ref[...]).astype(BF16)
    ln_ref[...] = ln
    out_ref[...] = dot(ln, w_ref[...], ((1,), (0,))).astype(BF16)


def norm_project(tokens, gain, bias, weight):
    rows, width = tokens.shape
    columns = weight.shape[1]
    tile = 512
    return pl.pallas_call(
        norm_project_kernel,
        grid=(rows // tile,),
        in_specs=[
            pl.BlockSpec((tile, width), lambda i: (i, 0)),
            pl.BlockSpec((1, width), lambda i: (0, 0)),
            pl.BlockSpec((1, width), lambda i: (0, 0)),
            pl.BlockSpec((width, columns), lambda i: (0, 0)),
        ],
        out_specs=[
            pl.BlockSpec((tile, width), lambda i: (i, 0)),
            pl.BlockSpec((tile, columns), lambda i: (i, 0)),
        ],
        out_shape=[
            jax.ShapeDtypeStruct((rows, width), BF16),
            jax.ShapeDtypeStruct((rows, columns), BF16),
        ],
        compiler_params=pltpu.CompilerParams(vmem_limit_bytes=40 << 20),
        cost_estimate=pl.CostEstimate(
            flops=2 * rows * width * columns,
            bytes_accessed=2 * (2 * rows * width + rows * columns + width * columns),
            transcendentals=rows,
        ),
    )(tokens, gain[None], bias[None], weight)


def attend_kernel(head_size, group, tile, len_ref, q_ref, k_ref, v_ref, o_ref, lse_ref):
    seq_len, lanes = q_ref.shape
    scale = head_size**-0.5
    limit = len_ref[pl.program_id(0)]
    keys = k_ref[...]
    values = v_ref[...]
    key_place = lax.broadcasted_iota(jnp.int32, (seq_len, lanes), 0)
    lane = lax.broadcasted_iota(jnp.int32, (seq_len, lanes), 1)
    causal = lax.broadcasted_iota(jnp.int32, (tile, tile), 0) <= lax.broadcasted_iota(
        jnp.int32, (tile, tile), 1
    )
    tall = lax.broadcasted_iota(jnp.int32, (lanes, tile), 0)
    lane_q = lax.broadcasted_iota(jnp.int32, (tile, lanes), 1)
    heads = []
    for a in range(group):
        mine = (lane >= a * head_size) & (lane < (a + 1) * head_size)
        spare = ((a + 1) % group) * head_size
        extra = jnp.where((lane == spare) & (key_place >= limit), MASKED, 0.0).astype(BF16)
        k_a = jnp.where(mine, keys, extra)
        v_a = jnp.where(mine, values, jnp.ones((), BF16))
        heads.append((k_a, v_a, spare))
    for i in range(seq_len // tile):
        end = (i + 1) * tile
        q = (q_ref[i * tile : end, :].astype(F32) * scale).astype(BF16)
        out = None
        for a in range(group):
            k_a, v_a, spare = heads[a]
            mine_q = (lane_q >= a * head_size) & (lane_q < (a + 1) * head_size)
            q_a = jnp.where(mine_q, q, jnp.where(lane_q == spare, 1.0, 0.0).astype(BF16))
            scores = dot(k_a[:end], q_a, ((1,), (1,)))
            last = jnp.where(causal, scores[i * tile :], MASKED)
            scores = jnp.concatenate([scores[: i * tile], last], axis=0) if i else last
            top = jnp.max(scores, axis=0, keepdims=True)
            probs = jnp.exp(scores - top).astype(BF16)
            result = dot(v_a[:end], probs, ((0,), (0,)))
            total = result[spare : spare + 1, :]
            lse_ref[0, 0, a : a + 1, i * tile : end] = top + jnp.log(total)
            result = result / total
            if out is None:
                out = result
            else:
                out = jnp.where((tall >= a * head_size) & (tall < (a + 1) * head_size), result, out)
        o_ref[i * tile : end, :] = out.T.astype(BF16)


def attend(projected, lengths, seqs, heads, head_size):
    rows = projected.shape[0]
    seq_len = rows // seqs
    group = 2
    lanes = group * head_size
    groups = heads // group
    tile = 256
    return pl.pallas_call(
        functools.partial(attend_kernel, head_size, group, tile),
        grid_spec=pltpu.PrefetchScalarGridSpec(
            num_scalar_prefetch=1,
            grid=(seqs, groups),
            in_specs=[
                pl.BlockSpec((seq_len, lanes), lambda s, g, n: (s, g)),
                pl.BlockSpec((seq_len, lanes), lambda s, g, n: (s, groups + g)),
                pl.BlockSpec((seq_len, lanes), lambda s, g, n: (s, 2 * groups + g)),
            ],
            out_specs=[
                pl.BlockSpec((seq_len, lanes), lambda s, g, n: (s, g)),
                pl.BlockSpec((1, 1, group, seq_len), lambda s, g, n: (s, g, 0, 0)),
            ],
        ),
        out_shape=[
            jax.ShapeDtypeStruct((rows, heads * head_size), BF16),
            jax.ShapeDtypeStruct((seqs, groups, group, seq_len), F32),
        ],
        compiler_params=pltpu.CompilerParams(vmem_limit_bytes=40 << 20),
        cost_estimate=pl.CostEstimate(
            flops=4 * rows * seq_len * heads * head_size,
            bytes_accessed=8 * rows * heads * head_size,
            transcendentals=rows * seq_len * heads // 2,
        ),
    )(lengths, projected, projected, projected)


def attend_back_kernel(head_size, group, tile, len_ref, q_ref, k_ref, v_ref, o_ref, do_ref, lse_ref, out_ref, dk_acc, dv_acc):
    seq_len, lanes = q_ref.shape
    scale = head_size**-0.5
    limit = len_ref[pl.program_id(0)]
    keys = k_ref[...]
    values = v_ref[...]
    zero = jnp.zeros((), BF16)

    def place(kind):
        block = kind * pl.num_programs(1) + pl.program_id(1)
        return pl.ds(pl.multiple_of(block * lanes, lanes), lanes)

    key_place = lax.broadcasted_iota(jnp.int32, (seq_len, lanes), 0)
    lane = lax.broadcasted_iota(jnp.int32, (seq_len, lanes), 1)
    causal = lax.broadcasted_iota(jnp.int32, (tile, tile), 0) <= lax.broadcasted_iota(
        jnp.int32, (tile, tile), 1
    )
    lane_q = lax.broadcasted_iota(jnp.int32, (tile, lanes), 1)
    heads = []
    for a in range(group):
        mine = (lane >= a * head_size) & (lane < (a + 1) * head_size)
        spare = ((a + 1) % group) * head_size
        extra = jnp.where((lane == spare) & (key_place >= limit), MASKED, 0.0).astype(BF16)
        k_a = jnp.where(mine, keys, extra)
        ones = jnp.where((lane == spare) | (lane == spare + 1), 1.0, 0.0).astype(BF16)
        v_a = jnp.where(mine, values, ones)
        heads.append((k_a, v_a, spare))
    steps = seq_len // tile
    for i in reversed(range(steps)):
        end = (i + 1) * tile
        q = (q_ref[i * tile : end, :].astype(F32) * scale).astype(BF16)
        do = do_ref[i * tile : end, :]
        product = do.astype(F32) * o_ref[i * tile : end, :].astype(F32)
        dq = None
        dk = None
        dv = None
        for a in range(group):
            k_a, v_a, spare = heads[a]
            mine_q = (lane_q >= a * head_size) & (lane_q < (a + 1) * head_size)
            q_m = jnp.where(mine_q, q, zero)
            q_a = jnp.where(mine_q, q, jnp.where(lane_q == spare, 1.0, 0.0).astype(BF16))
            delta = -jnp.sum(jnp.where(mine_q, product, 0.0), axis=1, keepdims=True)
            high = delta.astype(BF16)
            low = (delta - high.astype(F32)).astype(BF16)
            do_m = jnp.where(mine_q, do, zero)
            do_a = jnp.where(lane_q == spare, high, jnp.where(lane_q == spare + 1, low, do_m))
            scores = dot(k_a[:end], q_a, ((1,), (1,)))
            last = jnp.where(causal, scores[i * tile :], MASKED)
            scores = jnp.concatenate([scores[: i * tile], last], axis=0) if i else last
            probs = jnp.exp(scores - lse_ref[0, 0, a : a + 1, i * tile : end])
            grad = dot(v_a[:end], do_a, ((1,), (1,)))
            grad = (probs * grad).astype(BF16)
            term_v = dot(probs.astype(BF16), do_m, ((1,), (0,)))
            term_k = dot(grad, q_m, ((1,), (0,)))
            term_q = dot(k_a[:end], grad, ((0,), (0,)))
            dv = term_v if dv is None else dv + term_v
            dk = term_k if dk is None else dk + term_k
            if dq is None:
                dq = term_q
            else:
                tall = lax.broadcasted_iota(jnp.int32, (lanes, tile), 0)
                dq = jnp.where((tall >= a * head_size) & (tall < (a + 1) * head_size), term_q, dq)
        out_ref[i * tile : end, place(0)] = (dq.T * scale).astype(BF16)
        if i == steps - 1:
            dk_acc[...] = dk
            dv_acc[...] = dv
        else:
            dk_acc[:end, :] += dk
            dv_acc[:end, :] += dv
    out_ref[:, place(1)] = dk_acc[...].astype(BF16)
    out_ref[:, place(2)] = dv_acc[...].astype(BF16)


def attend_back(projected, attended, grad_attended, lse, lengths, seqs, heads, head_size):
    rows = projected.shape[0]
    seq_len = rows // seqs
    group = 2
    lanes = group * head_size
    groups = heads // group
    tile = 256
    spec = pl.BlockSpec((seq_len, lanes), lambda s, g, n: (s, g))
    return pl.pallas_call(
        functools.partial(attend_back_kernel, head_size, group, tile),
        grid_spec=pltpu.PrefetchScalarGridSpec(
            num_scalar_prefetch=1,
            grid=(seqs, groups),
            in_specs=[
                spec,
                pl.BlockSpec((seq_len, lanes), lambda s, g, n: (s, groups + g)),
                pl.BlockSpec((seq_len, lanes), lambda s, g, n: (s, 2 * groups + g)),
                spec,
                spec,
                pl.BlockSpec((1, 1, group, seq_len), lambda s, g, n: (s, g, 0, 0)),
            ],
            out_specs=pl.BlockSpec((seq_len, 3 * groups * lanes), lambda s, g, n: (s, 0)),
            scratch_shapes=[pltpu.VMEM((seq_len, lanes), F32), pltpu.VMEM((seq_len, lanes), F32)],
        ),
        out_shape=jax.ShapeDtypeStruct((rows, 3 * heads * head_size), BF16),
        compiler_params=pltpu.CompilerParams(vmem_limit_bytes=48 << 20),
        cost_estimate=pl.CostEstimate(
            flops=10 * rows * seq_len * heads * head_size,
            bytes_accessed=16 * rows * heads * head_size,
            transcendentals=rows * seq_len * heads // 2,
        ),
    )(lengths, projected, projected, projected, attended, grad_attended, lse)


def place_kernel(order_ref, out_ref):
    count = out_ref.shape[1]
    tile = order_ref.shape[0]
    step = pl.program_id(0)
    token = lax.broadcasted_iota(jnp.int32, (tile, count), 1)
    index = lax.broadcasted_iota(jnp.int32, (tile, 1), 0) + step * tile
    hit = jnp.sum(jnp.where(order_ref[...] == token, index, 0), axis=0, keepdims=True)

    @pl.when(step == 0)
    def _():
        out_ref[...] = hit

    @pl.when(step > 0)
    def _():
        out_ref[...] += hit


def rank_kernel(key_ref, keys_ref, out_ref):
    step = pl.program_id(0)
    keys = keys_ref[...]
    base = jnp.bitwise_and(keys, -4096)
    key = key_ref[...]
    hit = jnp.sum(jnp.where((key < keys) & (key >= base), 1, 0), axis=0, keepdims=True)

    @pl.when(step == 0)
    def _():
        out_ref[...] = hit

    @pl.when(step > 0)
    def _():
        out_ref[...] += hit


def tall_reduce(kernel, column, rows, count):
    tile = 512
    specs = [pl.BlockSpec((tile, 1), lambda i: (i, 0))]
    specs += [pl.BlockSpec((1, count), lambda i: (0, 0)) for _ in rows]
    return pl.pallas_call(
        kernel,
        grid=(count // tile,),
        in_specs=specs,
        out_specs=pl.BlockSpec((1, count), lambda i: (0, 0)),
        out_shape=jax.ShapeDtypeStruct((1, count), jnp.int32),
        cost_estimate=pl.CostEstimate(
            flops=4 * count * count, bytes_accessed=600 * count, transcendentals=0
        ),
    )(column, *rows)


def token_slots(routes, order, lengths, seq_len, capacity, padded, none):
    count = routes.shape[0]
    places = jnp.arange(count, dtype=jnp.int32)[None]
    limits = jnp.repeat(lengths, seq_len, total_repeat_length=count)[None]
    valid = places % seq_len < limits
    turn = tall_reduce(place_kernel, order.reshape(count, 1), [], count)
    route = routes.reshape(1, count)
    keys = jnp.where(valid, route * 4096 + turn, 1 << 20)
    rank = tall_reduce(rank_kernel, keys.reshape(count, 1), [keys], count)
    return jnp.where(valid & (rank < capacity), route * padded + rank, none)


def pick_kernel(share, experts_step, padded, first_ref, slots_ref, rows_ref, out_ref):
    step = pl.program_id(0)
    start = first_ref[0] + step * experts_step * padded
    count = rows_ref.shape[0]
    slot = lax.broadcasted_iota(jnp.int32, (share, count), 0) + start
    chosen = jnp.where(slots_ref[...] == slot, 1.0, 0.0).astype(BF16)
    out_ref[...] = dot(chosen, rows_ref[...], ((1,), (0,))).astype(BF16)


def pick_rows(rows, slots, first, blocks, share, step, padded):
    count, width = rows.shape
    return pl.pallas_call(
        functools.partial(pick_kernel, share, step, padded),
        grid_spec=pltpu.PrefetchScalarGridSpec(
            num_scalar_prefetch=1,
            grid=(blocks,),
            in_specs=[
                pl.BlockSpec((1, count), lambda i, n: (0, 0)),
                pl.BlockSpec((count, width), lambda i, n: (0, 0)),
            ],
            out_specs=pl.BlockSpec((share, width), lambda i, n: (i, 0)),
        ),
        out_shape=jax.ShapeDtypeStruct((blocks * share, width), BF16),
        compiler_params=pltpu.CompilerParams(vmem_limit_bytes=40 << 20),
        cost_estimate=pl.CostEstimate(
            flops=2 * blocks * share * count * width,
            bytes_accessed=2 * (count + blocks * share) * width,
            transcendentals=0,
        ),
    )(first, slots, rows)


def out_project_kernel(count, first_ref, *refs):
    piece_refs, w_ref, x_ref, out_ref, wide = refs[:count], *refs[count:]
    for i, piece in enumerate(piece_refs):
        width = piece.shape[1]
        start = pl.multiple_of(first_ref[i] * width, width)
        wide[:, pl.ds(start, width)] = piece[...]
    out_ref[...] = (x_ref[...].astype(F32) + dot(wide[...], w_ref[...], ((1,), (0,)))).astype(BF16)


def out_project(pieces, first, weight, tokens):
    rows, width = tokens.shape
    inner = weight.shape[0]
    count = len(pieces)
    tile = 512
    return pl.pallas_call(
        functools.partial(out_project_kernel, count),
        grid_spec=pltpu.PrefetchScalarGridSpec(
            num_scalar_prefetch=1,
            grid=(rows // tile,),
            in_specs=[pl.BlockSpec((tile, p.shape[1]), lambda i, n: (i, 0)) for p in pieces]
            + [
                pl.BlockSpec((inner, width), lambda i, n: (0, 0)),
                pl.BlockSpec((tile, width), lambda i, n: (i, 0)),
            ],
            out_specs=pl.BlockSpec((tile, width), lambda i, n: (i, 0)),
            scratch_shapes=[pltpu.VMEM((tile, inner), BF16)],
        ),
        out_shape=jax.ShapeDtypeStruct((rows, width), BF16),
        compiler_params=pltpu.CompilerParams(vmem_limit_bytes=40 << 20),
        cost_estimate=pl.CostEstimate(
            flops=2 * rows * width * inner,
            bytes_accessed=2 * (3 * rows * width + inner * width),
            transcendentals=0,
        ),
    )(first, *pieces, weight, tokens)


def spread(count, first_ref, place_ref, piece_refs):
    place = place_ref[...]
    total = None
    for i in range(count):
        rows = piece_refs[i].shape[0]
        index = lax.broadcasted_iota(jnp.int32, (place.shape[0], rows), 1) + first_ref[i]
        chosen = jnp.where(place == index, 1.0, 0.0).astype(BF16)
        term = dot(chosen, piece_refs[i][...], ((1,), (0,)))
        total = term if total is None else total + term
    return total


def combine_kernel(count, first_ref, place_ref, base_ref, *refs):
    total = spread(count, first_ref, place_ref, refs[:count])
    refs[count][...] = (base_ref[...].astype(F32) + total).astype(BF16)


def combine_project_kernel(count, first_ref, place_ref, base_ref, *refs):
    total = spread(count, first_ref, place_ref, refs[:count])
    w_ref, out_ref, back_ref = refs[count:]
    out = (base_ref[...].astype(F32) + total).astype(BF16)
    out_ref[...] = out
    back_ref[...] = dot(out, w_ref[...], ((1,), (1,))).astype(BF16)


def combine(pieces, first, place, base, weight=None):
    rows, width = base.shape
    count = len(pieces)
    tile = 512
    block = pl.BlockSpec((tile, width), lambda i, n: (i, 0))
    in_specs = [pl.BlockSpec((tile, 1), lambda i, n: (i, 0)), block]
    in_specs += [pl.BlockSpec(p.shape, lambda i, n: (0, 0), pipeline_mode=pl.Buffered(1)) for p in pieces]
    args = [place, base, *pieces]
    out_specs, out_shape = [block], [jax.ShapeDtypeStruct((rows, width), BF16)]
    kernel = combine_kernel
    table = sum(p.shape[0] for p in pieces)
    flops = 2 * rows * width * table
    if weight is not None:
        inner = weight.shape[0]
        in_specs.append(pl.BlockSpec((inner, width), lambda i, n: (0, 0)))
        args.append(weight)
        out_specs.append(pl.BlockSpec((tile, inner), lambda i, n: (i, 0)))
        out_shape.append(jax.ShapeDtypeStruct((rows, inner), BF16))
        kernel = combine_project_kernel
        flops += 2 * rows * width * inner
    return pl.pallas_call(
        functools.partial(kernel, count),
        grid_spec=pltpu.PrefetchScalarGridSpec(
            num_scalar_prefetch=1, grid=(rows // tile,), in_specs=in_specs, out_specs=out_specs
        ),
        out_shape=out_shape,
        compiler_params=pltpu.CompilerParams(vmem_limit_bytes=48 << 20),
        cost_estimate=pl.CostEstimate(
            flops=flops, bytes_accessed=2 * (2 * rows + table) * width, transcendentals=0
        ),
    )(first, *args)


def gelu_pair(pre):
    cdf = 0.5 + 0.5 * lax.erf(pre * (2.0**-0.5))
    density = jnp.exp(-0.5 * pre * pre) * ((2.0 * math.pi) ** -0.5)
    return (pre * cdf).astype(BF16), (cdf + pre * density).astype(BF16)


def without_base(kernel, count):
    def wrapped(*refs):
        kernel(*refs[:count], None, *refs[count:])

    return wrapped


def expert_forward_kernel(count, x_ref, base_ref, *refs):
    w_in, w_out = refs[:count], refs[count : 2 * count]
    act_ref, slope_ref, out_ref = refs[2 * count :]
    x = x_ref[...]
    total = base_ref[...] if base_ref is not None else None
    width = w_in[0].shape[1]
    chunk = min(width, 1024)
    blocks = [(i, c) for i in range(count) for c in range(0, width, chunk)]

    def into(i, c):
        return dot(x, w_in[i][:, c : c + chunk], ((1,), (0,)))

    ahead = into(*blocks[0])
    for n, (i, c) in enumerate(blocks):
        pre = ahead
        if n + 1 < len(blocks):
            ahead = into(*blocks[n + 1])
        act, slope = gelu_pair(pre)
        act_ref[:, i * width + c : i * width + c + chunk] = act
        slope_ref[:, i * width + c : i * width + c + chunk] = slope
        term = dot(act, w_out[i][c : c + chunk, :], ((1,), (0,)))
        total = term if total is None else total + term
    out_ref[...] = total.astype(out_ref.dtype)


def expert_forward(x, w_in, w_out, base=None):
    rows, width = x.shape
    count = len(w_in)
    hidden = sum(w.shape[1] for w in w_in)
    tile = rows // 2

    def row(n):
        return pl.BlockSpec((tile, n), lambda i: (i, 0))

    specs = [row(width)]
    args = [x]
    kernel = functools.partial(expert_forward_kernel, count)
    if base is not None:
        specs.append(row(width))
        args.append(base)
    else:
        kernel = without_base(kernel, 1)
    specs += [pl.BlockSpec(w.shape, lambda i: (0, 0), pipeline_mode=pl.Buffered(1)) for w in (*w_in, *w_out)]
    return pl.pallas_call(
        kernel,
        grid=(rows // tile,),
        in_specs=specs,
        out_specs=[row(hidden), row(hidden), row(width)],
        out_shape=[
            jax.ShapeDtypeStruct((rows, hidden), BF16),
            jax.ShapeDtypeStruct((rows, hidden), BF16),
            jax.ShapeDtypeStruct((rows, width), BF16 if base is None else F32),
        ],
        compiler_params=pltpu.CompilerParams(vmem_limit_bytes=48 << 20),
        cost_estimate=pl.CostEstimate(
            flops=4 * rows * width * hidden,
            bytes_accessed=4 * width * hidden + 4 * rows * hidden + 6 * rows * width,
            transcendentals=2 * rows * hidden,
        ),
    )(*args, *w_in, *w_out)


def expert_backward_kernel(count, g_ref, slope_ref, base_ref, *refs):
    w_in, w_out = refs[:count], refs[count : 2 * count]
    pre_ref, out_ref = refs[2 * count :]
    g = g_ref[...]
    total = base_ref[...] if base_ref is not None else None
    width = w_in[0].shape[1]
    chunk = min(width, 1024)
    blocks = [(i, c) for i in range(count) for c in range(0, width, chunk)]

    def into(i, c):
        return dot(g, w_out[i][c : c + chunk, :], ((1,), (1,)))

    ahead = into(*blocks[0])
    for n, (i, c) in enumerate(blocks):
        back = ahead
        if n + 1 < len(blocks):
            ahead = into(*blocks[n + 1])
        place = slice(i * width + c, i * width + c + chunk)
        pre = (back * slope_ref[:, place].astype(F32)).astype(BF16)
        pre_ref[:, place] = pre
        term = dot(pre, w_in[i][:, c : c + chunk], ((1,), (1,)))
        total = term if total is None else total + term
    out_ref[...] = total.astype(out_ref.dtype)


def expert_backward(g, slope, w_in, w_out, base=None):
    rows, width = g.shape
    count = len(w_in)
    hidden = slope.shape[1]
    tile = rows // 2

    def row(n):
        return pl.BlockSpec((tile, n), lambda i: (i, 0))

    specs = [row(width), row(hidden)]
    args = [g, slope]
    kernel = functools.partial(expert_backward_kernel, count)
    if base is not None:
        specs.append(row(width))
        args.append(base)
    else:
        kernel = without_base(kernel, 2)
    specs += [pl.BlockSpec(w.shape, lambda i: (0, 0), pipeline_mode=pl.Buffered(1)) for w in (*w_in, *w_out)]
    return pl.pallas_call(
        kernel,
        grid=(rows // tile,),
        in_specs=specs,
        out_specs=[row(hidden), row(width)],
        out_shape=[
            jax.ShapeDtypeStruct((rows, hidden), BF16),
            jax.ShapeDtypeStruct((rows, width), BF16 if base is None else F32),
        ],
        compiler_params=pltpu.CompilerParams(vmem_limit_bytes=48 << 20),
        cost_estimate=pl.CostEstimate(
            flops=4 * rows * width * hidden,
            bytes_accessed=4 * width * hidden + 4 * rows * hidden + 6 * rows * width,
            transcendentals=0,
        ),
    )(*args, *w_in, *w_out)


def outer_kernel(count, *refs):
    lefts, rights, out_ref = refs[:count], refs[count : 2 * count], refs[-1]
    total = None
    for a, b in zip(lefts, rights):
        term = dot(a[...], b[...], ((0,), (0,)))
        total = term if total is None else total + term
    out_ref[...] = total.astype(out_ref.dtype)


def outer(lefts, rights, left_block, right_block, left_width, right_width):
    rows = lefts[0].shape[0]
    count = len(lefts)
    tile = min(256, left_width)
    steps = left_width // tile
    return pl.pallas_call(
        functools.partial(outer_kernel, count),
        grid=(steps,),
        in_specs=[pl.BlockSpec((rows, tile), lambda i: (0, left_block * steps + i))] * count
        + [pl.BlockSpec((rows, right_width), lambda i: (0, right_block))] * count,
        out_specs=pl.BlockSpec((tile, right_width), lambda i: (i, 0)),
        out_shape=jax.ShapeDtypeStruct((left_width, right_width), BF16),
        compiler_params=pltpu.CompilerParams(vmem_limit_bytes=48 << 20),
        cost_estimate=pl.CostEstimate(
            flops=2 * count * rows * left_width * right_width,
            bytes_accessed=2 * (count * rows * (left_width + right_width) + left_width * right_width),
            transcendentals=0,
        ),
    )(*lefts, *rights)


class Grid:
    def __init__(self, shards, experts):
        self.size = shards
        self.experts = experts
        self.depth = experts // CORES

    def over_core(self, value):
        return lax.ppermute(value, "dp", [(d, d ^ 1) for d in range(self.experts)])

    def over_tensor(self, value, other):
        return lax.ppermute(value, "tensor", [(t, t ^ other) for t in range(self.size)])

    def sum_all(self, value):
        step = 1
        while step < self.size:
            value = value + self.over_tensor(value, step)
            step *= 2
        step = 1
        while step < self.experts:
            pairs = [(d, d ^ step) for d in range(self.experts)]
            value = value + lax.ppermute(value, "dp", pairs)
            step *= 2
        return value

    def exchange_depth(self, value):
        groups = [[CORES * z + c for z in range(self.depth)] for c in range(CORES)]
        return lax.all_to_all(
            value, "dp", split_axis=0, concat_axis=0, axis_index_groups=groups, tiled=True
        )


def owner_pairs(grid, back=False):
    pairs = []
    for z in range(grid.depth):
        for core in range(CORES):
            for y in range(2):
                for x in range(2):
                    here = (CORES * z + core) * 4 + 2 * y + x
                    there = (CORES * z + x) * 4 + 2 * y + core
                    pairs.append((there, here) if back else (here, there))
    return pairs


def fetch_hidden(grid, weight):
    if grid.size == 4:
        near = lax.ppermute(weight, ("dp", "tensor"), owner_pairs(grid))
        return [near, grid.over_tensor(near, 2)]
    core = lax.axis_index("dp") % CORES
    every = lax.all_gather(weight, "tensor", axis=0, tiled=False)
    chosen = jnp.where(lax.axis_index("tensor") % 2 == core, every, grid.over_core(every))
    return [jnp.where(core == 0, chosen[t], chosen[t + 1]) for t in range(0, grid.size, 2)]


def return_hidden(grid, pieces):
    if grid.size == 4:
        total = pieces[0].astype(F32) + grid.over_tensor(pieces[1], 2).astype(F32)
        return lax.ppermute(total.astype(BF16), ("dp", "tensor"), owner_pairs(grid, True)).astype(F32)
    core = lax.axis_index("dp") % CORES
    me = lax.axis_index("tensor")
    zero = jnp.zeros_like(pieces[0])
    wide = []
    for parity in range(2):
        row = []
        for piece in pieces:
            row += [jnp.where((me % 2 == parity) & (core == c), piece, zero) for c in range(CORES)]
        wide.append(jnp.stack(row))
    mine = lax.psum_scatter(jnp.stack(wide), "tensor", scatter_dimension=1, tiled=False)
    other = grid.over_core(jnp.where(core == 0, mine[1], mine[0]))
    return jnp.where(core == 0, mine[0], mine[1]).astype(F32) + other.astype(F32)


def gather_pieces(grid, value, balanced):
    if grid.size != 4:
        every = lax.all_gather(value, "tensor", axis=0, tiled=True)
        return [every], [jnp.int32(0)], [0]
    me = lax.axis_index("tensor")
    if not balanced:
        from_y = grid.over_tensor(value, 2)
        from_x = grid.over_tensor(value, 1)
        from_xy = grid.over_tensor(from_y, 1)
        return [value, from_x, from_y, from_xy], [jnp.bitwise_xor(me, o) for o in range(4)], [0] * 4
    half = value.shape[0] // 2
    first, second = value[:half], value[half:]
    first_x = grid.over_tensor(first, 1)
    second_y = grid.over_tensor(second, 2)
    first_y = grid.over_tensor(first, 2)
    second_x = grid.over_tensor(second, 1)
    first_xy = grid.over_tensor(first_x, 2)
    second_xy = grid.over_tensor(second_y, 1)
    pieces = [value, first_x, second_x, first_y, second_y, first_xy, second_xy]
    devices = [jnp.bitwise_xor(me, o) for o in (0, 1, 1, 2, 2, 3, 3)]
    return pieces, devices, [0, 0, half, 0, half, 0, half]


def gather_rows(grid, value, balanced=True):
    pieces, devices, starts = gather_pieces(grid, value, balanced)
    if len(pieces) == 1:
        return pieces[0]
    rows, width = value.shape
    out = jnp.zeros((grid.size * rows, width), value.dtype)
    for piece, device, start in zip(pieces, devices, starts):
        out = lax.dynamic_update_slice(out, piece, (device * rows + start, 0))
    return out


def scatter_rows(grid, term):
    size, rows, width = term.shape
    if size != 4:
        return lax.psum_scatter(term.astype(BF16), "tensor", scatter_dimension=0, tiled=False).astype(F32)
    me = lax.axis_index("tensor")
    half = width // 2

    def pick(other, low):
        place = jnp.bitwise_xor(me, other)
        return lax.dynamic_slice(term, (place, 0, low), (1, rows, half))[0]

    totals = []
    for low, near, far in ((0, 1, 2), (half, 2, 1)):
        got_far = grid.over_tensor(pick(3, low).astype(BF16), near)
        got_own = grid.over_tensor(pick(near, low).astype(BF16), near)
        onward = pick(far, low).astype(F32) + got_far.astype(F32)
        got = grid.over_tensor(onward.astype(BF16), far)
        totals.append(pick(0, low).astype(F32) + got_own.astype(F32) + got.astype(F32))
    return jnp.concatenate(totals, axis=1)


def body(
    tokens,
    lengths,
    routes,
    fill_order,
    norm_gain,
    norm_bias,
    qkv_weight,
    out_weight,
    centroids,
    expert_in,
    expert_out,
    cotangent,
):
    tok_count, model_width = tokens.shape
    seq_count = lengths.shape[0]
    seq_len = tok_count // seq_count
    heads_here = qkv_weight.shape[1]
    head_size = out_weight.shape[1]
    experts = lax.axis_size("dp")
    shards = lax.axis_size("tensor")
    grid = Grid(shards, experts)
    me = lax.axis_index("tensor")
    parity, part = me % 2, me // 2
    core = lax.axis_index("dp") % CORES
    depth = experts // CORES
    row_parts = shards // 2
    capacity = (9 * tok_count + 8 * experts - 1) // (8 * experts)
    share = 16 * -(-capacity // (16 * row_parts))
    padded = share * row_parts
    own_rows = depth * share
    tok_rows = tok_count // shards

    win, wout = [], []
    for k in range(2):
        win.append(fetch_hidden(grid, expert_in[0, k]))
        wout.append(fetch_hidden(grid, expert_out[0, k]))
    out_flat = out_weight.reshape(heads_here * head_size, model_width)
    out_all = gather_rows(grid, out_flat, False)
    centroid = jnp.where(parity == core, centroids[0], grid.over_core(centroids[0]))

    slots = token_slots(
        routes, fill_order, lengths, seq_len, capacity, padded, experts * padded
    )
    slot = slots.reshape(tok_count, 1)
    rank = slot % padded
    slot_device = (rank // share) * 2 + (slot // padded) % 2
    slot_place = (slot_device * depth + slot // (2 * padded)) * share + rank % share
    place = jnp.where(slot < experts * padded, slot_place, -1)
    own_first = (parity * padded + part * share).astype(jnp.int32).reshape(1)

    def to_experts(rows):
        picked = pick_rows(rows, slots, own_first, depth, share, CORES, padded)
        return grid.exchange_depth(picked.reshape(depth, share, model_width)).reshape(own_rows, model_width)

    def from_experts(rows, balanced):
        moved = grid.exchange_depth(rows.reshape(depth, share, model_width))
        pieces, devices, starts = gather_pieces(grid, moved.reshape(own_rows, model_width), balanced)
        first = [device * own_rows + start for device, start in zip(devices, starts)]
        return pieces, jnp.stack(first).astype(jnp.int32)

    grad_ret = to_experts(cotangent).astype(F32)
    heads = heads_here + heads_here % 2
    fused = qkv_weight.reshape(model_width, heads_here, 3, head_size)
    fused = jnp.swapaxes(fused, 1, 2)
    fused = jnp.pad(fused, ((0, 0), (0, 0), (0, heads - heads_here), (0, 0)))
    fused = fused.reshape(model_width, 3 * heads * head_size)
    inner = heads_here * head_size
    ln_in, projected = norm_project(tokens, norm_gain, norm_bias, fused)
    attended, log_total = attend(projected, lengths, seq_count, heads, head_size)
    if shards == 4:
        pieces, devices, unused = gather_pieces(grid, attended, False)
        first = jnp.stack(devices).astype(jnp.int32)
    else:
        every = lax.all_gather(attended[:, :inner], "tensor", axis=1, tiled=True)
        pieces, first = [every], jnp.zeros((1,), jnp.int32)
    sent = out_project(pieces, first, out_all, tokens)

    expert_rows = to_experts(sent)
    gate = jax.nn.sigmoid(jnp.dot(expert_rows, centroid, preferred_element_type=F32))[:, None]
    current = expert_rows.astype(F32)
    saved = []
    for k in range(2):
        here = current.astype(BF16)
        there = grid.over_core(here)
        act, slope, total = expert_forward(here, win[k], wout[k], current)
        act_there, slope_there, part = expert_forward(there, win[k], wout[k])
        current = total + grid.over_core(part).astype(F32)
        saved.append(([here, there], [act, act_there], [slope, slope_there]))
    pieces, first = from_experts((gate * current).astype(BF16), False)
    output = combine(pieces, first, place, sent)[0]

    grad_gate = jnp.sum(grad_ret * current, axis=1, keepdims=True)
    grad_logit = grad_gate * gate * (1.0 - gate)
    grad_current = gate * grad_ret
    branches = [None, None]
    for k in (1, 0):
        slopes = saved[k][2]
        here = grad_current.astype(BF16)
        there = grid.over_core(here)
        grad_pre, total = expert_backward(here, slopes[0], win[k], wout[k], grad_current)
        grad_pre_there, part = expert_backward(there, slopes[1], win[k], wout[k])
        grad_current = total + grid.over_core(part).astype(F32)
        branches[k] = ([here, there], [grad_pre, grad_pre_there])
    grad_rows = (grad_current + grad_logit * centroid.astype(F32)[None, :]).astype(BF16)
    centroid_part = jnp.sum(grad_logit * expert_rows.astype(F32), axis=0, keepdims=True)
    centroid_parts = lax.psum(
        jnp.concatenate([jnp.where(parity == p, centroid_part, 0.0) for p in range(2)], axis=0), "tensor"
    )
    centroid_parts = centroid_parts + grid.over_core(centroid_parts)
    grad_centroid = lax.dynamic_slice_in_dim(centroid_parts, core, 1, 0)
    pieces, first = from_experts(grad_rows, True)
    hidden = expert_in.shape[3]
    grads_in, grads_back = [None, None], [None, None]
    for k in (1, 0):
        rows_in, acts, unused = saved[k]
        branch, grad_pres = branches[k]
        blocks = range(len(win[k]))
        grads_back[k] = return_hidden(
            grid, [outer(acts, branch, j, 0, hidden, model_width) for j in blocks]
        )
        grads_in[k] = return_hidden(
            grid, [outer(rows_in, grad_pres, 0, j, model_width, hidden) for j in blocks]
        )
    out_padded = jnp.pad(out_flat, ((0, heads * head_size - inner), (0, 0)))
    grad_mixed, grad_attended = combine(pieces, first, place, cotangent, out_padded)
    grad_out_local = dot(attended[:, :inner], grad_mixed, ((0,), (0,))).reshape(
        heads_here, head_size, model_width
    )
    grad_projected = attend_back(
        projected, attended, grad_attended, log_total, lengths, seq_count, heads, head_size
    )
    grad_qkv_local = dot(ln_in, grad_projected, ((0,), (0,)))
    grad_ln_part = dot(grad_projected, fused, ((1,), (1,))).astype(BF16)
    grad_ln = scatter_rows(grid, grad_ln_part.reshape(shards, tok_rows, model_width))

    def own(rows):
        return lax.dynamic_slice_in_dim(rows, me * tok_rows, tok_rows, 0)

    own_tokens = own(tokens).astype(F32)
    centre = own_tokens - jnp.mean(own_tokens, axis=1, keepdims=True)
    own_scale = lax.rsqrt(jnp.mean(centre * centre, axis=1, keepdims=True) + EPSILON)
    own_normed = centre * own_scale
    grad_normed = grad_ln * norm_gain
    mean_plain = jnp.mean(grad_normed, axis=1, keepdims=True)
    mean_cross = jnp.mean(grad_normed * own_normed, axis=1, keepdims=True)
    grad_input = own(grad_mixed).astype(F32) + own_scale * (
        grad_normed - mean_plain - own_normed * mean_cross
    )
    grad_tokens = gather_rows(grid, grad_input.astype(BF16))
    norm_total = jnp.stack([jnp.sum(grad_ln * own_normed, axis=0), jnp.sum(grad_ln, axis=0)])
    norm_total = grid.sum_all(norm_total)
    norm_total = lax.dynamic_slice_in_dim(
        norm_total, me * (model_width // shards), model_width // shards, 1
    )
    grad_qkv, grad_out_weight = lax.psum(
        (grad_qkv_local.astype(BF16), grad_out_local.astype(BF16)), "dp"
    )
    grad_qkv = grad_qkv.astype(F32).reshape(model_width, 3, heads, head_size)[:, :, :heads_here]
    grad_qkv_weight = jnp.swapaxes(grad_qkv, 1, 2).reshape(model_width, heads_here, 3 * head_size)
    return (
        output,
        grad_tokens,
        norm_total[0],
        norm_total[1],
        grad_qkv_weight,
        grad_out_weight.astype(F32),
        grad_centroid,
        jnp.stack(grads_in)[None],
        jnp.stack(grads_back)[None],
    )


def solution(mesh):
    return jax.shard_map(
        body,
        mesh=mesh,
        in_specs=(
            P("dp", None),
            P("dp"),
            P("dp", None),
            P("dp", None),
            P(),
            P(),
            P(None, "tensor", None),
            P("tensor", None, None),
            P("dp", None),
            P("dp", None, None, "tensor"),
            P("dp", None, "tensor", None),
            P("dp", None),
        ),
        out_specs=(
            P("dp", None),
            P("dp", None),
            P("tensor"),
            P("tensor"),
            P(None, "tensor", None),
            P("tensor", None, None),
            P("dp", None),
            P("dp", None, None, "tensor"),
            P("dp", None, "tensor", None),
        ),
        check_vma=False,
    )
```

```python
import functools
import math

import jax
import jax.numpy as jnp
from jax import lax
from jax.experimental import pallas as pl
from jax.experimental.pallas import tpu as pltpu
from jax.sharding import PartitionSpec as P

EPSILON = 1e-05
MASKED = -1e30
F32 = jnp.float32
BF16 = jnp.bfloat16
CORES = 2


def after(value, *others):
    return lax.optimization_barrier((value, *others))[0]


def dot(a, b, contract):
    return lax.dot_general(a, b, (contract, ((), ())), preferred_element_type=F32)


def norm_project_kernel(x_ref, gain_ref, bias_ref, w_ref, ln_ref, out_ref):
    x = x_ref[...].astype(F32)
    centre = x - jnp.mean(x, axis=1, keepdims=True)
    scale = lax.rsqrt(jnp.mean(centre * centre, axis=1, keepdims=True) + EPSILON)
    ln = (centre * scale * gain_ref[...] + bias_ref[...]).astype(BF16)
    ln_ref[...] = ln
    out_ref[...] = dot(ln, w_ref[...], ((1,), (0,))).astype(BF16)


def norm_project(tokens, gain, bias, weight):
    rows, width = tokens.shape
    columns = weight.shape[1]
    tile = 512
    return pl.pallas_call(
        norm_project_kernel,
        grid=(rows // tile,),
        in_specs=[
            pl.BlockSpec((tile, width), lambda i: (i, 0)),
            pl.BlockSpec((1, width), lambda i: (0, 0)),
            pl.BlockSpec((1, width), lambda i: (0, 0)),
            pl.BlockSpec((width, columns), lambda i: (0, 0)),
        ],
        out_specs=[
            pl.BlockSpec((tile, width), lambda i: (i, 0)),
            pl.BlockSpec((tile, columns), lambda i: (i, 0)),
        ],
        out_shape=[
            jax.ShapeDtypeStruct((rows, width), BF16),
            jax.ShapeDtypeStruct((rows, columns), BF16),
        ],
        compiler_params=pltpu.CompilerParams(vmem_limit_bytes=40 << 20),
        cost_estimate=pl.CostEstimate(
            flops=2 * rows * width * columns,
            bytes_accessed=2 * (2 * rows * width + rows * columns + width * columns),
            transcendentals=rows,
        ),
    )(tokens, gain[None], bias[None], weight)


def attend_kernel(head_size, group, tile, len_ref, q_ref, k_ref, v_ref, o_ref, lse_ref):
    seq_len, lanes = q_ref.shape
    scale = head_size**-0.5
    limit = len_ref[pl.program_id(0)]
    keys = k_ref[...]
    values = v_ref[...]
    key_place = lax.broadcasted_iota(jnp.int32, (seq_len, lanes), 0)
    lane = lax.broadcasted_iota(jnp.int32, (seq_len, lanes), 1)
    causal = lax.broadcasted_iota(jnp.int32, (tile, tile), 0) <= lax.broadcasted_iota(
        jnp.int32, (tile, tile), 1
    )
    tall = lax.broadcasted_iota(jnp.int32, (lanes, tile), 0)
    lane_q = lax.broadcasted_iota(jnp.int32, (tile, lanes), 1)
    heads = []
    for a in range(group):
        mine = (lane >= a * head_size) & (lane < (a + 1) * head_size)
        spare = ((a + 1) % group) * head_size
        extra = jnp.where((lane == spare) & (key_place >= limit), MASKED, 0.0).astype(BF16)
        k_a = jnp.where(mine, keys, extra)
        v_a = jnp.where(mine, values, jnp.ones((), BF16))
        heads.append((k_a, v_a, spare))
    for i in range(seq_len // tile):
        end = (i + 1) * tile
        q = (q_ref[i * tile : end, :].astype(F32) * scale).astype(BF16)
        out = None
        for a in range(group):
            k_a, v_a, spare = heads[a]
            mine_q = (lane_q >= a * head_size) & (lane_q < (a + 1) * head_size)
            q_a = jnp.where(mine_q, q, jnp.where(lane_q == spare, 1.0, 0.0).astype(BF16))
            scores = dot(k_a[:end], q_a, ((1,), (1,)))
            last = jnp.where(causal, scores[i * tile :], MASKED)
            scores = jnp.concatenate([scores[: i * tile], last], axis=0) if i else last
            top = jnp.max(scores, axis=0, keepdims=True)
            probs = jnp.exp(scores - top).astype(BF16)
            result = dot(v_a[:end], probs, ((0,), (0,)))
            total = result[spare : spare + 1, :]
            lse_ref[0, 0, a : a + 1, i * tile : end] = top + jnp.log(total)
            result = result / total
            if out is None:
                out = result
            else:
                out = jnp.where((tall >= a * head_size) & (tall < (a + 1) * head_size), result, out)
        o_ref[i * tile : end, :] = out.T.astype(BF16)


def attend(projected, lengths, seqs, heads, head_size):
    rows = projected.shape[0]
    seq_len = rows // seqs
    group = 2
    lanes = group * head_size
    groups = heads // group
    tile = 256
    return pl.pallas_call(
        functools.partial(attend_kernel, head_size, group, tile),
        grid_spec=pltpu.PrefetchScalarGridSpec(
            num_scalar_prefetch=1,
            grid=(seqs, groups),
            in_specs=[
                pl.BlockSpec((seq_len, lanes), lambda s, g, n: (s, g)),
                pl.BlockSpec((seq_len, lanes), lambda s, g, n: (s, groups + g)),
                pl.BlockSpec((seq_len, lanes), lambda s, g, n: (s, 2 * groups + g)),
            ],
            out_specs=[
                pl.BlockSpec((seq_len, lanes), lambda s, g, n: (s, g)),
                pl.BlockSpec((1, 1, group, seq_len), lambda s, g, n: (s, g, 0, 0)),
            ],
        ),
        out_shape=[
            jax.ShapeDtypeStruct((rows, heads * head_size), BF16),
            jax.ShapeDtypeStruct((seqs, groups, group, seq_len), F32),
        ],
        compiler_params=pltpu.CompilerParams(vmem_limit_bytes=40 << 20),
        cost_estimate=pl.CostEstimate(
            flops=4 * rows * seq_len * heads * head_size,
            bytes_accessed=8 * rows * heads * head_size,
            transcendentals=rows * seq_len * heads // 2,
        ),
    )(lengths, projected, projected, projected)


def attend_back_kernel(head_size, group, tile, len_ref, q_ref, k_ref, v_ref, o_ref, do_ref, lse_ref, out_ref, dk_acc, dv_acc):
    seq_len, lanes = q_ref.shape
    scale = head_size**-0.5
    limit = len_ref[pl.program_id(0)]
    keys = k_ref[...]
    values = v_ref[...]
    zero = jnp.zeros((), BF16)

    def place(kind):
        block = kind * pl.num_programs(1) + pl.program_id(1)
        return pl.ds(pl.multiple_of(block * lanes, lanes), lanes)

    key_place = lax.broadcasted_iota(jnp.int32, (seq_len, lanes), 0)
    lane = lax.broadcasted_iota(jnp.int32, (seq_len, lanes), 1)
    causal = lax.broadcasted_iota(jnp.int32, (tile, tile), 0) <= lax.broadcasted_iota(
        jnp.int32, (tile, tile), 1
    )
    lane_q = lax.broadcasted_iota(jnp.int32, (tile, lanes), 1)
    heads = []
    for a in range(group):
        mine = (lane >= a * head_size) & (lane < (a + 1) * head_size)
        spare = ((a + 1) % group) * head_size
        extra = jnp.where((lane == spare) & (key_place >= limit), MASKED, 0.0).astype(BF16)
        k_a = jnp.where(mine, keys, extra)
        ones = jnp.where((lane == spare) | (lane == spare + 1), 1.0, 0.0).astype(BF16)
        v_a = jnp.where(mine, values, ones)
        heads.append((k_a, v_a, spare))
    steps = seq_len // tile
    for i in reversed(range(steps)):
        end = (i + 1) * tile
        q = (q_ref[i * tile : end, :].astype(F32) * scale).astype(BF16)
        do = do_ref[i * tile : end, :]
        product = do.astype(F32) * o_ref[i * tile : end, :].astype(F32)
        dq = None
        dk = None
        dv = None
        for a in range(group):
            k_a, v_a, spare = heads[a]
            mine_q = (lane_q >= a * head_size) & (lane_q < (a + 1) * head_size)
            q_m = jnp.where(mine_q, q, zero)
            q_a = jnp.where(mine_q, q, jnp.where(lane_q == spare, 1.0, 0.0).astype(BF16))
            delta = -jnp.sum(jnp.where(mine_q, product, 0.0), axis=1, keepdims=True)
            high = delta.astype(BF16)
            low = (delta - high.astype(F32)).astype(BF16)
            do_m = jnp.where(mine_q, do, zero)
            do_a = jnp.where(lane_q == spare, high, jnp.where(lane_q == spare + 1, low, do_m))
            scores = dot(k_a[:end], q_a, ((1,), (1,)))
            last = jnp.where(causal, scores[i * tile :], MASKED)
            scores = jnp.concatenate([scores[: i * tile], last], axis=0) if i else last
            probs = jnp.exp(scores - lse_ref[0, 0, a : a + 1, i * tile : end])
            grad = dot(v_a[:end], do_a, ((1,), (1,)))
            grad = (probs * grad).astype(BF16)
            term_v = dot(probs.astype(BF16), do_m, ((1,), (0,)))
            term_k = dot(grad, q_m, ((1,), (0,)))
            term_q = dot(k_a[:end], grad, ((0,), (0,)))
            dv = term_v if dv is None else dv + term_v
            dk = term_k if dk is None else dk + term_k
            if dq is None:
                dq = term_q
            else:
                tall = lax.broadcasted_iota(jnp.int32, (lanes, tile), 0)
                dq = jnp.where((tall >= a * head_size) & (tall < (a + 1) * head_size), term_q, dq)
        out_ref[i * tile : end, place(0)] = (dq.T * scale).astype(BF16)
        if i == steps - 1:
            dk_acc[...] = dk
            dv_acc[...] = dv
        else:
            dk_acc[:end, :] += dk
            dv_acc[:end, :] += dv
    out_ref[:, place(1)] = dk_acc[...].astype(BF16)
    out_ref[:, place(2)] = dv_acc[...].astype(BF16)


def attend_back(projected, attended, grad_attended, lse, lengths, seqs, heads, head_size):
    rows = projected.shape[0]
    seq_len = rows // seqs
    group = 2
    lanes = group * head_size
    groups = heads // group
    tile = 256
    spec = pl.BlockSpec((seq_len, lanes), lambda s, g, n: (s, g))
    return pl.pallas_call(
        functools.partial(attend_back_kernel, head_size, group, tile),
        grid_spec=pltpu.PrefetchScalarGridSpec(
            num_scalar_prefetch=1,
            grid=(seqs, groups),
            in_specs=[
                spec,
                pl.BlockSpec((seq_len, lanes), lambda s, g, n: (s, groups + g)),
                pl.BlockSpec((seq_len, lanes), lambda s, g, n: (s, 2 * groups + g)),
                spec,
                spec,
                pl.BlockSpec((1, 1, group, seq_len), lambda s, g, n: (s, g, 0, 0)),
            ],
            out_specs=pl.BlockSpec((seq_len, 3 * groups * lanes), lambda s, g, n: (s, 0)),
            scratch_shapes=[pltpu.VMEM((seq_len, lanes), F32), pltpu.VMEM((seq_len, lanes), F32)],
        ),
        out_shape=jax.ShapeDtypeStruct((rows, 3 * heads * head_size), BF16),
        compiler_params=pltpu.CompilerParams(vmem_limit_bytes=48 << 20),
        cost_estimate=pl.CostEstimate(
            flops=10 * rows * seq_len * heads * head_size,
            bytes_accessed=16 * rows * heads * head_size,
            transcendentals=rows * seq_len * heads // 2,
        ),
    )(lengths, projected, projected, projected, attended, grad_attended, lse)


def place_kernel(order_ref, out_ref):
    count = out_ref.shape[1]
    tile = order_ref.shape[0]
    step = pl.program_id(0)
    token = lax.broadcasted_iota(jnp.int32, (tile, count), 1)
    index = lax.broadcasted_iota(jnp.int32, (tile, 1), 0) + step * tile
    hit = jnp.sum(jnp.where(order_ref[...] == token, index, 0), axis=0, keepdims=True)

    @pl.when(step == 0)
    def _():
        out_ref[...] = hit

    @pl.when(step > 0)
    def _():
        out_ref[...] += hit


def rank_kernel(key_ref, keys_ref, out_ref):
    step = pl.program_id(0)
    keys = keys_ref[...]
    base = jnp.bitwise_and(keys, -4096)
    key = key_ref[...]
    hit = jnp.sum(jnp.where((key < keys) & (key >= base), 1, 0), axis=0, keepdims=True)

    @pl.when(step == 0)
    def _():
        out_ref[...] = hit

    @pl.when(step > 0)
    def _():
        out_ref[...] += hit


def tall_reduce(kernel, column, rows, count):
    tile = 512
    specs = [pl.BlockSpec((tile, 1), lambda i: (i, 0))]
    specs += [pl.BlockSpec((1, count), lambda i: (0, 0)) for _ in rows]
    return pl.pallas_call(
        kernel,
        grid=(count // tile,),
        in_specs=specs,
        out_specs=pl.BlockSpec((1, count), lambda i: (0, 0)),
        out_shape=jax.ShapeDtypeStruct((1, count), jnp.int32),
        cost_estimate=pl.CostEstimate(
            flops=4 * count * count, bytes_accessed=600 * count, transcendentals=0
        ),
    )(column, *rows)


def token_slots(routes, order, lengths, seq_len, capacity, padded, none):
    count = routes.shape[0]
    places = jnp.arange(count, dtype=jnp.int32)[None]
    limits = jnp.repeat(lengths, seq_len, total_repeat_length=count)[None]
    valid = places % seq_len < limits
    turn = tall_reduce(place_kernel, order.reshape(count, 1), [], count)
    route = routes.reshape(1, count)
    keys = jnp.where(valid, route * 4096 + turn, 1 << 20)
    rank = tall_reduce(rank_kernel, keys.reshape(count, 1), [keys], count)
    return jnp.where(valid & (rank < capacity), route * padded + rank, none)


def pick_kernel(share, experts_step, padded, first_ref, slots_ref, rows_ref, out_ref):
    step = pl.program_id(0)
    start = first_ref[0] + step * experts_step * padded
    count = rows_ref.shape[0]
    slot = lax.broadcasted_iota(jnp.int32, (share, count), 0) + start
    chosen = jnp.where(slots_ref[...] == slot, 1.0, 0.0).astype(BF16)
    out_ref[...] = dot(chosen, rows_ref[...], ((1,), (0,))).astype(BF16)


def pick_rows(rows, slots, first, blocks, share, step, padded):
    count, width = rows.shape
    return pl.pallas_call(
        functools.partial(pick_kernel, share, step, padded),
        grid_spec=pltpu.PrefetchScalarGridSpec(
            num_scalar_prefetch=1,
            grid=(blocks,),
            in_specs=[
                pl.BlockSpec((1, count), lambda i, n: (0, 0)),
                pl.BlockSpec((count, width), lambda i, n: (0, 0)),
            ],
            out_specs=pl.BlockSpec((share, width), lambda i, n: (i, 0)),
        ),
        out_shape=jax.ShapeDtypeStruct((blocks * share, width), BF16),
        compiler_params=pltpu.CompilerParams(vmem_limit_bytes=40 << 20),
        cost_estimate=pl.CostEstimate(
            flops=2 * blocks * share * count * width,
            bytes_accessed=2 * (count + blocks * share) * width,
            transcendentals=0,
        ),
    )(first, slots, rows)


def out_project_kernel(count, first_ref, *refs):
    piece_refs, w_ref, x_ref, out_ref, wide = refs[:count], *refs[count:]
    for i, piece in enumerate(piece_refs):
        width = piece.shape[1]
        start = pl.multiple_of(first_ref[i] * width, width)
        wide[:, pl.ds(start, width)] = piece[...]
    out_ref[...] = (x_ref[...].astype(F32) + dot(wide[...], w_ref[...], ((1,), (0,)))).astype(BF16)


def out_project(pieces, first, weight, tokens):
    rows, width = tokens.shape
    inner = weight.shape[0]
    count = len(pieces)
    tile = 512
    return pl.pallas_call(
        functools.partial(out_project_kernel, count),
        grid_spec=pltpu.PrefetchScalarGridSpec(
            num_scalar_prefetch=1,
            grid=(rows // tile,),
            in_specs=[pl.BlockSpec((tile, p.shape[1]), lambda i, n: (i, 0)) for p in pieces]
            + [
                pl.BlockSpec((inner, width), lambda i, n: (0, 0)),
                pl.BlockSpec((tile, width), lambda i, n: (i, 0)),
            ],
            out_specs=pl.BlockSpec((tile, width), lambda i, n: (i, 0)),
            scratch_shapes=[pltpu.VMEM((tile, inner), BF16)],
        ),
        out_shape=jax.ShapeDtypeStruct((rows, width), BF16),
        compiler_params=pltpu.CompilerParams(vmem_limit_bytes=40 << 20),
        cost_estimate=pl.CostEstimate(
            flops=2 * rows * width * inner,
            bytes_accessed=2 * (3 * rows * width + inner * width),
            transcendentals=0,
        ),
    )(first, *pieces, weight, tokens)


def spread(count, first_ref, place_ref, piece_refs):
    place = place_ref[...]
    total = None
    for i in range(count):
        rows = piece_refs[i].shape[0]
        index = lax.broadcasted_iota(jnp.int32, (place.shape[0], rows), 1) + first_ref[i]
        chosen = jnp.where(place == index, 1.0, 0.0).astype(BF16)
        term = dot(chosen, piece_refs[i][...], ((1,), (0,)))
        total = term if total is None else total + term
    return total


def combine_kernel(count, first_ref, place_ref, base_ref, *refs):
    total = spread(count, first_ref, place_ref, refs[:count])
    refs[count][...] = (base_ref[...].astype(F32) + total).astype(BF16)


def combine_project_kernel(count, first_ref, place_ref, base_ref, *refs):
    total = spread(count, first_ref, place_ref, refs[:count])
    w_ref, out_ref, back_ref = refs[count:]
    out = (base_ref[...].astype(F32) + total).astype(BF16)
    out_ref[...] = out
    back_ref[...] = dot(out, w_ref[...], ((1,), (1,))).astype(BF16)


def combine(pieces, first, place, base, weight=None):
    rows, width = base.shape
    count = len(pieces)
    tile = 512
    block = pl.BlockSpec((tile, width), lambda i, n: (i, 0))
    in_specs = [pl.BlockSpec((tile, 1), lambda i, n: (i, 0)), block]
    in_specs += [pl.BlockSpec(p.shape, lambda i, n: (0, 0), pipeline_mode=pl.Buffered(1)) for p in pieces]
    args = [place, base, *pieces]
    out_specs, out_shape = [block], [jax.ShapeDtypeStruct((rows, width), BF16)]
    kernel = combine_kernel
    table = sum(p.shape[0] for p in pieces)
    flops = 2 * rows * width * table
    if weight is not None:
        inner = weight.shape[0]
        in_specs.append(pl.BlockSpec((inner, width), lambda i, n: (0, 0)))
        args.append(weight)
        out_specs.append(pl.BlockSpec((tile, inner), lambda i, n: (i, 0)))
        out_shape.append(jax.ShapeDtypeStruct((rows, inner), BF16))
        kernel = combine_project_kernel
        flops += 2 * rows * width * inner
    return pl.pallas_call(
        functools.partial(kernel, count),
        grid_spec=pltpu.PrefetchScalarGridSpec(
            num_scalar_prefetch=1, grid=(rows // tile,), in_specs=in_specs, out_specs=out_specs
        ),
        out_shape=out_shape,
        compiler_params=pltpu.CompilerParams(vmem_limit_bytes=48 << 20),
        cost_estimate=pl.CostEstimate(
            flops=flops, bytes_accessed=2 * (2 * rows + table) * width, transcendentals=0
        ),
    )(first, *args)


def gelu_pair(pre):
    cdf = 0.5 + 0.5 * lax.erf(pre * (2.0**-0.5))
    density = jnp.exp(-0.5 * pre * pre) * ((2.0 * math.pi) ** -0.5)
    return (pre * cdf).astype(BF16), (cdf + pre * density).astype(BF16)


def without_base(kernel, count):
    def wrapped(*refs):
        kernel(*refs[:count], None, *refs[count:])

    return wrapped


def expert_forward_kernel(count, x_ref, base_ref, *refs):
    w_in, w_out = refs[:count], refs[count : 2 * count]
    act_ref, slope_ref, out_ref = refs[2 * count :]
    x = x_ref[...]
    total = base_ref[...] if base_ref is not None else None
    width = w_in[0].shape[1]
    chunk = min(width, 1024)
    blocks = [(i, c) for i in range(count) for c in range(0, width, chunk)]

    def into(i, c):
        return dot(x, w_in[i][:, c : c + chunk], ((1,), (0,)))

    ahead = into(*blocks[0])
    for n, (i, c) in enumerate(blocks):
        pre = ahead
        if n + 1 < len(blocks):
            ahead = into(*blocks[n + 1])
        act, slope = gelu_pair(pre)
        act_ref[:, i * width + c : i * width + c + chunk] = act
        slope_ref[:, i * width + c : i * width + c + chunk] = slope
        term = dot(act, w_out[i][c : c + chunk, :], ((1,), (0,)))
        total = term if total is None else total + term
    out_ref[...] = total.astype(out_ref.dtype)


def expert_forward(x, w_in, w_out, base=None):
    rows, width = x.shape
    count, unused, inner = w_in.shape
    hidden = count * inner
    tile = rows // 2

    def row(n):
        return pl.BlockSpec((tile, n), lambda i: (i, 0))

    specs = [row(width)]
    args = [x]
    kernel = functools.partial(expert_forward_kernel, count)
    if base is not None:
        specs.append(row(width))
        args.append(base)
    else:
        kernel = without_base(kernel, 1)
    specs += [
        pl.BlockSpec(
            (None, *w.shape[1:]), functools.partial(lambda j, i: (j, 0, 0), j), pipeline_mode=pl.Buffered(1)
        )
        for w in (w_in, w_out)
        for j in range(count)
    ]
    return pl.pallas_call(
        kernel,
        grid=(rows // tile,),
        in_specs=specs,
        out_specs=[row(hidden), row(hidden), row(width)],
        out_shape=[
            jax.ShapeDtypeStruct((rows, hidden), BF16),
            jax.ShapeDtypeStruct((rows, hidden), BF16),
            jax.ShapeDtypeStruct((rows, width), BF16 if base is None else F32),
        ],
        compiler_params=pltpu.CompilerParams(vmem_limit_bytes=48 << 20),
        cost_estimate=pl.CostEstimate(
            flops=4 * rows * width * hidden,
            bytes_accessed=4 * width * hidden + 4 * rows * hidden + 6 * rows * width,
            transcendentals=2 * rows * hidden,
        ),
    )(*args, *[w_in] * count, *[w_out] * count)


def expert_backward_kernel(count, g_ref, slope_ref, base_ref, *refs):
    w_in, w_out = refs[:count], refs[count : 2 * count]
    pre_ref, out_ref = refs[2 * count :]
    g = g_ref[...]
    total = base_ref[...] if base_ref is not None else None
    width = w_in[0].shape[1]
    chunk = min(width, 1024)
    blocks = [(i, c) for i in range(count) for c in range(0, width, chunk)]

    def into(i, c):
        return dot(g, w_out[i][c : c + chunk, :], ((1,), (1,)))

    ahead = into(*blocks[0])
    for n, (i, c) in enumerate(blocks):
        back = ahead
        if n + 1 < len(blocks):
            ahead = into(*blocks[n + 1])
        place = slice(i * width + c, i * width + c + chunk)
        pre = (back * slope_ref[:, place].astype(F32)).astype(BF16)
        pre_ref[:, place] = pre
        term = dot(pre, w_in[i][:, c : c + chunk], ((1,), (1,)))
        total = term if total is None else total + term
    out_ref[...] = total.astype(out_ref.dtype)


def expert_backward(g, slope, w_in, w_out, base=None):
    rows, width = g.shape
    count, unused, inner = w_in.shape
    hidden = slope.shape[1]
    tile = rows // 2

    def row(n):
        return pl.BlockSpec((tile, n), lambda i: (i, 0))

    specs = [row(width), row(hidden)]
    args = [g, slope]
    kernel = functools.partial(expert_backward_kernel, count)
    if base is not None:
        specs.append(row(width))
        args.append(base)
    else:
        kernel = without_base(kernel, 2)
    specs += [
        pl.BlockSpec(
            (None, *w.shape[1:]), functools.partial(lambda j, i: (j, 0, 0), j), pipeline_mode=pl.Buffered(1)
        )
        for w in (w_in, w_out)
        for j in range(count)
    ]
    return pl.pallas_call(
        kernel,
        grid=(rows // tile,),
        in_specs=specs,
        out_specs=[row(hidden), row(width)],
        out_shape=[
            jax.ShapeDtypeStruct((rows, hidden), BF16),
            jax.ShapeDtypeStruct((rows, width), BF16 if base is None else F32),
        ],
        compiler_params=pltpu.CompilerParams(vmem_limit_bytes=48 << 20),
        cost_estimate=pl.CostEstimate(
            flops=4 * rows * width * hidden,
            bytes_accessed=4 * width * hidden + 4 * rows * hidden + 6 * rows * width,
            transcendentals=0,
        ),
    )(*args, *[w_in] * count, *[w_out] * count)


def outer_kernel(count, *refs):
    lefts, rights, out_ref = refs[:count], refs[count : 2 * count], refs[-1]
    total = None
    for a, b in zip(lefts, rights):
        term = dot(a[...], b[...], ((0,), (0,)))
        total = term if total is None else total + term
    out_ref[...] = total.astype(out_ref.dtype)


def outer(lefts, rights, blocks):
    rows = lefts[0].shape[0]
    count = len(lefts)
    left_blocks = blocks if lefts[0].shape[1] > rights[0].shape[1] else 1
    right_blocks = blocks // left_blocks
    left_width = lefts[0].shape[1] // left_blocks
    right_width = rights[0].shape[1] // right_blocks
    tile = min(256, left_width)
    steps = left_width // tile
    if left_blocks > 1:
        left_spec = pl.BlockSpec((rows, tile), lambda j, i: (0, j * steps + i))
        right_spec = pl.BlockSpec((rows, right_width), lambda j, i: (0, 0))
    else:
        left_spec = pl.BlockSpec((rows, tile), lambda j, i: (0, i))
        right_spec = pl.BlockSpec((rows, right_width), lambda j, i: (0, j))
    return pl.pallas_call(
        functools.partial(outer_kernel, count),
        grid=(blocks, steps),
        in_specs=[left_spec] * count + [right_spec] * count,
        out_specs=pl.BlockSpec((None, tile, right_width), lambda j, i: (j, i, 0)),
        out_shape=jax.ShapeDtypeStruct((blocks, left_width, right_width), BF16),
        compiler_params=pltpu.CompilerParams(vmem_limit_bytes=48 << 20),
        cost_estimate=pl.CostEstimate(
            flops=2 * count * blocks * rows * left_width * right_width,
            bytes_accessed=2 * blocks * (count * rows * (left_width + right_width) + left_width * right_width),
            transcendentals=0,
        ),
    )(*lefts, *rights)


class Grid:
    def __init__(self, shards, experts):
        self.size = shards
        self.experts = experts
        self.depth = experts // CORES

    def over_core(self, value):
        return lax.ppermute(value, "dp", [(d, d ^ 1) for d in range(self.experts)])

    def over_tensor(self, value, other):
        return lax.ppermute(value, "tensor", [(t, t ^ other) for t in range(self.size)])

    def sum_tensor(self, value):
        step = 1
        while step < self.size:
            value = value + self.over_tensor(value, step)
            step *= 2
        return value

    def sum_all(self, value):
        value = self.sum_tensor(value)
        step = 1
        while step < self.experts:
            pairs = [(d, d ^ step) for d in range(self.experts)]
            value = value + lax.ppermute(value, "dp", pairs)
            step *= 2
        return value

    def exchange_depth(self, value):
        groups = [[CORES * z + c for z in range(self.depth)] for c in range(CORES)]
        return lax.all_to_all(
            value, "dp", split_axis=0, concat_axis=0, axis_index_groups=groups, tiled=True
        )


ROWS_OF_CHIPS = [[0, 2], [1, 3]]


def owner_pairs(grid, back=False):
    pairs = []
    for z in range(grid.depth):
        for core in range(CORES):
            for y in range(2):
                for x in range(2):
                    here = (CORES * z + core) * 4 + 2 * y + x
                    there = (CORES * z + 1 - x) * 4 + 2 * y + core
                    pairs.append((there, here) if back else (here, there))
    return pairs


def fetch_near(grid, weight):
    return lax.ppermute(weight, ("dp", "tensor"), owner_pairs(grid)) if grid.size == 4 else weight


def fetch_hidden(grid, weight):
    if grid.size == 4:
        return lax.all_gather(weight, "tensor", axis=0, axis_index_groups=ROWS_OF_CHIPS, tiled=False)
    core = lax.axis_index("dp") % CORES
    every = lax.all_gather(weight, "tensor", axis=0, tiled=False)
    chosen = jnp.where(lax.axis_index("tensor") % 2 == core, every, grid.over_core(every))
    chosen = chosen.reshape(grid.size // 2, 2, *weight.shape)
    return jnp.where(core == 0, chosen[:, 0], chosen[:, 1])


def sum_hidden(grid, pieces):
    if grid.size != 4:
        return pieces
    return lax.psum_scatter(
        pieces, "tensor", scatter_dimension=0, axis_index_groups=ROWS_OF_CHIPS, tiled=False
    )


def return_hidden(grid, pieces):
    if grid.size == 4:
        return lax.ppermute(pieces, ("dp", "tensor"), owner_pairs(grid, True))
    core = lax.axis_index("dp") % CORES
    me = lax.axis_index("tensor")
    zero = jnp.zeros_like(pieces)
    row = jnp.stack([jnp.where(core == c, pieces, zero) for c in range(CORES)], axis=1)
    row = row.reshape(grid.size, *pieces.shape[1:])
    wide = jnp.stack([jnp.where(me % 2 == parity, row, jnp.zeros_like(row)) for parity in range(2)])
    mine = lax.psum_scatter(wide, "tensor", scatter_dimension=1, tiled=False)
    other = grid.over_core(jnp.where(core == 0, mine[1], mine[0]))
    total = jnp.where(core == 0, mine[0], mine[1]).astype(F32) + other.astype(F32)
    return total.astype(BF16)


class Gather:
    def __init__(self, grid, value):
        self.grid = grid
        if grid.size != 4:
            self.pieces = [lax.all_gather(value, "tensor", axis=0, tiled=True)]
            self.devices = [jnp.int32(0)]
            return
        me = lax.axis_index("tensor")
        self.pieces = [value, grid.over_tensor(value, 1), grid.over_tensor(value, 2)]
        self.devices = [jnp.bitwise_xor(me, other) for other in range(4)]

    def ready(self):
        return self.pieces[1:3]

    def joined(self):
        if self.grid.size != 4:
            return self.pieces[0]
        rows, width = self.pieces[0].shape
        out = jnp.zeros((4 * rows, width), self.pieces[0].dtype)
        for piece, device in zip(self.pieces, self.devices):
            out = lax.dynamic_update_slice(out, piece, (device * rows, 0))
        return out

    def finish(self, *others, over=1):
        if self.grid.size == 4:
            self.pieces.append(self.grid.over_tensor(after(self.pieces[3 - over], *others), over))
        return self.pieces


def gather_rows(grid, value):
    if grid.size != 4:
        return lax.all_gather(value, "tensor", axis=0, tiled=True)
    rows, width = value.shape
    half = rows // 2
    first, second = value[:half], value[half:]
    first_x = grid.over_tensor(first, 1)
    second_y = grid.over_tensor(second, 2)
    first_y = grid.over_tensor(first, 2)
    second_x = grid.over_tensor(second, 1)
    first_xy = grid.over_tensor(first_x, 2)
    second_xy = grid.over_tensor(second_y, 1)
    me = lax.axis_index("tensor")
    out = jnp.zeros((4 * rows, width), value.dtype)
    out = lax.dynamic_update_slice(out, value, (me * rows, 0))
    for other, top, bottom in ((1, first_x, second_x), (2, first_y, second_y), (3, first_xy, second_xy)):
        place = jnp.bitwise_xor(me, other) * rows
        out = lax.dynamic_update_slice(out, top, (place, 0))
        out = lax.dynamic_update_slice(out, bottom, (place + half, 0))
    return out


def scatter_rows(grid, term):
    size, rows, width = term.shape
    if size != 4:
        total = lax.psum_scatter(term.astype(BF16), "tensor", scatter_dimension=0, tiled=False)
        return total.astype(F32), []
    me = lax.axis_index("tensor")
    half = width // 2

    def pick(other, low):
        place = jnp.bitwise_xor(me, other)
        return lax.dynamic_slice(term, (place, 0, low), (1, rows, half))[0]

    totals, arrived = [], []
    for low, near, far in ((0, 1, 2), (half, 2, 1)):
        got_far = grid.over_tensor(pick(3, low).astype(BF16), near)
        got_own = grid.over_tensor(pick(near, low).astype(BF16), near)
        onward = pick(far, low).astype(F32) + got_far.astype(F32)
        got = grid.over_tensor(onward.astype(BF16), far)
        arrived.append(got)
        totals.append(pick(0, low).astype(F32) + got_own.astype(F32) + got.astype(F32))
    return jnp.concatenate(totals, axis=1), arrived


def body(
    tokens,
    lengths,
    routes,
    fill_order,
    norm_gain,
    norm_bias,
    qkv_weight,
    out_weight,
    centroids,
    expert_in,
    expert_out,
    cotangent,
):
    tok_count, model_width = tokens.shape
    seq_count = lengths.shape[0]
    seq_len = tok_count // seq_count
    heads_here = qkv_weight.shape[1]
    head_size = out_weight.shape[1]
    experts = lax.axis_size("dp")
    shards = lax.axis_size("tensor")
    grid = Grid(shards, experts)
    me = lax.axis_index("tensor")
    parity, part = me % 2, me // 2
    core = lax.axis_index("dp") % CORES
    depth = experts // CORES
    row_parts = shards // 2
    capacity = (9 * tok_count + 8 * experts - 1) // (8 * experts)
    share = 16 * -(-capacity // (16 * row_parts))
    padded = share * row_parts
    own_rows = depth * share
    tok_rows = tok_count // shards

    near = [fetch_near(grid, w[0, k]) for k in range(2) for w in (expert_in, expert_out)]
    out_flat = out_weight.reshape(heads_here * head_size, model_width)
    out_gather = Gather(grid, out_flat)
    out_gather.finish(over=2)
    out_all = out_gather.joined()
    centroid = jnp.where(parity == core, centroids[0], grid.over_core(centroids[0]))

    slots = token_slots(
        routes, fill_order, lengths, seq_len, capacity, padded, experts * padded
    )
    slot = slots.reshape(tok_count, 1)
    rank = slot % padded
    slot_device = (rank // share) * 2 + (slot // padded) % 2
    slot_place = (slot_device * depth + slot // (2 * padded)) * share + rank % share
    place = jnp.where(slot < experts * padded, slot_place, -1)
    own_first = (parity * padded + part * share).astype(jnp.int32).reshape(1)

    def to_experts(rows):
        picked = pick_rows(rows, slots, own_first, depth, share, CORES, padded)
        return grid.exchange_depth(picked.reshape(depth, share, model_width)).reshape(own_rows, model_width)

    def leave_experts(rows):
        return grid.exchange_depth(rows.reshape(depth, share, model_width))

    def row_starts(gathered):
        return jnp.stack([device * own_rows for device in gathered.devices]).astype(jnp.int32)

    grad_ret = to_experts(cotangent).astype(F32)
    heads = heads_here + heads_here % 2
    fused = qkv_weight.reshape(model_width, heads_here, 3, head_size)
    fused = jnp.swapaxes(fused, 1, 2)
    fused = jnp.pad(fused, ((0, 0), (0, 0), (0, heads - heads_here), (0, 0)))
    fused = fused.reshape(model_width, 3 * heads * head_size)
    inner = heads_here * head_size
    ln_in, projected = norm_project(tokens, norm_gain, norm_bias, fused)
    near[0] = after(near[0], projected)
    attended, log_total = attend(projected, lengths, seq_count, heads, head_size)
    near[1:] = [after(piece, attended) for piece in near[1:]]
    win, wout = [fetch_hidden(grid, w) for w in near[::2]], [fetch_hidden(grid, w) for w in near[1::2]]
    if shards == 4:
        gathered = Gather(grid, attended)
        pieces = gathered.finish()
        first = jnp.stack(gathered.devices).astype(jnp.int32)
    else:
        every = lax.all_gather(attended[:, :inner], "tensor", axis=1, tiled=True)
        pieces, first = [every], jnp.zeros((1,), jnp.int32)
    sent = out_project(pieces, first, out_all, tokens)

    expert_rows = to_experts(sent)
    gate = jax.nn.sigmoid(jnp.dot(expert_rows, centroid, preferred_element_type=F32))[:, None]
    current = expert_rows.astype(F32)
    saved = []
    for k in range(2):
        here = current.astype(BF16)
        there = grid.over_core(here)
        act, slope, total = expert_forward(here, win[k], wout[k], current)
        act_there, slope_there, part = expert_forward(there, win[k], wout[k])
        current = total + grid.over_core(part).astype(F32)
        saved.append(([here, there], [act, act_there], [slope, slope_there]))
    returned = leave_experts((gate * current).astype(BF16))

    grad_gate = jnp.sum(grad_ret * current, axis=1, keepdims=True)
    grad_logit = grad_gate * gate * (1.0 - gate)
    grad_current = gate * grad_ret
    branches = [None, None]
    for k in (1, 0):
        slopes = saved[k][2]
        here = grad_current.astype(BF16)
        there = grid.over_core(here)
        grad_pre, total = expert_backward(here, slopes[0], win[k], wout[k], grad_current)
        grad_pre_there, part = expert_backward(there, slopes[1], win[k], wout[k])
        grad_current = total + grid.over_core(part).astype(F32)
        branches[k] = ([here, there], [grad_pre, grad_pre_there])
    grad_rows = (grad_current + grad_logit * centroid.astype(F32)[None, :]).astype(BF16)
    centroid_part = jnp.sum(grad_logit * expert_rows.astype(F32), axis=0, keepdims=True)
    centroid_parts = jnp.concatenate(
        [jnp.where(parity == p, centroid_part, 0.0) for p in range(2)], axis=0
    )

    moved = leave_experts(grad_rows)
    outers, sums = [], []
    for k in (1, 0):
        rows_in, acts, unused = saved[k]
        branch, grad_pres = branches[k]
        blocks = win[k].shape[0]
        outers += [outer(rows_in, grad_pres, blocks), outer(acts, branch, blocks)]
    sums_in2, sums_back2, sums_in1, sums_back1 = [sum_hidden(grid, pieces) for pieces in outers]
    moved = after(moved, *outers)
    grad_gather = Gather(grid, moved.reshape(own_rows, model_width))
    pieces = grad_gather.finish()
    first = row_starts(grad_gather)
    out_padded = jnp.pad(out_flat, ((0, heads * head_size - inner), (0, 0)))
    grad_mixed, grad_attended = combine(pieces, first, place, cotangent, out_padded)
    out_gather = Gather(grid, after(returned, *pieces[1:]).reshape(own_rows, model_width))
    out_first = row_starts(out_gather)
    back_in2 = return_hidden(grid, after(sums_in2, *pieces[1:]))
    back_out2 = return_hidden(grid, after(sums_back2, *pieces[1:]))
    grad_projected = attend_back(
        projected, attended, grad_attended, log_total, lengths, seq_count, heads, head_size
    )
    grad_projected = after(grad_projected, back_in2, back_out2, *out_gather.ready())
    out_pieces = out_gather.finish()
    grad_out_local = dot(attended[:, :inner], grad_mixed, ((0,), (0,))).reshape(
        heads_here, head_size, model_width
    )
    grad_qkv_local = dot(ln_in, grad_projected, ((0,), (0,)))
    grad_ln_part = dot(grad_projected, fused, ((1,), (1,))).astype(BF16)
    grad_ln, scattered = scatter_rows(grid, grad_ln_part.reshape(shards, tok_rows, model_width))
    scattered = scattered + [grad_projected]
    back_in1 = return_hidden(grid, after(sums_in1, *scattered))
    back_out1 = return_hidden(grid, after(sums_back1, *scattered))
    centroid_parts = grid.sum_tensor(after(centroid_parts, *scattered))
    centroid_parts = centroid_parts + grid.over_core(centroid_parts)
    grad_centroid = lax.dynamic_slice_in_dim(centroid_parts, core, 1, 0)

    def own(rows):
        return lax.dynamic_slice_in_dim(rows, me * tok_rows, tok_rows, 0)

    own_tokens = own(tokens).astype(F32)
    centre = own_tokens - jnp.mean(own_tokens, axis=1, keepdims=True)
    own_scale = lax.rsqrt(jnp.mean(centre * centre, axis=1, keepdims=True) + EPSILON)
    own_normed = centre * own_scale
    grad_normed = grad_ln * norm_gain
    mean_plain = jnp.mean(grad_normed, axis=1, keepdims=True)
    mean_cross = jnp.mean(grad_normed * own_normed, axis=1, keepdims=True)
    grad_input = own(grad_mixed).astype(F32) + own_scale * (
        grad_normed - mean_plain - own_normed * mean_cross
    )
    grad_tokens = gather_rows(grid, grad_input.astype(BF16))
    output = combine(out_pieces, out_first, place, after(sent, *scattered))[0]
    norm_total = jnp.stack([jnp.sum(grad_ln * own_normed, axis=0), jnp.sum(grad_ln, axis=0)])
    norm_total = grid.sum_all(norm_total)
    norm_total = lax.dynamic_slice_in_dim(
        norm_total, me * (model_width // shards), model_width // shards, 1
    )
    grad_qkv, grad_out_weight = lax.psum(
        (grad_qkv_local.astype(BF16), grad_out_local.astype(BF16)), "dp"
    )
    grad_qkv = grad_qkv.astype(F32).reshape(model_width, 3, heads, head_size)[:, :, :heads_here]
    grad_qkv_weight = jnp.swapaxes(grad_qkv, 1, 2).reshape(model_width, heads_here, 3 * head_size)
    return (
        output,
        grad_tokens,
        norm_total[0],
        norm_total[1],
        grad_qkv_weight,
        grad_out_weight.astype(F32),
        grad_centroid,
        jnp.stack([back_in1, back_in2])[None].astype(F32),
        jnp.stack([back_out1, back_out2])[None].astype(F32),
    )


def solution(mesh):
    return jax.shard_map(
        body,
        mesh=mesh,
        in_specs=(
            P("dp", None),
            P("dp"),
            P("dp", None),
            P("dp", None),
            P(),
            P(),
            P(None, "tensor", None),
            P("tensor", None, None),
            P("dp", None),
            P("dp", None, None, "tensor"),
            P("dp", None, "tensor", None),
            P("dp", None),
        ),
        out_specs=(
            P("dp", None),
            P("dp", None),
            P("tensor"),
            P("tensor"),
            P(None, "tensor", None),
            P("tensor", None, None),
            P("dp", None),
            P("dp", None, None, "tensor"),
            P("dp", None, "tensor", None),
        ),
        check_vma=False,
    )
```

```python
import functools
import math

import jax
import jax.numpy as jnp
from jax import lax
from jax.experimental import pallas as pl
from jax.experimental.pallas import tpu as pltpu
from jax.sharding import PartitionSpec as P

EPSILON = 1e-05
MASKED = -1e30
F32 = jnp.float32
BF16 = jnp.bfloat16
CORES = 2


def after(value, *others):
    return lax.optimization_barrier((value, *others))[0]


def together(*values):
    return lax.optimization_barrier(values)


def dot(a, b, contract):
    return lax.dot_general(a, b, (contract, ((), ())), preferred_element_type=F32)


def norm_project_kernel(x_ref, gain_ref, bias_ref, w_ref, ln_ref, out_ref):
    x = x_ref[...].astype(F32)
    centre = x - jnp.mean(x, axis=1, keepdims=True)
    scale = lax.rsqrt(jnp.mean(centre * centre, axis=1, keepdims=True) + EPSILON)
    ln = (centre * scale * gain_ref[...] + bias_ref[...]).astype(BF16)
    ln_ref[...] = ln
    out_ref[...] = dot(ln, w_ref[...], ((1,), (0,))).astype(BF16)


def norm_project(tokens, gain, bias, weight):
    rows, width = tokens.shape
    columns = weight.shape[1]
    tile = 512
    return pl.pallas_call(
        norm_project_kernel,
        grid=(rows // tile,),
        in_specs=[
            pl.BlockSpec((tile, width), lambda i: (i, 0)),
            pl.BlockSpec((1, width), lambda i: (0, 0)),
            pl.BlockSpec((1, width), lambda i: (0, 0)),
            pl.BlockSpec((width, columns), lambda i: (0, 0)),
        ],
        out_specs=[
            pl.BlockSpec((tile, width), lambda i: (i, 0)),
            pl.BlockSpec((tile, columns), lambda i: (i, 0)),
        ],
        out_shape=[
            jax.ShapeDtypeStruct((rows, width), BF16),
            jax.ShapeDtypeStruct((rows, columns), BF16),
        ],
        compiler_params=pltpu.CompilerParams(vmem_limit_bytes=40 << 20),
        cost_estimate=pl.CostEstimate(
            flops=2 * rows * width * columns,
            bytes_accessed=2 * (2 * rows * width + rows * columns + width * columns),
            transcendentals=rows,
        ),
    )(tokens, gain[None], bias[None], weight)


def attend_kernel(head_size, group, tile, len_ref, q_ref, k_ref, v_ref, o_ref, lse_ref):
    seq_len, lanes = q_ref.shape
    scale = head_size**-0.5
    limit = len_ref[pl.program_id(0)]
    keys = k_ref[...]
    values = v_ref[...]
    key_place = lax.broadcasted_iota(jnp.int32, (seq_len, lanes), 0)
    lane = lax.broadcasted_iota(jnp.int32, (seq_len, lanes), 1)
    causal = lax.broadcasted_iota(jnp.int32, (tile, tile), 0) <= lax.broadcasted_iota(
        jnp.int32, (tile, tile), 1
    )
    tall = lax.broadcasted_iota(jnp.int32, (lanes, tile), 0)
    lane_q = lax.broadcasted_iota(jnp.int32, (tile, lanes), 1)
    heads = []
    for a in range(group):
        mine = (lane >= a * head_size) & (lane < (a + 1) * head_size)
        spare = ((a + 1) % group) * head_size
        extra = jnp.where((lane == spare) & (key_place >= limit), MASKED, 0.0).astype(BF16)
        k_a = jnp.where(mine, keys, extra)
        v_a = jnp.where(mine, values, jnp.ones((), BF16))
        heads.append((k_a, v_a, spare))
    for i in range(seq_len // tile):
        end = (i + 1) * tile
        q = (q_ref[i * tile : end, :].astype(F32) * scale).astype(BF16)
        out = None
        for a in range(group):
            k_a, v_a, spare = heads[a]
            mine_q = (lane_q >= a * head_size) & (lane_q < (a + 1) * head_size)
            q_a = jnp.where(mine_q, q, jnp.where(lane_q == spare, 1.0, 0.0).astype(BF16))
            scores = dot(k_a[:end], q_a, ((1,), (1,)))
            last = jnp.where(causal, scores[i * tile :], MASKED)
            scores = jnp.concatenate([scores[: i * tile], last], axis=0) if i else last
            top = jnp.max(scores, axis=0, keepdims=True)
            probs = jnp.exp(scores - top).astype(BF16)
            result = dot(v_a[:end], probs, ((0,), (0,)))
            total = result[spare : spare + 1, :]
            lse_ref[0, 0, a : a + 1, i * tile : end] = top + jnp.log(total)
            result = result / total
            if out is None:
                out = result
            else:
                out = jnp.where((tall >= a * head_size) & (tall < (a + 1) * head_size), result, out)
        o_ref[i * tile : end, :] = out.T.astype(BF16)


def attend(projected, lengths, seqs, heads, head_size):
    rows = projected.shape[0]
    seq_len = rows // seqs
    group = 2
    lanes = group * head_size
    groups = heads // group
    tile = 256
    return pl.pallas_call(
        functools.partial(attend_kernel, head_size, group, tile),
        grid_spec=pltpu.PrefetchScalarGridSpec(
            num_scalar_prefetch=1,
            grid=(seqs, groups),
            in_specs=[
                pl.BlockSpec((seq_len, lanes), lambda s, g, n: (s, g)),
                pl.BlockSpec((seq_len, lanes), lambda s, g, n: (s, groups + g)),
                pl.BlockSpec((seq_len, lanes), lambda s, g, n: (s, 2 * groups + g)),
            ],
            out_specs=[
                pl.BlockSpec((seq_len, lanes), lambda s, g, n: (s, g)),
                pl.BlockSpec((1, 1, group, seq_len), lambda s, g, n: (s, g, 0, 0)),
            ],
        ),
        out_shape=[
            jax.ShapeDtypeStruct((rows, heads * head_size), BF16),
            jax.ShapeDtypeStruct((seqs, groups, group, seq_len), F32),
        ],
        compiler_params=pltpu.CompilerParams(vmem_limit_bytes=40 << 20),
        cost_estimate=pl.CostEstimate(
            flops=4 * rows * seq_len * heads * head_size,
            bytes_accessed=8 * rows * heads * head_size,
            transcendentals=rows * seq_len * heads // 2,
        ),
    )(lengths, projected, projected, projected)


def attend_back_kernel(head_size, group, tile, len_ref, q_ref, k_ref, v_ref, o_ref, do_ref, lse_ref, out_ref, dk_acc, dv_acc):
    seq_len, lanes = q_ref.shape
    scale = head_size**-0.5
    limit = len_ref[pl.program_id(0)]
    keys = k_ref[...]
    values = v_ref[...]
    zero = jnp.zeros((), BF16)

    def place(kind):
        block = kind * pl.num_programs(1) + pl.program_id(1)
        return pl.ds(pl.multiple_of(block * lanes, lanes), lanes)

    key_place = lax.broadcasted_iota(jnp.int32, (seq_len, lanes), 0)
    lane = lax.broadcasted_iota(jnp.int32, (seq_len, lanes), 1)
    causal = lax.broadcasted_iota(jnp.int32, (tile, tile), 0) <= lax.broadcasted_iota(
        jnp.int32, (tile, tile), 1
    )
    lane_q = lax.broadcasted_iota(jnp.int32, (tile, lanes), 1)
    heads = []
    for a in range(group):
        mine = (lane >= a * head_size) & (lane < (a + 1) * head_size)
        spare = ((a + 1) % group) * head_size
        extra = jnp.where((lane == spare) & (key_place >= limit), MASKED, 0.0).astype(BF16)
        k_a = jnp.where(mine, keys, extra)
        ones = jnp.where((lane == spare) | (lane == spare + 1), 1.0, 0.0).astype(BF16)
        v_a = jnp.where(mine, values, ones)
        heads.append((k_a, v_a, spare))
    steps = seq_len // tile
    for i in reversed(range(steps)):
        end = (i + 1) * tile
        q = (q_ref[i * tile : end, :].astype(F32) * scale).astype(BF16)
        do = do_ref[i * tile : end, :]
        product = do.astype(F32) * o_ref[i * tile : end, :].astype(F32)
        dq = None
        dk = None
        dv = None
        for a in range(group):
            k_a, v_a, spare = heads[a]
            mine_q = (lane_q >= a * head_size) & (lane_q < (a + 1) * head_size)
            q_m = jnp.where(mine_q, q, zero)
            q_a = jnp.where(mine_q, q, jnp.where(lane_q == spare, 1.0, 0.0).astype(BF16))
            delta = -jnp.sum(jnp.where(mine_q, product, 0.0), axis=1, keepdims=True)
            high = delta.astype(BF16)
            low = (delta - high.astype(F32)).astype(BF16)
            do_m = jnp.where(mine_q, do, zero)
            do_a = jnp.where(lane_q == spare, high, jnp.where(lane_q == spare + 1, low, do_m))
            scores = dot(k_a[:end], q_a, ((1,), (1,)))
            last = jnp.where(causal, scores[i * tile :], MASKED)
            scores = jnp.concatenate([scores[: i * tile], last], axis=0) if i else last
            probs = jnp.exp(scores - lse_ref[0, 0, a : a + 1, i * tile : end])
            grad = dot(v_a[:end], do_a, ((1,), (1,)))
            grad = (probs * grad).astype(BF16)
            term_v = dot(probs.astype(BF16), do_m, ((1,), (0,)))
            term_k = dot(grad, q_m, ((1,), (0,)))
            term_q = dot(k_a[:end], grad, ((0,), (0,)))
            dv = term_v if dv is None else dv + term_v
            dk = term_k if dk is None else dk + term_k
            if dq is None:
                dq = term_q
            else:
                tall = lax.broadcasted_iota(jnp.int32, (lanes, tile), 0)
                dq = jnp.where((tall >= a * head_size) & (tall < (a + 1) * head_size), term_q, dq)
        out_ref[i * tile : end, place(0)] = (dq.T * scale).astype(BF16)
        if i == steps - 1:
            dk_acc[...] = dk
            dv_acc[...] = dv
        else:
            dk_acc[:end, :] += dk
            dv_acc[:end, :] += dv
    out_ref[:, place(1)] = dk_acc[...].astype(BF16)
    out_ref[:, place(2)] = dv_acc[...].astype(BF16)


def attend_back(projected, attended, grad_attended, lse, lengths, seqs, heads, head_size):
    rows = projected.shape[0]
    seq_len = rows // seqs
    group = 2
    lanes = group * head_size
    groups = heads // group
    tile = 256
    spec = pl.BlockSpec((seq_len, lanes), lambda s, g, n: (s, g))
    return pl.pallas_call(
        functools.partial(attend_back_kernel, head_size, group, tile),
        grid_spec=pltpu.PrefetchScalarGridSpec(
            num_scalar_prefetch=1,
            grid=(seqs, groups),
            in_specs=[
                spec,
                pl.BlockSpec((seq_len, lanes), lambda s, g, n: (s, groups + g)),
                pl.BlockSpec((seq_len, lanes), lambda s, g, n: (s, 2 * groups + g)),
                spec,
                spec,
                pl.BlockSpec((1, 1, group, seq_len), lambda s, g, n: (s, g, 0, 0)),
            ],
            out_specs=pl.BlockSpec((seq_len, 3 * groups * lanes), lambda s, g, n: (s, 0)),
            scratch_shapes=[pltpu.VMEM((seq_len, lanes), F32), pltpu.VMEM((seq_len, lanes), F32)],
        ),
        out_shape=jax.ShapeDtypeStruct((rows, 3 * heads * head_size), BF16),
        compiler_params=pltpu.CompilerParams(vmem_limit_bytes=48 << 20),
        cost_estimate=pl.CostEstimate(
            flops=10 * rows * seq_len * heads * head_size,
            bytes_accessed=16 * rows * heads * head_size,
            transcendentals=rows * seq_len * heads // 2,
        ),
    )(lengths, projected, projected, projected, attended, grad_attended, lse)


def place_kernel(order_ref, out_ref):
    count = out_ref.shape[1]
    tile = order_ref.shape[0]
    step = pl.program_id(0)
    token = lax.broadcasted_iota(jnp.int32, (tile, count), 1)
    index = lax.broadcasted_iota(jnp.int32, (tile, 1), 0) + step * tile
    hit = jnp.sum(jnp.where(order_ref[...] == token, index, 0), axis=0, keepdims=True)

    @pl.when(step == 0)
    def _():
        out_ref[...] = hit

    @pl.when(step > 0)
    def _():
        out_ref[...] += hit


def rank_kernel(key_ref, keys_ref, out_ref):
    step = pl.program_id(0)
    keys = keys_ref[...]
    base = jnp.bitwise_and(keys, -4096)
    key = key_ref[...]
    hit = jnp.sum(jnp.where((key < keys) & (key >= base), 1, 0), axis=0, keepdims=True)

    @pl.when(step == 0)
    def _():
        out_ref[...] = hit

    @pl.when(step > 0)
    def _():
        out_ref[...] += hit


def tall_reduce(kernel, column, rows, count):
    tile = 512
    specs = [pl.BlockSpec((tile, 1), lambda i: (i, 0))]
    specs += [pl.BlockSpec((1, count), lambda i: (0, 0)) for _ in rows]
    return pl.pallas_call(
        kernel,
        grid=(count // tile,),
        in_specs=specs,
        out_specs=pl.BlockSpec((1, count), lambda i: (0, 0)),
        out_shape=jax.ShapeDtypeStruct((1, count), jnp.int32),
        cost_estimate=pl.CostEstimate(
            flops=4 * count * count, bytes_accessed=600 * count, transcendentals=0
        ),
    )(column, *rows)


def token_slots(routes, order, lengths, seq_len, capacity, padded, none):
    count = routes.shape[0]
    places = jnp.arange(count, dtype=jnp.int32)[None]
    limits = jnp.repeat(lengths, seq_len, total_repeat_length=count)[None]
    valid = places % seq_len < limits
    turn = tall_reduce(place_kernel, order.reshape(count, 1), [], count)
    route = routes.reshape(1, count)
    keys = jnp.where(valid, route * 4096 + turn, 1 << 20)
    rank = tall_reduce(rank_kernel, keys.reshape(count, 1), [keys], count)
    return jnp.where(valid & (rank < capacity), route * padded + rank, none)


def pick_kernel(share, experts_step, padded, first_ref, slots_ref, rows_ref, out_ref):
    step = pl.program_id(0)
    start = first_ref[0] + step * experts_step * padded
    count = rows_ref.shape[0]
    slot = lax.broadcasted_iota(jnp.int32, (share, count), 0) + start
    chosen = jnp.where(slots_ref[...] == slot, 1.0, 0.0).astype(BF16)
    out_ref[...] = dot(chosen, rows_ref[...], ((1,), (0,))).astype(BF16)


def pick_rows(rows, slots, first, blocks, share, step, padded):
    count, width = rows.shape
    return pl.pallas_call(
        functools.partial(pick_kernel, share, step, padded),
        grid_spec=pltpu.PrefetchScalarGridSpec(
            num_scalar_prefetch=1,
            grid=(blocks,),
            in_specs=[
                pl.BlockSpec((1, count), lambda i, n: (0, 0)),
                pl.BlockSpec((count, width), lambda i, n: (0, 0)),
            ],
            out_specs=pl.BlockSpec((share, width), lambda i, n: (i, 0)),
        ),
        out_shape=jax.ShapeDtypeStruct((blocks * share, width), BF16),
        compiler_params=pltpu.CompilerParams(vmem_limit_bytes=40 << 20),
        cost_estimate=pl.CostEstimate(
            flops=2 * blocks * share * count * width,
            bytes_accessed=2 * (count + blocks * share) * width,
            transcendentals=0,
        ),
    )(first, slots, rows)


def out_project_kernel(count, first_ref, *refs):
    piece_refs, w_ref, x_ref, out_ref, wide = refs[:count], *refs[count:]
    for i, piece in enumerate(piece_refs):
        width = piece.shape[1]
        start = pl.multiple_of(first_ref[i] * width, width)
        wide[:, pl.ds(start, width)] = piece[...]
    out_ref[...] = (x_ref[...].astype(F32) + dot(wide[...], w_ref[...], ((1,), (0,)))).astype(BF16)


def out_project(pieces, first, weight, tokens):
    rows, width = tokens.shape
    inner = weight.shape[0]
    count = len(pieces)
    tile = 512
    return pl.pallas_call(
        functools.partial(out_project_kernel, count),
        grid_spec=pltpu.PrefetchScalarGridSpec(
            num_scalar_prefetch=1,
            grid=(rows // tile,),
            in_specs=[pl.BlockSpec((tile, p.shape[1]), lambda i, n: (i, 0)) for p in pieces]
            + [
                pl.BlockSpec((inner, width), lambda i, n: (0, 0)),
                pl.BlockSpec((tile, width), lambda i, n: (i, 0)),
            ],
            out_specs=pl.BlockSpec((tile, width), lambda i, n: (i, 0)),
            scratch_shapes=[pltpu.VMEM((tile, inner), BF16)],
        ),
        out_shape=jax.ShapeDtypeStruct((rows, width), BF16),
        compiler_params=pltpu.CompilerParams(vmem_limit_bytes=40 << 20),
        cost_estimate=pl.CostEstimate(
            flops=2 * rows * width * inner,
            bytes_accessed=2 * (3 * rows * width + inner * width),
            transcendentals=0,
        ),
    )(first, *pieces, weight, tokens)


def spread(count, first_ref, place_ref, piece_refs):
    place = place_ref[...]
    total = None
    for i in range(count):
        rows = piece_refs[i].shape[0]
        index = lax.broadcasted_iota(jnp.int32, (place.shape[0], rows), 1) + first_ref[i]
        chosen = jnp.where(place == index, 1.0, 0.0).astype(BF16)
        term = dot(chosen, piece_refs[i][...], ((1,), (0,)))
        total = term if total is None else total + term
    return total


def combine_kernel(count, first_ref, place_ref, base_ref, *refs):
    total = spread(count, first_ref, place_ref, refs[:count])
    refs[count][...] = (base_ref[...].astype(F32) + total).astype(BF16)


def combine_project_kernel(count, first_ref, place_ref, base_ref, *refs):
    total = spread(count, first_ref, place_ref, refs[:count])
    w_ref, out_ref, back_ref = refs[count:]
    out = (base_ref[...].astype(F32) + total).astype(BF16)
    out_ref[...] = out
    back_ref[...] = dot(out, w_ref[...], ((1,), (1,))).astype(BF16)


def combine(pieces, first, place, base, weight=None):
    rows, width = base.shape
    count = len(pieces)
    tile = 512
    block = pl.BlockSpec((tile, width), lambda i, n: (i, 0))
    in_specs = [pl.BlockSpec((tile, 1), lambda i, n: (i, 0)), block]
    in_specs += [pl.BlockSpec(p.shape, lambda i, n: (0, 0), pipeline_mode=pl.Buffered(1)) for p in pieces]
    args = [place, base, *pieces]
    out_specs, out_shape = [block], [jax.ShapeDtypeStruct((rows, width), BF16)]
    kernel = combine_kernel
    table = sum(p.shape[0] for p in pieces)
    flops = 2 * rows * width * table
    if weight is not None:
        inner = weight.shape[0]
        in_specs.append(pl.BlockSpec((inner, width), lambda i, n: (0, 0)))
        args.append(weight)
        out_specs.append(pl.BlockSpec((tile, inner), lambda i, n: (i, 0)))
        out_shape.append(jax.ShapeDtypeStruct((rows, inner), BF16))
        kernel = combine_project_kernel
        flops += 2 * rows * width * inner
    return pl.pallas_call(
        functools.partial(kernel, count),
        grid_spec=pltpu.PrefetchScalarGridSpec(
            num_scalar_prefetch=1, grid=(rows // tile,), in_specs=in_specs, out_specs=out_specs
        ),
        out_shape=out_shape,
        compiler_params=pltpu.CompilerParams(vmem_limit_bytes=48 << 20),
        cost_estimate=pl.CostEstimate(
            flops=flops, bytes_accessed=2 * (2 * rows + table) * width, transcendentals=0
        ),
    )(first, *args)


def gelu_pair(pre):
    cdf = 0.5 + 0.5 * lax.erf(pre * (2.0**-0.5))
    density = jnp.exp(-0.5 * pre * pre) * ((2.0 * math.pi) ** -0.5)
    return (pre * cdf).astype(BF16), (cdf + pre * density).astype(BF16)


def without_base(kernel, count):
    def wrapped(*refs):
        kernel(*refs[:count], None, *refs[count:])

    return wrapped


def expert_forward_kernel(count, x_ref, base_ref, *refs):
    w_in, w_out = refs[:count], refs[count : 2 * count]
    act_ref, slope_ref, out_ref = refs[2 * count :]
    x = x_ref[...]
    total = base_ref[...] if base_ref is not None else None
    width = w_in[0].shape[1]
    chunk = min(width, 1024)
    blocks = [(i, c) for i in range(count) for c in range(0, width, chunk)]

    def into(i, c):
        return dot(x, w_in[i][:, c : c + chunk], ((1,), (0,)))

    ahead = into(*blocks[0])
    for n, (i, c) in enumerate(blocks):
        pre = ahead
        if n + 1 < len(blocks):
            ahead = into(*blocks[n + 1])
        act, slope = gelu_pair(pre)
        act_ref[:, i * width + c : i * width + c + chunk] = act
        slope_ref[:, i * width + c : i * width + c + chunk] = slope
        term = dot(act, w_out[i][c : c + chunk, :], ((1,), (0,)))
        total = term if total is None else total + term
    out_ref[...] = total.astype(out_ref.dtype)


def expert_forward(x, w_in, w_out, base=None):
    rows, width = x.shape
    count, unused, inner = w_in.shape
    hidden = count * inner
    tile = rows // 2

    def row(n):
        return pl.BlockSpec((tile, n), lambda i: (i, 0))

    specs = [row(width)]
    args = [x]
    kernel = functools.partial(expert_forward_kernel, count)
    if base is not None:
        specs.append(row(width))
        args.append(base)
    else:
        kernel = without_base(kernel, 1)
    specs += [
        pl.BlockSpec(
            (None, *w.shape[1:]), functools.partial(lambda j, i: (j, 0, 0), j), pipeline_mode=pl.Buffered(1)
        )
        for w in (w_in, w_out)
        for j in range(count)
    ]
    return pl.pallas_call(
        kernel,
        grid=(rows // tile,),
        in_specs=specs,
        out_specs=[row(hidden), row(hidden), row(width)],
        out_shape=[
            jax.ShapeDtypeStruct((rows, hidden), BF16),
            jax.ShapeDtypeStruct((rows, hidden), BF16),
            jax.ShapeDtypeStruct((rows, width), BF16 if base is None else F32),
        ],
        compiler_params=pltpu.CompilerParams(vmem_limit_bytes=48 << 20),
        cost_estimate=pl.CostEstimate(
            flops=4 * rows * width * hidden,
            bytes_accessed=4 * width * hidden + 4 * rows * hidden + 6 * rows * width,
            transcendentals=2 * rows * hidden,
        ),
    )(*args, *[w_in] * count, *[w_out] * count)


def expert_backward_kernel(count, g_ref, slope_ref, base_ref, *refs):
    w_in, w_out = refs[:count], refs[count : 2 * count]
    pre_ref, out_ref = refs[2 * count :]
    g = g_ref[...]
    total = base_ref[...] if base_ref is not None else None
    width = w_in[0].shape[1]
    chunk = min(width, 1024)
    blocks = [(i, c) for i in range(count) for c in range(0, width, chunk)]

    def into(i, c):
        return dot(g, w_out[i][c : c + chunk, :], ((1,), (1,)))

    ahead = into(*blocks[0])
    for n, (i, c) in enumerate(blocks):
        back = ahead
        if n + 1 < len(blocks):
            ahead = into(*blocks[n + 1])
        place = slice(i * width + c, i * width + c + chunk)
        pre = (back * slope_ref[:, place].astype(F32)).astype(BF16)
        pre_ref[:, place] = pre
        term = dot(pre, w_in[i][:, c : c + chunk], ((1,), (1,)))
        total = term if total is None else total + term
    out_ref[...] = total.astype(out_ref.dtype)


def expert_backward(g, slope, w_in, w_out, base=None):
    rows, width = g.shape
    count, unused, inner = w_in.shape
    hidden = slope.shape[1]
    tile = rows // 2

    def row(n):
        return pl.BlockSpec((tile, n), lambda i: (i, 0))

    specs = [row(width), row(hidden)]
    args = [g, slope]
    kernel = functools.partial(expert_backward_kernel, count)
    if base is not None:
        specs.append(row(width))
        args.append(base)
    else:
        kernel = without_base(kernel, 2)
    specs += [
        pl.BlockSpec(
            (None, *w.shape[1:]), functools.partial(lambda j, i: (j, 0, 0), j), pipeline_mode=pl.Buffered(1)
        )
        for w in (w_in, w_out)
        for j in range(count)
    ]
    return pl.pallas_call(
        kernel,
        grid=(rows // tile,),
        in_specs=specs,
        out_specs=[row(hidden), row(width)],
        out_shape=[
            jax.ShapeDtypeStruct((rows, hidden), BF16),
            jax.ShapeDtypeStruct((rows, width), BF16 if base is None else F32),
        ],
        compiler_params=pltpu.CompilerParams(vmem_limit_bytes=48 << 20),
        cost_estimate=pl.CostEstimate(
            flops=4 * rows * width * hidden,
            bytes_accessed=4 * width * hidden + 4 * rows * hidden + 6 * rows * width,
            transcendentals=0,
        ),
    )(*args, *[w_in] * count, *[w_out] * count)


def outer_kernel(count, *refs):
    lefts, rights, out_ref = refs[:count], refs[count : 2 * count], refs[-1]
    total = None
    for a, b in zip(lefts, rights):
        term = dot(a[...], b[...], ((0,), (0,)))
        total = term if total is None else total + term
    out_ref[...] = total.astype(out_ref.dtype)


def outer(lefts, rights, blocks):
    rows = lefts[0].shape[0]
    count = len(lefts)
    left_blocks = blocks if lefts[0].shape[1] > rights[0].shape[1] else 1
    right_blocks = blocks // left_blocks
    left_width = lefts[0].shape[1] // left_blocks
    right_width = rights[0].shape[1] // right_blocks
    tile = min(256, left_width)
    steps = left_width // tile
    if left_blocks > 1:
        left_spec = pl.BlockSpec((rows, tile), lambda j, i: (0, j * steps + i))
        right_spec = pl.BlockSpec((rows, right_width), lambda j, i: (0, 0))
    else:
        left_spec = pl.BlockSpec((rows, tile), lambda j, i: (0, i))
        right_spec = pl.BlockSpec((rows, right_width), lambda j, i: (0, j))
    return pl.pallas_call(
        functools.partial(outer_kernel, count),
        grid=(blocks, steps),
        in_specs=[left_spec] * count + [right_spec] * count,
        out_specs=pl.BlockSpec((None, tile, right_width), lambda j, i: (j, i, 0)),
        out_shape=jax.ShapeDtypeStruct((blocks, left_width, right_width), BF16),
        compiler_params=pltpu.CompilerParams(vmem_limit_bytes=48 << 20),
        cost_estimate=pl.CostEstimate(
            flops=2 * count * blocks * rows * left_width * right_width,
            bytes_accessed=2 * blocks * (count * rows * (left_width + right_width) + left_width * right_width),
            transcendentals=0,
        ),
    )(*lefts, *rights)


class Grid:
    def __init__(self, shards, experts):
        self.size = shards
        self.experts = experts
        self.depth = experts // CORES

    def over_core(self, value):
        return lax.ppermute(value, "dp", [(d, d ^ 1) for d in range(self.experts)])

    def over_tensor(self, value, other):
        return lax.ppermute(value, "tensor", [(t, t ^ other) for t in range(self.size)])

    def sum_tensor(self, value):
        step = 1
        while step < self.size:
            value = value + self.over_tensor(value, step)
            step *= 2
        return value

    def sum_dp(self, value):
        step = 1
        while step < self.experts:
            pairs = [(d, d ^ step) for d in range(self.experts)]
            value = value + lax.ppermute(value, "dp", pairs)
            step *= 2
        return value

    def exchange_depth(self, value):
        groups = [[CORES * z + c for z in range(self.depth)] for c in range(CORES)]
        return lax.all_to_all(
            value, "dp", split_axis=0, concat_axis=0, axis_index_groups=groups, tiled=True
        )


ROWS_OF_CHIPS = [[0, 2], [1, 3]]


def owner_pairs(grid, back=False):
    pairs = []
    for z in range(grid.depth):
        for core in range(CORES):
            for y in range(2):
                for x in range(2):
                    here = (CORES * z + core) * 4 + 2 * y + x
                    there = (CORES * z + 1 - x) * 4 + 2 * y + core
                    pairs.append((there, here) if back else (here, there))
    return pairs


def fetch_near(grid, weight):
    return lax.ppermute(weight, ("dp", "tensor"), owner_pairs(grid)) if grid.size == 4 else weight


def fetch_hidden(grid, weight):
    if grid.size == 4:
        return lax.all_gather(weight, "tensor", axis=0, axis_index_groups=ROWS_OF_CHIPS, tiled=False)
    core = lax.axis_index("dp") % CORES
    every = lax.all_gather(weight, "tensor", axis=0, tiled=False)
    chosen = jnp.where(lax.axis_index("tensor") % 2 == core, every, grid.over_core(every))
    chosen = chosen.reshape(grid.size // 2, 2, *weight.shape)
    return jnp.where(core == 0, chosen[:, 0], chosen[:, 1])


def sum_hidden(grid, pieces):
    if grid.size != 4:
        return pieces
    return lax.psum_scatter(
        pieces, "tensor", scatter_dimension=0, axis_index_groups=ROWS_OF_CHIPS, tiled=False
    )


def return_hidden(grid, pieces):
    if grid.size == 4:
        return lax.ppermute(pieces, ("dp", "tensor"), owner_pairs(grid, True))
    core = lax.axis_index("dp") % CORES
    me = lax.axis_index("tensor")
    zero = jnp.zeros_like(pieces)
    row = jnp.stack([jnp.where(core == c, pieces, zero) for c in range(CORES)], axis=1)
    row = row.reshape(grid.size, *pieces.shape[1:])
    wide = jnp.stack([jnp.where(me % 2 == parity, row, jnp.zeros_like(row)) for parity in range(2)])
    mine = lax.psum_scatter(wide, "tensor", scatter_dimension=1, tiled=False)
    other = grid.over_core(jnp.where(core == 0, mine[1], mine[0]))
    total = jnp.where(core == 0, mine[0], mine[1]).astype(F32) + other.astype(F32)
    return total.astype(BF16)


class Gather:
    def __init__(self, grid, value):
        self.grid = grid
        if grid.size != 4:
            self.pieces = [lax.all_gather(value, "tensor", axis=0, tiled=True)]
            self.devices = [jnp.int32(0)]
            return
        me = lax.axis_index("tensor")
        self.pieces = [value, grid.over_tensor(value, 1), grid.over_tensor(value, 2)]
        self.devices = [jnp.bitwise_xor(me, other) for other in range(4)]

    def ready(self):
        return self.pieces[1:3]

    def joined(self):
        if self.grid.size != 4:
            return self.pieces[0]
        rows, width = self.pieces[0].shape
        out = jnp.zeros((4 * rows, width), self.pieces[0].dtype)
        for piece, device in zip(self.pieces, self.devices):
            out = lax.dynamic_update_slice(out, piece, (device * rows, 0))
        return out

    def finish(self, *others, over=1):
        if self.grid.size == 4:
            self.pieces.append(self.grid.over_tensor(after(self.pieces[3 - over], *others), over))
        return self.pieces


def gather_rows(grid, value):
    if grid.size != 4:
        return lax.all_gather(value, "tensor", axis=0, tiled=True), [], []
    rows, width = value.shape
    half = rows // 2
    first, second = value[:half], value[half:]
    first_x = grid.over_tensor(first, 1)
    second_y = grid.over_tensor(second, 2)
    first_y = grid.over_tensor(first, 2)
    second_x = grid.over_tensor(second, 1)
    first_xy = grid.over_tensor(first_x, 2)
    second_xy = grid.over_tensor(second_y, 1)
    me = lax.axis_index("tensor")
    out = jnp.zeros((4 * rows, width), value.dtype)
    out = lax.dynamic_update_slice(out, value, (me * rows, 0))
    for other, top, bottom in ((1, first_x, second_x), (2, first_y, second_y), (3, first_xy, second_xy)):
        place = jnp.bitwise_xor(me, other) * rows
        out = lax.dynamic_update_slice(out, top, (place, 0))
        out = lax.dynamic_update_slice(out, bottom, (place + half, 0))
    return out, [first_x, second_y], [first_xy, second_xy]


def scatter_rows(grid, term, beside):
    size, rows, width = term.shape
    if size != 4:
        total = lax.psum_scatter(term.astype(BF16), "tensor", scatter_dimension=0, tiled=False)
        return total.astype(F32), [], beside
    me = lax.axis_index("tensor")
    half = width // 2

    def pick(other, low):
        place = jnp.bitwise_xor(me, other)
        return lax.dynamic_slice(term, (place, 0, low), (1, rows, half))[0]

    halves = ((0, 1, 2), (half, 2, 1))
    got_far = [grid.over_tensor(pick(3, low).astype(BF16), near) for low, near, far in halves]
    got_own = [grid.over_tensor(pick(near, low).astype(BF16), near) for low, near, far in halves]
    first, second, *beside = together(*got_far, *beside)
    totals, arrived = [], []
    for (low, near, far), far_term, own_term in zip(halves, (first, second), got_own):
        onward = pick(far, low).astype(F32) + far_term.astype(F32)
        got = grid.over_tensor(onward.astype(BF16), far)
        arrived.append(got)
        totals.append(pick(0, low).astype(F32) + own_term.astype(F32) + got.astype(F32))
    return jnp.concatenate(totals, axis=1), arrived, beside


def body(
    tokens,
    lengths,
    routes,
    fill_order,
    norm_gain,
    norm_bias,
    qkv_weight,
    out_weight,
    centroids,
    expert_in,
    expert_out,
    cotangent,
):
    tok_count, model_width = tokens.shape
    seq_count = lengths.shape[0]
    seq_len = tok_count // seq_count
    heads_here = qkv_weight.shape[1]
    head_size = out_weight.shape[1]
    experts = lax.axis_size("dp")
    shards = lax.axis_size("tensor")
    grid = Grid(shards, experts)
    me = lax.axis_index("tensor")
    parity, part = me % 2, me // 2
    core = lax.axis_index("dp") % CORES
    depth = experts // CORES
    row_parts = shards // 2
    capacity = (9 * tok_count + 8 * experts - 1) // (8 * experts)
    share = 16 * -(-capacity // (16 * row_parts))
    padded = share * row_parts
    own_rows = depth * share
    tok_rows = tok_count // shards

    near = [fetch_near(grid, w[0, k]) for k in range(2) for w in (expert_in, expert_out)]
    out_flat = out_weight.reshape(heads_here * head_size, model_width)
    out_gather = Gather(grid, out_flat)
    out_gather.finish(over=2)
    out_all = out_gather.joined()
    centroid = jnp.where(parity == core, centroids[0], grid.over_core(centroids[0]))

    slots = token_slots(
        routes, fill_order, lengths, seq_len, capacity, padded, experts * padded
    )
    slot = slots.reshape(tok_count, 1)
    rank = slot % padded
    slot_device = (rank // share) * 2 + (slot // padded) % 2
    slot_place = (slot_device * depth + slot // (2 * padded)) * share + rank % share
    place = jnp.where(slot < experts * padded, slot_place, -1)
    own_first = (parity * padded + part * share).astype(jnp.int32).reshape(1)

    def to_experts(rows):
        picked = pick_rows(rows, slots, own_first, depth, share, CORES, padded)
        return grid.exchange_depth(picked.reshape(depth, share, model_width)).reshape(own_rows, model_width)

    def leave_experts(rows):
        return grid.exchange_depth(rows.reshape(depth, share, model_width))

    def row_starts(gathered):
        return jnp.stack([device * own_rows for device in gathered.devices]).astype(jnp.int32)

    grad_ret = to_experts(cotangent).astype(F32)
    heads = heads_here + heads_here % 2
    fused = qkv_weight.reshape(model_width, heads_here, 3, head_size)
    fused = jnp.swapaxes(fused, 1, 2)
    fused = jnp.pad(fused, ((0, 0), (0, 0), (0, heads - heads_here), (0, 0)))
    fused = fused.reshape(model_width, 3 * heads * head_size)
    inner = heads_here * head_size
    ln_in, projected = norm_project(tokens, norm_gain, norm_bias, fused)
    near[0] = after(near[0], projected)
    attended, log_total = attend(projected, lengths, seq_count, heads, head_size)
    near[1:] = [after(piece, attended) for piece in near[1:]]
    win, wout = [fetch_hidden(grid, w) for w in near[::2]], [fetch_hidden(grid, w) for w in near[1::2]]
    if shards == 4:
        gathered = Gather(grid, attended)
        pieces = gathered.finish()
        first = jnp.stack(gathered.devices).astype(jnp.int32)
    else:
        every = lax.all_gather(attended[:, :inner], "tensor", axis=1, tiled=True)
        pieces, first = [every], jnp.zeros((1,), jnp.int32)
    sent = out_project(pieces, first, out_all, tokens)

    expert_rows = to_experts(sent)
    gate = jax.nn.sigmoid(jnp.dot(expert_rows, centroid, preferred_element_type=F32))[:, None]
    current = expert_rows.astype(F32)
    saved = []
    for k in range(2):
        here = current.astype(BF16)
        there = grid.over_core(here)
        act, slope, total = expert_forward(here, win[k], wout[k], current)
        act_there, slope_there, part = expert_forward(there, win[k], wout[k])
        current = total + grid.over_core(part).astype(F32)
        saved.append(([here, there], [act, act_there], [slope, slope_there]))
    returned = leave_experts((gate * current).astype(BF16))

    grad_gate = jnp.sum(grad_ret * current, axis=1, keepdims=True)
    grad_logit = grad_gate * gate * (1.0 - gate)
    grad_current = gate * grad_ret
    branches = [None, None]
    for k in (1, 0):
        slopes = saved[k][2]
        here = grad_current.astype(BF16)
        there = grid.over_core(here)
        grad_pre_there, part = expert_backward(there, slopes[1], win[k], wout[k])
        grad_pre, total = expert_backward(here, slopes[0], win[k], wout[k], grad_current)
        grad_current = total + grid.over_core(part).astype(F32)
        branches[k] = ([here, there], [grad_pre, grad_pre_there])
    grad_rows = (grad_current + grad_logit * centroid.astype(F32)[None, :]).astype(BF16)
    centroid_part = jnp.sum(grad_logit * expert_rows.astype(F32), axis=0, keepdims=True)
    centroid_parts = grid.sum_tensor(
        jnp.concatenate([jnp.where(parity == p, centroid_part, 0.0) for p in range(2)], axis=0)
    )
    centroid_other = grid.over_core(centroid_parts)
    grad_centroid = lax.dynamic_slice_in_dim(centroid_parts + centroid_other, core, 1, 0)

    moved = leave_experts(grad_rows)
    outers = []
    for k in (1, 0):
        rows_in, acts, unused = saved[k]
        branch, grad_pres = branches[k]
        blocks = win[k].shape[0]
        outers += [outer(rows_in, grad_pres, blocks), outer(acts, branch, blocks)]
    sums_in2, sums_back2 = [sum_hidden(grid, pieces) for pieces in outers[:2]]
    moved = after(moved, *outers, centroid_other)
    grad_gather = Gather(grid, moved.reshape(own_rows, model_width))
    sums_in1, sums_back1 = [
        sum_hidden(grid, after(pieces, *grad_gather.ready())) for pieces in outers[2:]
    ]
    pieces = grad_gather.finish()
    first = row_starts(grad_gather)
    out_padded = jnp.pad(out_flat, ((0, heads * head_size - inner), (0, 0)))
    grad_mixed, grad_attended = combine(pieces, first, place, cotangent, out_padded)
    back_in2 = return_hidden(grid, after(sums_in2, *pieces[1:]))
    back_out2 = return_hidden(grid, after(sums_back2, *pieces[1:]))
    out_gather = Gather(grid, after(returned, *pieces[1:]).reshape(own_rows, model_width))
    grad_projected = attend_back(
        projected,
        attended,
        grad_attended,
        log_total,
        lengths,
        seq_count,
        heads,
        head_size,
    )
    grad_ln_part = dot(grad_projected, fused, ((1,), (1,))).astype(BF16)
    grad_ln_part, grad_mixed, grad_projected = together(
        grad_ln_part, grad_mixed, grad_projected, back_in2, back_out2, sums_in1, sums_back1, *out_gather.ready()
    )[:3]
    grad_out_local = dot(attended[:, :inner], grad_mixed, ((0,), (0,))).reshape(
        heads_here, head_size, model_width
    )
    grad_qkv_local = dot(ln_in, grad_projected, ((0,), (0,)))
    grad_sums = (grad_qkv_local.astype(BF16), grad_out_local.astype(BF16))
    grad_ln, scattered, grad_sums = scatter_rows(
        grid, grad_ln_part.reshape(shards, tok_rows, model_width), grad_sums
    )
    grad_sums = lax.psum(grad_sums, "dp")
    scattered = scattered + [grad_projected]
    out_pieces = out_gather.finish(*scattered, over=2)

    def own(rows):
        return lax.dynamic_slice_in_dim(rows, me * tok_rows, tok_rows, 0)

    own_tokens = own(tokens).astype(F32)
    centre = own_tokens - jnp.mean(own_tokens, axis=1, keepdims=True)
    own_scale = lax.rsqrt(jnp.mean(centre * centre, axis=1, keepdims=True) + EPSILON)
    own_normed = centre * own_scale
    grad_normed = grad_ln * norm_gain
    mean_plain = jnp.mean(grad_normed, axis=1, keepdims=True)
    mean_cross = jnp.mean(grad_normed * own_normed, axis=1, keepdims=True)
    grad_input = own(grad_mixed).astype(F32) + own_scale * (
        grad_normed - mean_plain - own_normed * mean_cross
    )
    grad_tokens, halfway, gathered = gather_rows(grid, grad_input.astype(BF16))
    output = combine(out_pieces, first, place, after(sent, *scattered))[0]
    norm_total = jnp.stack([jnp.sum(grad_ln * own_normed, axis=0), jnp.sum(grad_ln, axis=0)])
    norm_total = grid.sum_tensor(after(norm_total, *halfway))
    halfway = halfway + [norm_total]
    back_in1 = return_hidden(grid, after(sums_in1, *halfway))
    back_out1 = return_hidden(grid, after(sums_back1, *halfway))
    norm_total = grid.sum_dp(norm_total)
    norm_total = lax.dynamic_slice_in_dim(
        norm_total, me * (model_width // shards), model_width // shards, 1
    )
    grad_qkv, grad_out_weight = [after(total, *gathered) for total in grad_sums]
    grad_qkv = grad_qkv.astype(F32).reshape(model_width, 3, heads, head_size)[:, :, :heads_here]
    grad_qkv_weight = jnp.swapaxes(grad_qkv, 1, 2).reshape(model_width, heads_here, 3 * head_size)
    return (
        output,
        grad_tokens,
        norm_total[0],
        norm_total[1],
        grad_qkv_weight,
        grad_out_weight.astype(F32),
        grad_centroid,
        jnp.stack([back_in1, back_in2])[None].astype(F32),
        jnp.stack([back_out1, back_out2])[None].astype(F32),
    )


def solution(mesh):
    return jax.shard_map(
        body,
        mesh=mesh,
        in_specs=(
            P("dp", None),
            P("dp"),
            P("dp", None),
            P("dp", None),
            P(),
            P(),
            P(None, "tensor", None),
            P("tensor", None, None),
            P("dp", None),
            P("dp", None, None, "tensor"),
            P("dp", None, "tensor", None),
            P("dp", None),
        ),
        out_specs=(
            P("dp", None),
            P("dp", None),
            P("tensor"),
            P("tensor"),
            P(None, "tensor", None),
            P("tensor", None, None),
            P("dp", None),
            P("dp", None, None, "tensor"),
            P("dp", None, "tensor", None),
        ),
        check_vma=False,
    )
```

```python
import functools
import math

import jax
import jax.numpy as jnp
from jax import lax
from jax.experimental import pallas as pl
from jax.experimental.pallas import tpu as pltpu
from jax.sharding import PartitionSpec as P

EPSILON = 1e-05
MASKED = -1e30
F32 = jnp.float32
BF16 = jnp.bfloat16
CORES = 2


def after(value, *others):
    return lax.optimization_barrier((value, *others))[0]


def together(*values):
    return lax.optimization_barrier(values)


def dot(a, b, contract):
    return lax.dot_general(a, b, (contract, ((), ())), preferred_element_type=F32)


def norm_project_kernel(x_ref, gain_ref, bias_ref, w_ref, ln_ref, out_ref):
    x = x_ref[...].astype(F32)
    centre = x - jnp.mean(x, axis=1, keepdims=True)
    scale = lax.rsqrt(jnp.mean(centre * centre, axis=1, keepdims=True) + EPSILON)
    ln = (centre * scale * gain_ref[...] + bias_ref[...]).astype(BF16)
    ln_ref[...] = ln
    out_ref[...] = dot(ln, w_ref[...], ((1,), (0,))).astype(BF16)


def norm_project(tokens, gain, bias, weight):
    rows, width = tokens.shape
    columns = weight.shape[1]
    tile = 512
    return pl.pallas_call(
        norm_project_kernel,
        grid=(rows // tile,),
        in_specs=[
            pl.BlockSpec((tile, width), lambda i: (i, 0)),
            pl.BlockSpec((1, width), lambda i: (0, 0)),
            pl.BlockSpec((1, width), lambda i: (0, 0)),
            pl.BlockSpec((width, columns), lambda i: (0, 0)),
        ],
        out_specs=[
            pl.BlockSpec((tile, width), lambda i: (i, 0)),
            pl.BlockSpec((tile, columns), lambda i: (i, 0)),
        ],
        out_shape=[
            jax.ShapeDtypeStruct((rows, width), BF16),
            jax.ShapeDtypeStruct((rows, columns), BF16),
        ],
        compiler_params=pltpu.CompilerParams(vmem_limit_bytes=40 << 20),
        cost_estimate=pl.CostEstimate(
            flops=2 * rows * width * columns,
            bytes_accessed=2 * (2 * rows * width + rows * columns + width * columns),
            transcendentals=rows,
        ),
    )(tokens, gain[None], bias[None], weight)


def attend_kernel(head_size, group, tile, len_ref, q_ref, k_ref, v_ref, o_ref, lse_ref):
    seq_len, lanes = q_ref.shape
    scale = head_size**-0.5
    limit = len_ref[pl.program_id(0)]
    keys = k_ref[...]
    values = v_ref[...]
    key_place = lax.broadcasted_iota(jnp.int32, (seq_len, lanes), 0)
    lane = lax.broadcasted_iota(jnp.int32, (seq_len, lanes), 1)
    causal = lax.broadcasted_iota(jnp.int32, (tile, tile), 0) <= lax.broadcasted_iota(
        jnp.int32, (tile, tile), 1
    )
    tall = lax.broadcasted_iota(jnp.int32, (lanes, tile), 0)
    lane_q = lax.broadcasted_iota(jnp.int32, (tile, lanes), 1)
    heads = []
    for a in range(group):
        mine = (lane >= a * head_size) & (lane < (a + 1) * head_size)
        spare = ((a + 1) % group) * head_size
        extra = jnp.where((lane == spare) & (key_place >= limit), MASKED, 0.0).astype(BF16)
        k_a = jnp.where(mine, keys, extra)
        v_a = jnp.where(mine, values, jnp.ones((), BF16))
        heads.append((k_a, v_a, spare))
    for i in range(seq_len // tile):
        end = (i + 1) * tile
        q = (q_ref[i * tile : end, :].astype(F32) * scale).astype(BF16)
        out = None
        for a in range(group):
            k_a, v_a, spare = heads[a]
            mine_q = (lane_q >= a * head_size) & (lane_q < (a + 1) * head_size)
            q_a = jnp.where(mine_q, q, jnp.where(lane_q == spare, 1.0, 0.0).astype(BF16))
            scores = dot(k_a[:end], q_a, ((1,), (1,)))
            last = jnp.where(causal, scores[i * tile :], MASKED)
            scores = jnp.concatenate([scores[: i * tile], last], axis=0) if i else last
            top = jnp.max(scores, axis=0, keepdims=True)
            probs = jnp.exp(scores - top).astype(BF16)
            result = dot(v_a[:end], probs, ((0,), (0,)))
            total = result[spare : spare + 1, :]
            lse_ref[0, 0, a : a + 1, i * tile : end] = top + jnp.log(total)
            result = result / total
            if out is None:
                out = result
            else:
                out = jnp.where((tall >= a * head_size) & (tall < (a + 1) * head_size), result, out)
        o_ref[i * tile : end, :] = out.T.astype(BF16)


def attend(projected, lengths, seqs, heads, head_size):
    rows = projected.shape[0]
    seq_len = rows // seqs
    group = 2
    lanes = group * head_size
    groups = heads // group
    tile = 256
    return pl.pallas_call(
        functools.partial(attend_kernel, head_size, group, tile),
        grid_spec=pltpu.PrefetchScalarGridSpec(
            num_scalar_prefetch=1,
            grid=(seqs, groups),
            in_specs=[
                pl.BlockSpec((seq_len, lanes), lambda s, g, n: (s, g)),
                pl.BlockSpec((seq_len, lanes), lambda s, g, n: (s, groups + g)),
                pl.BlockSpec((seq_len, lanes), lambda s, g, n: (s, 2 * groups + g)),
            ],
            out_specs=[
                pl.BlockSpec((seq_len, lanes), lambda s, g, n: (s, g)),
                pl.BlockSpec((1, 1, group, seq_len), lambda s, g, n: (s, g, 0, 0)),
            ],
        ),
        out_shape=[
            jax.ShapeDtypeStruct((rows, heads * head_size), BF16),
            jax.ShapeDtypeStruct((seqs, groups, group, seq_len), F32),
        ],
        compiler_params=pltpu.CompilerParams(vmem_limit_bytes=40 << 20),
        cost_estimate=pl.CostEstimate(
            flops=4 * rows * seq_len * heads * head_size,
            bytes_accessed=8 * rows * heads * head_size,
            transcendentals=rows * seq_len * heads // 2,
        ),
    )(lengths, projected, projected, projected)


def attend_back_kernel(head_size, group, tile, len_ref, q_ref, k_ref, v_ref, o_ref, do_ref, lse_ref, out_ref, dk_acc, dv_acc):
    seq_len, lanes = q_ref.shape
    scale = head_size**-0.5
    limit = len_ref[pl.program_id(0)]
    keys = k_ref[...]
    values = v_ref[...]
    zero = jnp.zeros((), BF16)

    def place(kind):
        block = kind * pl.num_programs(1) + pl.program_id(1)
        return pl.ds(pl.multiple_of(block * lanes, lanes), lanes)

    key_place = lax.broadcasted_iota(jnp.int32, (seq_len, lanes), 0)
    lane = lax.broadcasted_iota(jnp.int32, (seq_len, lanes), 1)
    causal = lax.broadcasted_iota(jnp.int32, (tile, tile), 0) <= lax.broadcasted_iota(
        jnp.int32, (tile, tile), 1
    )
    lane_q = lax.broadcasted_iota(jnp.int32, (tile, lanes), 1)
    heads = []
    for a in range(group):
        mine = (lane >= a * head_size) & (lane < (a + 1) * head_size)
        spare = ((a + 1) % group) * head_size
        extra = jnp.where((lane == spare) & (key_place >= limit), MASKED, 0.0).astype(BF16)
        k_a = jnp.where(mine, keys, extra)
        ones = jnp.where((lane == spare) | (lane == spare + 1), 1.0, 0.0).astype(BF16)
        v_a = jnp.where(mine, values, ones)
        heads.append((k_a, v_a, spare))
    steps = seq_len // tile
    for i in reversed(range(steps)):
        end = (i + 1) * tile
        q = (q_ref[i * tile : end, :].astype(F32) * scale).astype(BF16)
        do = do_ref[i * tile : end, :]
        product = do.astype(F32) * o_ref[i * tile : end, :].astype(F32)
        dq = None
        dk = None
        dv = None
        for a in range(group):
            k_a, v_a, spare = heads[a]
            mine_q = (lane_q >= a * head_size) & (lane_q < (a + 1) * head_size)
            q_m = jnp.where(mine_q, q, zero)
            q_a = jnp.where(mine_q, q, jnp.where(lane_q == spare, 1.0, 0.0).astype(BF16))
            delta = -jnp.sum(jnp.where(mine_q, product, 0.0), axis=1, keepdims=True)
            high = delta.astype(BF16)
            low = (delta - high.astype(F32)).astype(BF16)
            do_m = jnp.where(mine_q, do, zero)
            do_a = jnp.where(lane_q == spare, high, jnp.where(lane_q == spare + 1, low, do_m))
            scores = dot(k_a[:end], q_a, ((1,), (1,)))
            last = jnp.where(causal, scores[i * tile :], MASKED)
            scores = jnp.concatenate([scores[: i * tile], last], axis=0) if i else last
            probs = jnp.exp(scores - lse_ref[0, 0, a : a + 1, i * tile : end])
            grad = dot(v_a[:end], do_a, ((1,), (1,)))
            grad = (probs * grad).astype(BF16)
            term_v = dot(probs.astype(BF16), do_m, ((1,), (0,)))
            term_k = dot(grad, q_m, ((1,), (0,)))
            term_q = dot(k_a[:end], grad, ((0,), (0,)))
            dv = term_v if dv is None else dv + term_v
            dk = term_k if dk is None else dk + term_k
            if dq is None:
                dq = term_q
            else:
                tall = lax.broadcasted_iota(jnp.int32, (lanes, tile), 0)
                dq = jnp.where((tall >= a * head_size) & (tall < (a + 1) * head_size), term_q, dq)
        out_ref[i * tile : end, place(0)] = (dq.T * scale).astype(BF16)
        if i == steps - 1:
            dk_acc[...] = dk
            dv_acc[...] = dv
        else:
            dk_acc[:end, :] += dk
            dv_acc[:end, :] += dv
    out_ref[:, place(1)] = dk_acc[...].astype(BF16)
    out_ref[:, place(2)] = dv_acc[...].astype(BF16)


def attend_back(projected, attended, grad_attended, lse, lengths, seqs, heads, head_size):
    rows = projected.shape[0]
    seq_len = rows // seqs
    group = 2
    lanes = group * head_size
    groups = heads // group
    tile = 256
    spec = pl.BlockSpec((seq_len, lanes), lambda s, g, n: (s, g))
    return pl.pallas_call(
        functools.partial(attend_back_kernel, head_size, group, tile),
        grid_spec=pltpu.PrefetchScalarGridSpec(
            num_scalar_prefetch=1,
            grid=(seqs, groups),
            in_specs=[
                spec,
                pl.BlockSpec((seq_len, lanes), lambda s, g, n: (s, groups + g)),
                pl.BlockSpec((seq_len, lanes), lambda s, g, n: (s, 2 * groups + g)),
                spec,
                spec,
                pl.BlockSpec((1, 1, group, seq_len), lambda s, g, n: (s, g, 0, 0)),
            ],
            out_specs=pl.BlockSpec((seq_len, 3 * groups * lanes), lambda s, g, n: (s, 0)),
            scratch_shapes=[pltpu.VMEM((seq_len, lanes), F32), pltpu.VMEM((seq_len, lanes), F32)],
        ),
        out_shape=jax.ShapeDtypeStruct((rows, 3 * heads * head_size), BF16),
        compiler_params=pltpu.CompilerParams(vmem_limit_bytes=48 << 20),
        cost_estimate=pl.CostEstimate(
            flops=10 * rows * seq_len * heads * head_size,
            bytes_accessed=16 * rows * heads * head_size,
            transcendentals=rows * seq_len * heads // 2,
        ),
    )(lengths, projected, projected, projected, attended, grad_attended, lse)


def place_kernel(order_ref, out_ref):
    count = out_ref.shape[1]
    tile = order_ref.shape[0]
    step = pl.program_id(0)
    token = lax.broadcasted_iota(jnp.int32, (tile, count), 1)
    index = lax.broadcasted_iota(jnp.int32, (tile, 1), 0) + step * tile
    hit = jnp.sum(jnp.where(order_ref[...] == token, index, 0), axis=0, keepdims=True)

    @pl.when(step == 0)
    def _():
        out_ref[...] = hit

    @pl.when(step > 0)
    def _():
        out_ref[...] += hit


def rank_kernel(key_ref, keys_ref, out_ref):
    step = pl.program_id(0)
    keys = keys_ref[...]
    base = jnp.bitwise_and(keys, -4096)
    key = key_ref[...]
    hit = jnp.sum(jnp.where((key < keys) & (key >= base), 1, 0), axis=0, keepdims=True)

    @pl.when(step == 0)
    def _():
        out_ref[...] = hit

    @pl.when(step > 0)
    def _():
        out_ref[...] += hit


def tall_reduce(kernel, column, rows, count):
    tile = 512
    specs = [pl.BlockSpec((tile, 1), lambda i: (i, 0))]
    specs += [pl.BlockSpec((1, count), lambda i: (0, 0)) for _ in rows]
    return pl.pallas_call(
        kernel,
        grid=(count // tile,),
        in_specs=specs,
        out_specs=pl.BlockSpec((1, count), lambda i: (0, 0)),
        out_shape=jax.ShapeDtypeStruct((1, count), jnp.int32),
        cost_estimate=pl.CostEstimate(
            flops=4 * count * count, bytes_accessed=600 * count, transcendentals=0
        ),
    )(column, *rows)


def token_slots(routes, order, lengths, seq_len, capacity, padded, none):
    count = routes.shape[0]
    places = jnp.arange(count, dtype=jnp.int32)[None]
    limits = jnp.repeat(lengths, seq_len, total_repeat_length=count)[None]
    valid = places % seq_len < limits
    turn = tall_reduce(place_kernel, order.reshape(count, 1), [], count)
    route = routes.reshape(1, count)
    keys = jnp.where(valid, route * 4096 + turn, 1 << 20)
    rank = tall_reduce(rank_kernel, keys.reshape(count, 1), [keys], count)
    return jnp.where(valid & (rank < capacity), route * padded + rank, none)


def pick_kernel(share, experts_step, padded, first_ref, slots_ref, rows_ref, out_ref):
    step = pl.program_id(0)
    start = first_ref[0] + step * experts_step * padded
    count = rows_ref.shape[0]
    slot = lax.broadcasted_iota(jnp.int32, (share, count), 0) + start
    chosen = jnp.where(slots_ref[...] == slot, 1.0, 0.0).astype(BF16)
    out_ref[...] = dot(chosen, rows_ref[...], ((1,), (0,))).astype(BF16)


def pick_rows(rows, slots, first, blocks, share, step, padded):
    count, width = rows.shape
    return pl.pallas_call(
        functools.partial(pick_kernel, share, step, padded),
        grid_spec=pltpu.PrefetchScalarGridSpec(
            num_scalar_prefetch=1,
            grid=(blocks,),
            in_specs=[
                pl.BlockSpec((1, count), lambda i, n: (0, 0)),
                pl.BlockSpec((count, width), lambda i, n: (0, 0)),
            ],
            out_specs=pl.BlockSpec((share, width), lambda i, n: (i, 0)),
        ),
        out_shape=jax.ShapeDtypeStruct((blocks * share, width), BF16),
        compiler_params=pltpu.CompilerParams(vmem_limit_bytes=40 << 20),
        cost_estimate=pl.CostEstimate(
            flops=2 * blocks * share * count * width,
            bytes_accessed=2 * (count + blocks * share) * width,
            transcendentals=0,
        ),
    )(first, slots, rows)


def out_project_kernel(count, first_ref, *refs):
    piece_refs, w_ref, x_ref, out_ref, wide = refs[:count], *refs[count:]
    for i, piece in enumerate(piece_refs):
        width = piece.shape[1]
        start = pl.multiple_of(first_ref[i] * width, width)
        wide[:, pl.ds(start, width)] = piece[...]
    out_ref[...] = (x_ref[...].astype(F32) + dot(wide[...], w_ref[...], ((1,), (0,)))).astype(BF16)


def out_project(pieces, first, weight, tokens):
    rows, width = tokens.shape
    inner = weight.shape[0]
    count = len(pieces)
    tile = 512
    return pl.pallas_call(
        functools.partial(out_project_kernel, count),
        grid_spec=pltpu.PrefetchScalarGridSpec(
            num_scalar_prefetch=1,
            grid=(rows // tile,),
            in_specs=[pl.BlockSpec((tile, p.shape[1]), lambda i, n: (i, 0)) for p in pieces]
            + [
                pl.BlockSpec((inner, width), lambda i, n: (0, 0)),
                pl.BlockSpec((tile, width), lambda i, n: (i, 0)),
            ],
            out_specs=pl.BlockSpec((tile, width), lambda i, n: (i, 0)),
            scratch_shapes=[pltpu.VMEM((tile, inner), BF16)],
        ),
        out_shape=jax.ShapeDtypeStruct((rows, width), BF16),
        compiler_params=pltpu.CompilerParams(vmem_limit_bytes=40 << 20),
        cost_estimate=pl.CostEstimate(
            flops=2 * rows * width * inner,
            bytes_accessed=2 * (3 * rows * width + inner * width),
            transcendentals=0,
        ),
    )(first, *pieces, weight, tokens)


def spread(count, first_ref, place_ref, piece_refs):
    place = place_ref[...]
    total = None
    for i in range(count):
        rows = piece_refs[i].shape[0]
        index = lax.broadcasted_iota(jnp.int32, (place.shape[0], rows), 1) + first_ref[i]
        chosen = jnp.where(place == index, 1.0, 0.0).astype(BF16)
        term = dot(chosen, piece_refs[i][...], ((1,), (0,)))
        total = term if total is None else total + term
    return total


def combine_kernel(count, first_ref, place_ref, base_ref, *refs):
    total = spread(count, first_ref, place_ref, refs[:count])
    refs[count][...] = (base_ref[...].astype(F32) + total).astype(BF16)


def combine_project_kernel(count, first_ref, place_ref, base_ref, *refs):
    total = spread(count, first_ref, place_ref, refs[:count])
    w_ref, out_ref, back_ref = refs[count:]
    out = (base_ref[...].astype(F32) + total).astype(BF16)
    out_ref[...] = out
    back_ref[...] = dot(out, w_ref[...], ((1,), (1,))).astype(BF16)


def combine(pieces, first, place, base, weight=None):
    rows, width = base.shape
    count = len(pieces)
    tile = 512
    block = pl.BlockSpec((tile, width), lambda i, n: (i, 0))
    in_specs = [pl.BlockSpec((tile, 1), lambda i, n: (i, 0)), block]
    in_specs += [pl.BlockSpec(p.shape, lambda i, n: (0, 0), pipeline_mode=pl.Buffered(1)) for p in pieces]
    args = [place, base, *pieces]
    out_specs, out_shape = [block], [jax.ShapeDtypeStruct((rows, width), BF16)]
    kernel = combine_kernel
    table = sum(p.shape[0] for p in pieces)
    flops = 2 * rows * width * table
    if weight is not None:
        inner = weight.shape[0]
        in_specs.append(pl.BlockSpec((inner, width), lambda i, n: (0, 0)))
        args.append(weight)
        out_specs.append(pl.BlockSpec((tile, inner), lambda i, n: (i, 0)))
        out_shape.append(jax.ShapeDtypeStruct((rows, inner), BF16))
        kernel = combine_project_kernel
        flops += 2 * rows * width * inner
    return pl.pallas_call(
        functools.partial(kernel, count),
        grid_spec=pltpu.PrefetchScalarGridSpec(
            num_scalar_prefetch=1, grid=(rows // tile,), in_specs=in_specs, out_specs=out_specs
        ),
        out_shape=out_shape,
        compiler_params=pltpu.CompilerParams(vmem_limit_bytes=48 << 20),
        cost_estimate=pl.CostEstimate(
            flops=flops, bytes_accessed=2 * (2 * rows + table) * width, transcendentals=0
        ),
    )(first, *args)


def gelu_pair(pre):
    cdf = 0.5 + 0.5 * lax.erf(pre * (2.0**-0.5))
    density = jnp.exp(-0.5 * pre * pre) * ((2.0 * math.pi) ** -0.5)
    return (pre * cdf).astype(BF16), (cdf + pre * density).astype(BF16)


def without_base(kernel, count):
    def wrapped(*refs):
        kernel(*refs[:count], None, *refs[count:])

    return wrapped


def expert_forward_kernel(count, x_ref, base_ref, *refs):
    w_in, w_out = refs[:count], refs[count : 2 * count]
    act_ref, slope_ref, out_ref = refs[2 * count :]
    x = x_ref[...]
    total = base_ref[...] if base_ref is not None else None
    width = w_in[0].shape[1]
    chunk = min(width, 1024)
    blocks = [(i, c) for i in range(count) for c in range(0, width, chunk)]

    def into(i, c):
        return dot(x, w_in[i][:, c : c + chunk], ((1,), (0,)))

    ahead = into(*blocks[0])
    for n, (i, c) in enumerate(blocks):
        pre = ahead
        if n + 1 < len(blocks):
            ahead = into(*blocks[n + 1])
        act, slope = gelu_pair(pre)
        act_ref[:, i * width + c : i * width + c + chunk] = act
        slope_ref[:, i * width + c : i * width + c + chunk] = slope
        term = dot(act, w_out[i][c : c + chunk, :], ((1,), (0,)))
        total = term if total is None else total + term
    out_ref[...] = total.astype(out_ref.dtype)


def expert_forward(x, w_in, w_out, base=None):
    rows, width = x.shape
    count, unused, inner = w_in.shape
    hidden = count * inner
    tile = rows // 2

    def row(n):
        return pl.BlockSpec((tile, n), lambda i: (i, 0))

    specs = [row(width)]
    args = [x]
    kernel = functools.partial(expert_forward_kernel, count)
    if base is not None:
        specs.append(row(width))
        args.append(base)
    else:
        kernel = without_base(kernel, 1)
    specs += [
        pl.BlockSpec(
            (None, *w.shape[1:]), functools.partial(lambda j, i: (j, 0, 0), j), pipeline_mode=pl.Buffered(1)
        )
        for w in (w_in, w_out)
        for j in range(count)
    ]
    return pl.pallas_call(
        kernel,
        grid=(rows // tile,),
        in_specs=specs,
        out_specs=[row(hidden), row(hidden), row(width)],
        out_shape=[
            jax.ShapeDtypeStruct((rows, hidden), BF16),
            jax.ShapeDtypeStruct((rows, hidden), BF16),
            jax.ShapeDtypeStruct((rows, width), BF16 if base is None else F32),
        ],
        compiler_params=pltpu.CompilerParams(vmem_limit_bytes=48 << 20),
        cost_estimate=pl.CostEstimate(
            flops=4 * rows * width * hidden,
            bytes_accessed=4 * width * hidden + 4 * rows * hidden + 6 * rows * width,
            transcendentals=2 * rows * hidden,
        ),
    )(*args, *[w_in] * count, *[w_out] * count)


def expert_backward_kernel(count, g_ref, slope_ref, base_ref, *refs):
    w_in, w_out = refs[:count], refs[count : 2 * count]
    pre_ref, out_ref = refs[2 * count :]
    g = g_ref[...]
    total = base_ref[...] if base_ref is not None else None
    width = w_in[0].shape[1]
    chunk = min(width, 1024)
    blocks = [(i, c) for i in range(count) for c in range(0, width, chunk)]

    def into(i, c):
        return dot(g, w_out[i][c : c + chunk, :], ((1,), (1,)))

    ahead = into(*blocks[0])
    for n, (i, c) in enumerate(blocks):
        back = ahead
        if n + 1 < len(blocks):
            ahead = into(*blocks[n + 1])
        place = slice(i * width + c, i * width + c + chunk)
        pre = (back * slope_ref[:, place].astype(F32)).astype(BF16)
        pre_ref[:, place] = pre
        term = dot(pre, w_in[i][:, c : c + chunk], ((1,), (1,)))
        total = term if total is None else total + term
    out_ref[...] = total.astype(out_ref.dtype)


def expert_backward(g, slope, w_in, w_out, base=None):
    rows, width = g.shape
    count, unused, inner = w_in.shape
    hidden = slope.shape[1]
    tile = rows // 2

    def row(n):
        return pl.BlockSpec((tile, n), lambda i: (i, 0))

    specs = [row(width), row(hidden)]
    args = [g, slope]
    kernel = functools.partial(expert_backward_kernel, count)
    if base is not None:
        specs.append(row(width))
        args.append(base)
    else:
        kernel = without_base(kernel, 2)
    specs += [
        pl.BlockSpec(
            (None, *w.shape[1:]), functools.partial(lambda j, i: (j, 0, 0), j), pipeline_mode=pl.Buffered(1)
        )
        for w in (w_in, w_out)
        for j in range(count)
    ]
    return pl.pallas_call(
        kernel,
        grid=(rows // tile,),
        in_specs=specs,
        out_specs=[row(hidden), row(width)],
        out_shape=[
            jax.ShapeDtypeStruct((rows, hidden), BF16),
            jax.ShapeDtypeStruct((rows, width), BF16 if base is None else F32),
        ],
        compiler_params=pltpu.CompilerParams(vmem_limit_bytes=48 << 20),
        cost_estimate=pl.CostEstimate(
            flops=4 * rows * width * hidden,
            bytes_accessed=4 * width * hidden + 4 * rows * hidden + 6 * rows * width,
            transcendentals=0,
        ),
    )(*args, *[w_in] * count, *[w_out] * count)


def outer_kernel(count, *refs):
    lefts, rights, out_ref = refs[:count], refs[count : 2 * count], refs[-1]
    total = None
    for a, b in zip(lefts, rights):
        term = dot(a[...], b[...], ((0,), (0,)))
        total = term if total is None else total + term
    out_ref[...] = total.astype(out_ref.dtype)


def outer(lefts, rights, blocks):
    rows = lefts[0].shape[0]
    count = len(lefts)
    left_blocks = blocks if lefts[0].shape[1] > rights[0].shape[1] else 1
    right_blocks = blocks // left_blocks
    left_width = lefts[0].shape[1] // left_blocks
    right_width = rights[0].shape[1] // right_blocks
    tile = min(256, left_width)
    steps = left_width // tile
    if left_blocks > 1:
        left_spec = pl.BlockSpec((rows, tile), lambda j, i: (0, j * steps + i))
        right_spec = pl.BlockSpec((rows, right_width), lambda j, i: (0, 0))
    else:
        left_spec = pl.BlockSpec((rows, tile), lambda j, i: (0, i))
        right_spec = pl.BlockSpec((rows, right_width), lambda j, i: (0, j))
    return pl.pallas_call(
        functools.partial(outer_kernel, count),
        grid=(blocks, steps),
        in_specs=[left_spec] * count + [right_spec] * count,
        out_specs=pl.BlockSpec((None, tile, right_width), lambda j, i: (j, i, 0)),
        out_shape=jax.ShapeDtypeStruct((blocks, left_width, right_width), BF16),
        compiler_params=pltpu.CompilerParams(vmem_limit_bytes=48 << 20),
        cost_estimate=pl.CostEstimate(
            flops=2 * count * blocks * rows * left_width * right_width,
            bytes_accessed=2 * blocks * (count * rows * (left_width + right_width) + left_width * right_width),
            transcendentals=0,
        ),
    )(*lefts, *rights)


class Grid:
    def __init__(self, shards, experts):
        self.size = shards
        self.experts = experts
        self.depth = experts // CORES

    def over_core(self, value):
        return lax.ppermute(value, "dp", [(d, d ^ 1) for d in range(self.experts)])

    def over_tensor(self, value, other):
        return lax.ppermute(value, "tensor", [(t, t ^ other) for t in range(self.size)])

    def sum_tensor(self, value):
        step = 1
        while step < self.size:
            value = value + self.over_tensor(value, step)
            step *= 2
        return value

    def sum_dp(self, value):
        step = 1
        while step < self.experts:
            pairs = [(d, d ^ step) for d in range(self.experts)]
            value = value + lax.ppermute(value, "dp", pairs)
            step *= 2
        return value

    def exchange_depth(self, value):
        groups = [[CORES * z + c for z in range(self.depth)] for c in range(CORES)]
        return lax.all_to_all(
            value, "dp", split_axis=0, concat_axis=0, axis_index_groups=groups, tiled=True
        )


ROWS_OF_CHIPS = [[0, 2], [1, 3]]


def owner_pairs(grid, back=False):
    pairs = []
    for z in range(grid.depth):
        for core in range(CORES):
            for y in range(2):
                for x in range(2):
                    here = (CORES * z + core) * 4 + 2 * y + x
                    there = (CORES * z + 1 - x) * 4 + 2 * y + core
                    pairs.append((there, here) if back else (here, there))
    return pairs


def fetch_near(grid, weight):
    return lax.ppermute(weight, ("dp", "tensor"), owner_pairs(grid)) if grid.size == 4 else weight


def fetch_hidden(grid, weight):
    if grid.size == 4:
        return lax.all_gather(weight, "tensor", axis=0, axis_index_groups=ROWS_OF_CHIPS, tiled=False)
    core = lax.axis_index("dp") % CORES
    every = lax.all_gather(weight, "tensor", axis=0, tiled=False)
    chosen = jnp.where(lax.axis_index("tensor") % 2 == core, every, grid.over_core(every))
    chosen = chosen.reshape(grid.size // 2, 2, *weight.shape)
    return jnp.where(core == 0, chosen[:, 0], chosen[:, 1])


def sum_hidden(grid, pieces):
    if grid.size != 4:
        return pieces
    return lax.psum_scatter(
        pieces, "tensor", scatter_dimension=0, axis_index_groups=ROWS_OF_CHIPS, tiled=False
    )


def return_hidden(grid, pieces):
    if grid.size == 4:
        return lax.ppermute(pieces, ("dp", "tensor"), owner_pairs(grid, True))
    core = lax.axis_index("dp") % CORES
    me = lax.axis_index("tensor")
    zero = jnp.zeros_like(pieces)
    row = jnp.stack([jnp.where(core == c, pieces, zero) for c in range(CORES)], axis=1)
    row = row.reshape(grid.size, *pieces.shape[1:])
    wide = jnp.stack([jnp.where(me % 2 == parity, row, jnp.zeros_like(row)) for parity in range(2)])
    mine = lax.psum_scatter(wide, "tensor", scatter_dimension=1, tiled=False)
    other = grid.over_core(jnp.where(core == 0, mine[1], mine[0]))
    total = jnp.where(core == 0, mine[0], mine[1]).astype(F32) + other.astype(F32)
    return total.astype(BF16)


class Gather:
    def __init__(self, grid, value):
        self.grid = grid
        if grid.size != 4:
            self.pieces = [lax.all_gather(value, "tensor", axis=0, tiled=True)]
            self.devices = [jnp.int32(0)]
            return
        me = lax.axis_index("tensor")
        self.pieces = [value, grid.over_tensor(value, 1), grid.over_tensor(value, 2)]
        self.devices = [jnp.bitwise_xor(me, other) for other in range(4)]

    def ready(self):
        return self.pieces[1:3]

    def joined(self):
        if self.grid.size != 4:
            return self.pieces[0]
        rows, width = self.pieces[0].shape
        out = jnp.zeros((4 * rows, width), self.pieces[0].dtype)
        for piece, device in zip(self.pieces, self.devices):
            out = lax.dynamic_update_slice(out, piece, (device * rows, 0))
        return out

    def finish(self, *others, over=1):
        if self.grid.size == 4:
            self.pieces.append(self.grid.over_tensor(after(self.pieces[3 - over], *others), over))
        return self.pieces


def gather_rows(grid, value):
    if grid.size != 4:
        return lax.all_gather(value, "tensor", axis=0, tiled=True), [], []
    rows, width = value.shape
    half = rows // 2
    first, second = value[:half], value[half:]
    first_x = grid.over_tensor(first, 1)
    second_y = grid.over_tensor(second, 2)
    first_y = grid.over_tensor(first, 2)
    second_x = grid.over_tensor(second, 1)
    first_xy = grid.over_tensor(first_x, 2)
    second_xy = grid.over_tensor(second_y, 1)
    me = lax.axis_index("tensor")
    out = jnp.zeros((4 * rows, width), value.dtype)
    out = lax.dynamic_update_slice(out, value, (me * rows, 0))
    for other, top, bottom in ((1, first_x, second_x), (2, first_y, second_y), (3, first_xy, second_xy)):
        place = jnp.bitwise_xor(me, other) * rows
        out = lax.dynamic_update_slice(out, top, (place, 0))
        out = lax.dynamic_update_slice(out, bottom, (place + half, 0))
    return out, [first_x, second_y], [first_xy, second_xy]


def scatter_rows(grid, term, beside):
    size, rows, width = term.shape
    if size != 4:
        total = lax.psum_scatter(term.astype(BF16), "tensor", scatter_dimension=0, tiled=False)
        return total.astype(F32), [], beside
    me = lax.axis_index("tensor")
    half = width // 2

    def pick(other, low):
        place = jnp.bitwise_xor(me, other)
        return lax.dynamic_slice(term, (place, 0, low), (1, rows, half))[0]

    halves = ((0, 1, 2), (half, 2, 1))
    got_far = [grid.over_tensor(pick(3, low).astype(BF16), near) for low, near, far in halves]
    got_own = [grid.over_tensor(pick(near, low).astype(BF16), near) for low, near, far in halves]
    first, second, *beside = together(*got_far, *beside)
    totals, arrived = [], []
    for (low, near, far), far_term, own_term in zip(halves, (first, second), got_own):
        onward = pick(far, low).astype(F32) + far_term.astype(F32)
        got = grid.over_tensor(onward.astype(BF16), far)
        arrived.append(got)
        totals.append(pick(0, low).astype(F32) + own_term.astype(F32) + got.astype(F32))
    return jnp.concatenate(totals, axis=1), arrived, beside


def body(
    tokens,
    lengths,
    routes,
    fill_order,
    norm_gain,
    norm_bias,
    qkv_weight,
    out_weight,
    centroids,
    expert_in,
    expert_out,
    cotangent,
):
    tok_count, model_width = tokens.shape
    seq_count = lengths.shape[0]
    seq_len = tok_count // seq_count
    heads_here = qkv_weight.shape[1]
    head_size = out_weight.shape[1]
    experts = lax.axis_size("dp")
    shards = lax.axis_size("tensor")
    grid = Grid(shards, experts)
    me = lax.axis_index("tensor")
    parity, part = me % 2, me // 2
    core = lax.axis_index("dp") % CORES
    depth = experts // CORES
    row_parts = shards // 2
    capacity = (9 * tok_count + 8 * experts - 1) // (8 * experts)
    share = 16 * -(-capacity // (16 * row_parts))
    padded = share * row_parts
    own_rows = depth * share
    tok_rows = tok_count // shards

    near = [fetch_near(grid, w[0, k]) for k in range(2) for w in (expert_in, expert_out)]
    out_flat = out_weight.reshape(heads_here * head_size, model_width)
    out_gather = Gather(grid, out_flat)
    out_gather.finish(over=2)
    out_all = out_gather.joined()
    centroid = jnp.where(parity == core, centroids[0], grid.over_core(centroids[0]))

    slots = token_slots(
        routes, fill_order, lengths, seq_len, capacity, padded, experts * padded
    )
    slot = slots.reshape(tok_count, 1)
    rank = slot % padded
    slot_device = (rank // share) * 2 + (slot // padded) % 2
    slot_place = (slot_device * depth + slot // (2 * padded)) * share + rank % share
    place = jnp.where(slot < experts * padded, slot_place, -1)
    own_first = (parity * padded + part * share).astype(jnp.int32).reshape(1)

    def to_experts(rows):
        picked = pick_rows(rows, slots, own_first, depth, share, CORES, padded)
        return grid.exchange_depth(picked.reshape(depth, share, model_width)).reshape(own_rows, model_width)

    def leave_experts(rows):
        return grid.exchange_depth(rows.reshape(depth, share, model_width))

    def row_starts(gathered):
        return jnp.stack([device * own_rows for device in gathered.devices]).astype(jnp.int32)

    grad_ret = to_experts(cotangent).astype(F32)
    heads = heads_here + heads_here % 2
    fused = qkv_weight.reshape(model_width, heads_here, 3, head_size)
    fused = jnp.swapaxes(fused, 1, 2)
    fused = jnp.pad(fused, ((0, 0), (0, 0), (0, heads - heads_here), (0, 0)))
    fused = fused.reshape(model_width, 3 * heads * head_size)
    inner = heads_here * head_size
    ln_in, projected = norm_project(tokens, norm_gain, norm_bias, fused)
    near[0] = after(near[0], projected)
    attended, log_total = attend(projected, lengths, seq_count, heads, head_size)
    near[1:] = [after(piece, attended) for piece in near[1:]]
    win, wout = [fetch_hidden(grid, w) for w in near[::2]], [fetch_hidden(grid, w) for w in near[1::2]]
    if shards == 4:
        gathered = Gather(grid, attended)
        pieces = gathered.finish()
        first = jnp.stack(gathered.devices).astype(jnp.int32)
    else:
        every = lax.all_gather(attended[:, :inner], "tensor", axis=1, tiled=True)
        pieces, first = [every], jnp.zeros((1,), jnp.int32)
    sent = out_project(pieces, first, out_all, tokens)

    expert_rows = to_experts(sent)
    gate = jax.nn.sigmoid(jnp.dot(expert_rows, centroid, preferred_element_type=F32))[:, None]
    current = expert_rows.astype(F32)
    saved = []
    for k in range(2):
        here = current.astype(BF16)
        there = grid.over_core(here)
        act, slope, total = expert_forward(here, win[k], wout[k], current)
        act_there, slope_there, part = expert_forward(there, win[k], wout[k])
        current = total + grid.over_core(part).astype(F32)
        saved.append(([here, there], [act, act_there], [slope, slope_there]))
    returned = leave_experts((gate * current).astype(BF16))

    grad_gate = jnp.sum(grad_ret * current, axis=1, keepdims=True)
    grad_logit = grad_gate * gate * (1.0 - gate)
    grad_current = gate * grad_ret
    branches = [None, None]
    for k in (1, 0):
        slopes = saved[k][2]
        here = grad_current.astype(BF16)
        there = grid.over_core(here)
        grad_pre_there, part = expert_backward(there, slopes[1], win[k], wout[k])
        grad_pre, total = expert_backward(here, slopes[0], win[k], wout[k], grad_current)
        grad_current = total + grid.over_core(part).astype(F32)
        branches[k] = ([here, there], [grad_pre, grad_pre_there])
    grad_rows = (grad_current + grad_logit * centroid.astype(F32)[None, :]).astype(BF16)
    centroid_part = jnp.sum(grad_logit * expert_rows.astype(F32), axis=0, keepdims=True)
    centroid_parts = grid.sum_tensor(
        jnp.concatenate([jnp.where(parity == p, centroid_part, 0.0) for p in range(2)], axis=0)
    )
    centroid_other = grid.over_core(centroid_parts)
    grad_centroid = lax.dynamic_slice_in_dim(centroid_parts + centroid_other, core, 1, 0)

    moved = leave_experts(grad_rows)
    outers = []
    for k in (1, 0):
        rows_in, acts, unused = saved[k]
        branch, grad_pres = branches[k]
        blocks = win[k].shape[0]
        outers += [outer(rows_in, grad_pres, blocks), outer(acts, branch, blocks)]
    sums_in2, sums_back2 = [sum_hidden(grid, pieces) for pieces in outers[:2]]
    moved = after(moved, *outers, centroid_other)
    grad_gather = Gather(grid, moved.reshape(own_rows, model_width))
    sums_in1, sums_back1 = [
        sum_hidden(grid, after(pieces, *grad_gather.ready())) for pieces in outers[2:]
    ]
    pieces = grad_gather.finish()
    first = row_starts(grad_gather)
    out_padded = jnp.pad(out_flat, ((0, heads * head_size - inner), (0, 0)))
    grad_mixed, grad_attended = combine(pieces, first, place, cotangent, out_padded)
    back_in2 = return_hidden(grid, after(sums_in2, *pieces[1:]))
    back_out2 = return_hidden(grid, after(sums_back2, *pieces[1:]))
    out_gather = Gather(grid, after(returned, *pieces[1:]).reshape(own_rows, model_width))
    grad_projected = attend_back(
        projected,
        attended,
        grad_attended,
        log_total,
        lengths,
        seq_count,
        heads,
        head_size,
    )
    grad_ln_part = dot(grad_projected, fused, ((1,), (1,))).astype(BF16)
    grad_ln_part, grad_mixed, grad_projected = together(
        grad_ln_part, grad_mixed, grad_projected, back_in2, back_out2, sums_in1, sums_back1, *out_gather.ready()
    )[:3]
    grad_out_local = dot(attended[:, :inner], grad_mixed, ((0,), (0,))).reshape(
        heads_here, head_size, model_width
    )
    grad_qkv_local = dot(ln_in, grad_projected, ((0,), (0,)))
    grad_sums = (grad_qkv_local.astype(BF16), grad_out_local.astype(BF16))
    grad_ln, scattered, grad_sums = scatter_rows(
        grid, grad_ln_part.reshape(shards, tok_rows, model_width), grad_sums
    )
    grad_sums = lax.psum(grad_sums, "dp")
    scattered = scattered + [grad_projected]
    out_pieces = out_gather.finish(*scattered, over=2)

    def own(rows):
        return lax.dynamic_slice_in_dim(rows, me * tok_rows, tok_rows, 0)

    own_tokens = own(tokens).astype(F32)
    centre = own_tokens - jnp.mean(own_tokens, axis=1, keepdims=True)
    own_scale = lax.rsqrt(jnp.mean(centre * centre, axis=1, keepdims=True) + EPSILON)
    own_normed = centre * own_scale
    grad_normed = grad_ln * norm_gain
    mean_plain = jnp.mean(grad_normed, axis=1, keepdims=True)
    mean_cross = jnp.mean(grad_normed * own_normed, axis=1, keepdims=True)
    grad_input = own(grad_mixed).astype(F32) + own_scale * (
        grad_normed - mean_plain - own_normed * mean_cross
    )
    grad_tokens, halfway, gathered = gather_rows(grid, grad_input.astype(BF16))
    output = combine(out_pieces, first, place, after(sent, *scattered))[0]
    norm_total = jnp.stack([jnp.sum(grad_ln * own_normed, axis=0), jnp.sum(grad_ln, axis=0)])
    norm_total = grid.sum_tensor(after(norm_total, *halfway))
    back_in1 = return_hidden(grid, after(sums_in1, *halfway))
    back_out1 = return_hidden(grid, after(sums_back1, *halfway))
    norm_total = grid.sum_dp(after(norm_total, output))
    norm_total = lax.dynamic_slice_in_dim(
        norm_total, me * (model_width // shards), model_width // shards, 1
    )
    grad_qkv, grad_out_weight = [after(total, *gathered) for total in grad_sums]
    grad_qkv = grad_qkv.astype(F32).reshape(model_width, 3, heads, head_size)[:, :, :heads_here]
    grad_qkv_weight = jnp.swapaxes(grad_qkv, 1, 2).reshape(model_width, heads_here, 3 * head_size)
    return (
        output,
        grad_tokens,
        norm_total[0],
        norm_total[1],
        grad_qkv_weight,
        grad_out_weight.astype(F32),
        grad_centroid,
        jnp.stack([back_in1, back_in2])[None].astype(F32),
        jnp.stack([back_out1, back_out2])[None].astype(F32),
    )


def solution(mesh):
    return jax.shard_map(
        body,
        mesh=mesh,
        in_specs=(
            P("dp", None),
            P("dp"),
            P("dp", None),
            P("dp", None),
            P(),
            P(),
            P(None, "tensor", None),
            P("tensor", None, None),
            P("dp", None),
            P("dp", None, None, "tensor"),
            P("dp", None, "tensor", None),
            P("dp", None),
        ),
        out_specs=(
            P("dp", None),
            P("dp", None),
            P("tensor"),
            P("tensor"),
            P(None, "tensor", None),
            P("tensor", None, None),
            P("dp", None),
            P("dp", None, None, "tensor"),
            P("dp", None, "tensor", None),
        ),
        check_vma=False,
    )
```

```python
import functools
import math

import jax
import jax.numpy as jnp
from jax import lax
from jax.experimental import pallas as pl
from jax.experimental.pallas import tpu as pltpu
from jax.sharding import PartitionSpec as P

EPSILON = 1e-05
MASKED = -1e30
F32 = jnp.float32
BF16 = jnp.bfloat16
CORES = 2


def after(value, *others):
    return lax.optimization_barrier((value, *others))[0]


def together(*values):
    return lax.optimization_barrier(values)


def dot(a, b, contract):
    return lax.dot_general(a, b, (contract, ((), ())), preferred_element_type=F32)


def norm_project_kernel(x_ref, gain_ref, bias_ref, w_ref, ln_ref, out_ref):
    x = x_ref[...].astype(F32)
    centre = x - jnp.mean(x, axis=1, keepdims=True)
    scale = lax.rsqrt(jnp.mean(centre * centre, axis=1, keepdims=True) + EPSILON)
    ln = (centre * scale * gain_ref[...] + bias_ref[...]).astype(BF16)
    ln_ref[...] = ln
    out_ref[...] = dot(ln, w_ref[...], ((1,), (0,))).astype(BF16)


def norm_project(tokens, gain, bias, weight):
    rows, width = tokens.shape
    columns = weight.shape[1]
    tile = 512
    return pl.pallas_call(
        norm_project_kernel,
        grid=(rows // tile,),
        in_specs=[
            pl.BlockSpec((tile, width), lambda i: (i, 0)),
            pl.BlockSpec((1, width), lambda i: (0, 0)),
            pl.BlockSpec((1, width), lambda i: (0, 0)),
            pl.BlockSpec((width, columns), lambda i: (0, 0)),
        ],
        out_specs=[
            pl.BlockSpec((tile, width), lambda i: (i, 0)),
            pl.BlockSpec((tile, columns), lambda i: (i, 0)),
        ],
        out_shape=[
            jax.ShapeDtypeStruct((rows, width), BF16),
            jax.ShapeDtypeStruct((rows, columns), BF16),
        ],
        compiler_params=pltpu.CompilerParams(vmem_limit_bytes=40 << 20),
        cost_estimate=pl.CostEstimate(
            flops=2 * rows * width * columns,
            bytes_accessed=2 * (2 * rows * width + rows * columns + width * columns),
            transcendentals=rows,
        ),
    )(tokens, gain[None], bias[None], weight)


def attend_kernel(head_size, group, tile, len_ref, q_ref, k_ref, v_ref, o_ref, lse_ref):
    seq_len, lanes = q_ref.shape
    scale = head_size**-0.5
    limit = len_ref[pl.program_id(0)]
    keys = k_ref[...]
    values = v_ref[...]
    key_place = lax.broadcasted_iota(jnp.int32, (seq_len, lanes), 0)
    lane = lax.broadcasted_iota(jnp.int32, (seq_len, lanes), 1)
    causal = lax.broadcasted_iota(jnp.int32, (tile, tile), 0) <= lax.broadcasted_iota(
        jnp.int32, (tile, tile), 1
    )
    tall = lax.broadcasted_iota(jnp.int32, (lanes, tile), 0)
    lane_q = lax.broadcasted_iota(jnp.int32, (tile, lanes), 1)
    heads = []
    for a in range(group):
        mine = (lane >= a * head_size) & (lane < (a + 1) * head_size)
        spare = ((a + 1) % group) * head_size
        extra = jnp.where((lane == spare) & (key_place >= limit), MASKED, 0.0).astype(BF16)
        k_a = jnp.where(mine, keys, extra)
        v_a = jnp.where(mine, values, jnp.ones((), BF16))
        heads.append((k_a, v_a, spare))
    for i in range(seq_len // tile):
        end = (i + 1) * tile
        q = (q_ref[i * tile : end, :].astype(F32) * scale).astype(BF16)
        out = None
        for a in range(group):
            k_a, v_a, spare = heads[a]
            mine_q = (lane_q >= a * head_size) & (lane_q < (a + 1) * head_size)
            q_a = jnp.where(mine_q, q, jnp.where(lane_q == spare, 1.0, 0.0).astype(BF16))
            last = jnp.where(causal, dot(k_a[i * tile : end], q_a, ((1,), (1,))), MASKED)
            top = jnp.max(last, axis=0, keepdims=True)
            if i:
                scores = dot(k_a[: i * tile], q_a, ((1,), (1,)))
                top = jnp.maximum(top, jnp.max(scores, axis=0, keepdims=True))
            result = dot(v_a[i * tile : end], jnp.exp(last - top).astype(BF16), ((0,), (0,)))
            if i:
                result += dot(v_a[: i * tile], jnp.exp(scores - top).astype(BF16), ((0,), (0,)))
            total = result[spare : spare + 1, :]
            lse_ref[0, 0, a : a + 1, i * tile : end] = top + jnp.log(total)
            result = result / total
            if out is None:
                out = result
            else:
                out = jnp.where((tall >= a * head_size) & (tall < (a + 1) * head_size), result, out)
        o_ref[i * tile : end, :] = out.T.astype(BF16)


def attend(projected, lengths, seqs, heads, head_size):
    rows = projected.shape[0]
    seq_len = rows // seqs
    group = 2
    lanes = group * head_size
    groups = heads // group
    tile = 256
    return pl.pallas_call(
        functools.partial(attend_kernel, head_size, group, tile),
        grid_spec=pltpu.PrefetchScalarGridSpec(
            num_scalar_prefetch=1,
            grid=(seqs, groups),
            in_specs=[
                pl.BlockSpec((seq_len, lanes), lambda s, g, n: (s, g)),
                pl.BlockSpec((seq_len, lanes), lambda s, g, n: (s, groups + g)),
                pl.BlockSpec((seq_len, lanes), lambda s, g, n: (s, 2 * groups + g)),
            ],
            out_specs=[
                pl.BlockSpec((seq_len, lanes), lambda s, g, n: (s, g)),
                pl.BlockSpec((1, 1, group, seq_len), lambda s, g, n: (s, g, 0, 0)),
            ],
        ),
        out_shape=[
            jax.ShapeDtypeStruct((rows, heads * head_size), BF16),
            jax.ShapeDtypeStruct((seqs, groups, group, seq_len), F32),
        ],
        compiler_params=pltpu.CompilerParams(vmem_limit_bytes=40 << 20),
        cost_estimate=pl.CostEstimate(
            flops=4 * rows * seq_len * heads * head_size,
            bytes_accessed=8 * rows * heads * head_size,
            transcendentals=rows * seq_len * heads // 2,
        ),
    )(lengths, projected, projected, projected)


def attend_back_kernel(head_size, group, tile, len_ref, q_ref, k_ref, v_ref, o_ref, do_ref, lse_ref, out_ref, dk_acc, dv_acc):
    seq_len, lanes = q_ref.shape
    scale = head_size**-0.5
    limit = len_ref[pl.program_id(0)]
    keys = k_ref[...]
    values = v_ref[...]
    zero = jnp.zeros((), BF16)

    def place(kind):
        block = kind * pl.num_programs(1) + pl.program_id(1)
        return pl.ds(pl.multiple_of(block * lanes, lanes), lanes)

    key_place = lax.broadcasted_iota(jnp.int32, (seq_len, lanes), 0)
    lane = lax.broadcasted_iota(jnp.int32, (seq_len, lanes), 1)
    causal = lax.broadcasted_iota(jnp.int32, (tile, tile), 0) <= lax.broadcasted_iota(
        jnp.int32, (tile, tile), 1
    )
    lane_q = lax.broadcasted_iota(jnp.int32, (tile, lanes), 1)
    heads = []
    for a in range(group):
        mine = (lane >= a * head_size) & (lane < (a + 1) * head_size)
        spare = ((a + 1) % group) * head_size
        extra = jnp.where((lane == spare) & (key_place >= limit), MASKED, 0.0).astype(BF16)
        k_a = jnp.where(mine, keys, extra)
        ones = jnp.where((lane == spare) | (lane == spare + 1), 1.0, 0.0).astype(BF16)
        v_a = jnp.where(mine, values, ones)
        heads.append((k_a, v_a, spare))
    steps = seq_len // tile
    for i in reversed(range(steps)):
        end = (i + 1) * tile
        q = (q_ref[i * tile : end, :].astype(F32) * scale).astype(BF16)
        do = do_ref[i * tile : end, :]
        product = do.astype(F32) * o_ref[i * tile : end, :].astype(F32)
        dq = None
        dk = None
        dv = None
        for a in range(group):
            k_a, v_a, spare = heads[a]
            mine_q = (lane_q >= a * head_size) & (lane_q < (a + 1) * head_size)
            q_m = jnp.where(mine_q, q, zero)
            q_a = jnp.where(mine_q, q, jnp.where(lane_q == spare, 1.0, 0.0).astype(BF16))
            delta = -jnp.sum(jnp.where(mine_q, product, 0.0), axis=1, keepdims=True)
            high = delta.astype(BF16)
            low = (delta - high.astype(F32)).astype(BF16)
            do_m = jnp.where(mine_q, do, zero)
            do_a = jnp.where(lane_q == spare, high, jnp.where(lane_q == spare + 1, low, do_m))
            scores = dot(k_a[:end], q_a, ((1,), (1,)))
            last = jnp.where(causal, scores[i * tile :], MASKED)
            scores = jnp.concatenate([scores[: i * tile], last], axis=0) if i else last
            probs = jnp.exp(scores - lse_ref[0, 0, a : a + 1, i * tile : end])
            grad = dot(v_a[:end], do_a, ((1,), (1,)))
            grad = (probs * grad).astype(BF16)
            term_v = dot(probs.astype(BF16), do_m, ((1,), (0,)))
            term_k = dot(grad, q_m, ((1,), (0,)))
            term_q = dot(k_a[:end], grad, ((0,), (0,)))
            dv = term_v if dv is None else dv + term_v
            dk = term_k if dk is None else dk + term_k
            if dq is None:
                dq = term_q
            else:
                tall = lax.broadcasted_iota(jnp.int32, (lanes, tile), 0)
                dq = jnp.where((tall >= a * head_size) & (tall < (a + 1) * head_size), term_q, dq)
        out_ref[i * tile : end, place(0)] = (dq.T * scale).astype(BF16)
        if i == steps - 1:
            dk_acc[...] = dk
            dv_acc[...] = dv
        else:
            dk_acc[:end, :] += dk
            dv_acc[:end, :] += dv
    out_ref[:, place(1)] = dk_acc[...].astype(BF16)
    out_ref[:, place(2)] = dv_acc[...].astype(BF16)


def attend_back(projected, attended, grad_attended, lse, lengths, seqs, heads, head_size):
    rows = projected.shape[0]
    seq_len = rows // seqs
    group = 2
    lanes = group * head_size
    groups = heads // group
    tile = 256
    spec = pl.BlockSpec((seq_len, lanes), lambda s, g, n: (s, g))
    return pl.pallas_call(
        functools.partial(attend_back_kernel, head_size, group, tile),
        grid_spec=pltpu.PrefetchScalarGridSpec(
            num_scalar_prefetch=1,
            grid=(seqs, groups),
            in_specs=[
                spec,
                pl.BlockSpec((seq_len, lanes), lambda s, g, n: (s, groups + g)),
                pl.BlockSpec((seq_len, lanes), lambda s, g, n: (s, 2 * groups + g)),
                spec,
                spec,
                pl.BlockSpec((1, 1, group, seq_len), lambda s, g, n: (s, g, 0, 0)),
            ],
            out_specs=pl.BlockSpec((seq_len, 3 * groups * lanes), lambda s, g, n: (s, 0)),
            scratch_shapes=[pltpu.VMEM((seq_len, lanes), F32), pltpu.VMEM((seq_len, lanes), F32)],
        ),
        out_shape=jax.ShapeDtypeStruct((rows, 3 * heads * head_size), BF16),
        compiler_params=pltpu.CompilerParams(vmem_limit_bytes=48 << 20),
        cost_estimate=pl.CostEstimate(
            flops=10 * rows * seq_len * heads * head_size,
            bytes_accessed=16 * rows * heads * head_size,
            transcendentals=rows * seq_len * heads // 2,
        ),
    )(lengths, projected, projected, projected, attended, grad_attended, lse)


def place_kernel(order_ref, out_ref):
    count = out_ref.shape[1]
    tile = order_ref.shape[0]
    step = pl.program_id(0)
    token = lax.broadcasted_iota(jnp.int32, (tile, count), 1)
    index = lax.broadcasted_iota(jnp.int32, (tile, 1), 0) + step * tile
    hit = jnp.sum(jnp.where(order_ref[...] == token, index, 0), axis=0, keepdims=True)

    @pl.when(step == 0)
    def _():
        out_ref[...] = hit

    @pl.when(step > 0)
    def _():
        out_ref[...] += hit


def rank_kernel(key_ref, keys_ref, out_ref):
    step = pl.program_id(0)
    keys = keys_ref[...]
    base = jnp.bitwise_and(keys, -4096)
    key = key_ref[...]
    hit = jnp.sum(jnp.where((key < keys) & (key >= base), 1, 0), axis=0, keepdims=True)

    @pl.when(step == 0)
    def _():
        out_ref[...] = hit

    @pl.when(step > 0)
    def _():
        out_ref[...] += hit


def tall_reduce(kernel, column, rows, count):
    tile = 512
    specs = [pl.BlockSpec((tile, 1), lambda i: (i, 0))]
    specs += [pl.BlockSpec((1, count), lambda i: (0, 0)) for _ in rows]
    return pl.pallas_call(
        kernel,
        grid=(count // tile,),
        in_specs=specs,
        out_specs=pl.BlockSpec((1, count), lambda i: (0, 0)),
        out_shape=jax.ShapeDtypeStruct((1, count), jnp.int32),
        cost_estimate=pl.CostEstimate(
            flops=4 * count * count, bytes_accessed=600 * count, transcendentals=0
        ),
    )(column, *rows)


def token_slots(routes, order, lengths, seq_len, capacity, padded, none):
    count = routes.shape[0]
    places = jnp.arange(count, dtype=jnp.int32)[None]
    limits = jnp.repeat(lengths, seq_len, total_repeat_length=count)[None]
    valid = places % seq_len < limits
    turn = tall_reduce(place_kernel, order.reshape(count, 1), [], count)
    route = routes.reshape(1, count)
    keys = jnp.where(valid, route * 4096 + turn, 1 << 20)
    rank = tall_reduce(rank_kernel, keys.reshape(count, 1), [keys], count)
    return jnp.where(valid & (rank < capacity), route * padded + rank, none)


def pick_kernel(share, experts_step, padded, first_ref, slots_ref, rows_ref, out_ref):
    step = pl.program_id(0)
    start = first_ref[0] + step * experts_step * padded
    count = rows_ref.shape[0]
    slot = lax.broadcasted_iota(jnp.int32, (share, count), 0) + start
    chosen = jnp.where(slots_ref[...] == slot, 1.0, 0.0).astype(BF16)
    out_ref[...] = dot(chosen, rows_ref[...], ((1,), (0,))).astype(BF16)


def pick_rows(rows, slots, first, blocks, share, step, padded):
    count, width = rows.shape
    return pl.pallas_call(
        functools.partial(pick_kernel, share, step, padded),
        grid_spec=pltpu.PrefetchScalarGridSpec(
            num_scalar_prefetch=1,
            grid=(blocks,),
            in_specs=[
                pl.BlockSpec((1, count), lambda i, n: (0, 0)),
                pl.BlockSpec((count, width), lambda i, n: (0, 0)),
            ],
            out_specs=pl.BlockSpec((share, width), lambda i, n: (i, 0)),
        ),
        out_shape=jax.ShapeDtypeStruct((blocks * share, width), BF16),
        compiler_params=pltpu.CompilerParams(vmem_limit_bytes=40 << 20),
        cost_estimate=pl.CostEstimate(
            flops=2 * blocks * share * count * width,
            bytes_accessed=2 * (count + blocks * share) * width,
            transcendentals=0,
        ),
    )(first, slots, rows)


def out_project_kernel(count, first_ref, *refs):
    piece_refs, w_ref, x_ref, out_ref, wide = refs[:count], *refs[count:]
    for i, piece in enumerate(piece_refs):
        width = piece.shape[1]
        start = pl.multiple_of(first_ref[i] * width, width)
        wide[:, pl.ds(start, width)] = piece[...]
    out_ref[...] = (x_ref[...].astype(F32) + dot(wide[...], w_ref[...], ((1,), (0,)))).astype(BF16)


def out_project(pieces, first, weight, tokens):
    rows, width = tokens.shape
    inner = weight.shape[0]
    count = len(pieces)
    tile = 512
    return pl.pallas_call(
        functools.partial(out_project_kernel, count),
        grid_spec=pltpu.PrefetchScalarGridSpec(
            num_scalar_prefetch=1,
            grid=(rows // tile,),
            in_specs=[pl.BlockSpec((tile, p.shape[1]), lambda i, n: (i, 0)) for p in pieces]
            + [
                pl.BlockSpec((inner, width), lambda i, n: (0, 0)),
                pl.BlockSpec((tile, width), lambda i, n: (i, 0)),
            ],
            out_specs=pl.BlockSpec((tile, width), lambda i, n: (i, 0)),
            scratch_shapes=[pltpu.VMEM((tile, inner), BF16)],
        ),
        out_shape=jax.ShapeDtypeStruct((rows, width), BF16),
        compiler_params=pltpu.CompilerParams(vmem_limit_bytes=40 << 20),
        cost_estimate=pl.CostEstimate(
            flops=2 * rows * width * inner,
            bytes_accessed=2 * (3 * rows * width + inner * width),
            transcendentals=0,
        ),
    )(first, *pieces, weight, tokens)


def spread(count, first_ref, place_ref, piece_refs):
    place = place_ref[...]
    total = None
    for i in range(count):
        rows = piece_refs[i].shape[0]
        index = lax.broadcasted_iota(jnp.int32, (place.shape[0], rows), 1) + first_ref[i]
        chosen = jnp.where(place == index, 1.0, 0.0).astype(BF16)
        term = dot(chosen, piece_refs[i][...], ((1,), (0,)))
        total = term if total is None else total + term
    return total


def combine_kernel(count, first_ref, place_ref, base_ref, *refs):
    total = spread(count, first_ref, place_ref, refs[:count])
    refs[count][...] = (base_ref[...].astype(F32) + total).astype(BF16)


def combine_project_kernel(count, first_ref, place_ref, base_ref, *refs):
    total = spread(count, first_ref, place_ref, refs[:count])
    w_ref, out_ref, back_ref = refs[count:]
    out = (base_ref[...].astype(F32) + total).astype(BF16)
    out_ref[...] = out
    back_ref[...] = dot(out, w_ref[...], ((1,), (1,))).astype(BF16)


def combine(pieces, first, place, base, weight=None):
    rows, width = base.shape
    count = len(pieces)
    tile = 512
    block = pl.BlockSpec((tile, width), lambda i, n: (i, 0))
    in_specs = [pl.BlockSpec((tile, 1), lambda i, n: (i, 0)), block]
    in_specs += [pl.BlockSpec(p.shape, lambda i, n: (0, 0), pipeline_mode=pl.Buffered(1)) for p in pieces]
    args = [place, base, *pieces]
    out_specs, out_shape = [block], [jax.ShapeDtypeStruct((rows, width), BF16)]
    kernel = combine_kernel
    table = sum(p.shape[0] for p in pieces)
    flops = 2 * rows * width * table
    if weight is not None:
        inner = weight.shape[0]
        in_specs.append(pl.BlockSpec((inner, width), lambda i, n: (0, 0)))
        args.append(weight)
        out_specs.append(pl.BlockSpec((tile, inner), lambda i, n: (i, 0)))
        out_shape.append(jax.ShapeDtypeStruct((rows, inner), BF16))
        kernel = combine_project_kernel
        flops += 2 * rows * width * inner
    return pl.pallas_call(
        functools.partial(kernel, count),
        grid_spec=pltpu.PrefetchScalarGridSpec(
            num_scalar_prefetch=1, grid=(rows // tile,), in_specs=in_specs, out_specs=out_specs
        ),
        out_shape=out_shape,
        compiler_params=pltpu.CompilerParams(vmem_limit_bytes=48 << 20),
        cost_estimate=pl.CostEstimate(
            flops=flops, bytes_accessed=2 * (2 * rows + table) * width, transcendentals=0
        ),
    )(first, *args)


def gelu_pair(pre):
    cdf = 0.5 + 0.5 * lax.erf(pre * (2.0**-0.5))
    density = jnp.exp(-0.5 * pre * pre) * ((2.0 * math.pi) ** -0.5)
    return (pre * cdf).astype(BF16), (cdf + pre * density).astype(BF16)


def without_base(kernel, count):
    def wrapped(*refs):
        kernel(*refs[:count], None, *refs[count:])

    return wrapped


def expert_forward_kernel(count, x_ref, base_ref, *refs):
    w_in, w_out = refs[:count], refs[count : 2 * count]
    act_ref, slope_ref, out_ref = refs[2 * count :]
    x = x_ref[...]
    total = base_ref[...] if base_ref is not None else None
    width = w_in[0].shape[1]
    chunk = min(width, 1024)
    blocks = [(i, c) for i in range(count) for c in range(0, width, chunk)]

    def into(i, c):
        return dot(x, w_in[i][:, c : c + chunk], ((1,), (0,)))

    ahead = into(*blocks[0])
    for n, (i, c) in enumerate(blocks):
        pre = ahead
        if n + 1 < len(blocks):
            ahead = into(*blocks[n + 1])
        act, slope = gelu_pair(pre)
        act_ref[:, i * width + c : i * width + c + chunk] = act
        slope_ref[:, i * width + c : i * width + c + chunk] = slope
        term = dot(act, w_out[i][c : c + chunk, :], ((1,), (0,)))
        total = term if total is None else total + term
    out_ref[...] = total.astype(out_ref.dtype)


def expert_forward(x, w_in, w_out, base=None):
    rows, width = x.shape
    count, unused, inner = w_in.shape
    hidden = count * inner
    tile = rows // 2

    def row(n):
        return pl.BlockSpec((tile, n), lambda i: (i, 0))

    specs = [row(width)]
    args = [x]
    kernel = functools.partial(expert_forward_kernel, count)
    if base is not None:
        specs.append(row(width))
        args.append(base)
    else:
        kernel = without_base(kernel, 1)
    specs += [
        pl.BlockSpec(
            (None, *w.shape[1:]), functools.partial(lambda j, i: (j, 0, 0), j), pipeline_mode=pl.Buffered(1)
        )
        for w in (w_in, w_out)
        for j in range(count)
    ]
    return pl.pallas_call(
        kernel,
        grid=(rows // tile,),
        in_specs=specs,
        out_specs=[row(hidden), row(hidden), row(width)],
        out_shape=[
            jax.ShapeDtypeStruct((rows, hidden), BF16),
            jax.ShapeDtypeStruct((rows, hidden), BF16),
            jax.ShapeDtypeStruct((rows, width), BF16 if base is None else F32),
        ],
        compiler_params=pltpu.CompilerParams(vmem_limit_bytes=48 << 20),
        cost_estimate=pl.CostEstimate(
            flops=4 * rows * width * hidden,
            bytes_accessed=4 * width * hidden + 4 * rows * hidden + 6 * rows * width,
            transcendentals=2 * rows * hidden,
        ),
    )(*args, *[w_in] * count, *[w_out] * count)


def expert_backward_kernel(count, g_ref, slope_ref, base_ref, *refs):
    w_in, w_out = refs[:count], refs[count : 2 * count]
    pre_ref, out_ref = refs[2 * count :]
    g = g_ref[...]
    total = base_ref[...] if base_ref is not None else None
    width = w_in[0].shape[1]
    chunk = min(width, 1024)
    blocks = [(i, c) for i in range(count) for c in range(0, width, chunk)]

    def into(i, c):
        return dot(g, w_out[i][c : c + chunk, :], ((1,), (1,)))

    ahead = into(*blocks[0])
    for n, (i, c) in enumerate(blocks):
        back = ahead
        if n + 1 < len(blocks):
            ahead = into(*blocks[n + 1])
        place = slice(i * width + c, i * width + c + chunk)
        pre = (back * slope_ref[:, place].astype(F32)).astype(BF16)
        pre_ref[:, place] = pre
        term = dot(pre, w_in[i][:, c : c + chunk], ((1,), (1,)))
        total = term if total is None else total + term
    out_ref[...] = total.astype(out_ref.dtype)


def expert_backward(g, slope, w_in, w_out, base=None):
    rows, width = g.shape
    count, unused, inner = w_in.shape
    hidden = slope.shape[1]
    tile = rows // 2

    def row(n):
        return pl.BlockSpec((tile, n), lambda i: (i, 0))

    specs = [row(width), row(hidden)]
    args = [g, slope]
    kernel = functools.partial(expert_backward_kernel, count)
    if base is not None:
        specs.append(row(width))
        args.append(base)
    else:
        kernel = without_base(kernel, 2)
    specs += [
        pl.BlockSpec(
            (None, *w.shape[1:]), functools.partial(lambda j, i: (j, 0, 0), j), pipeline_mode=pl.Buffered(1)
        )
        for w in (w_in, w_out)
        for j in range(count)
    ]
    return pl.pallas_call(
        kernel,
        grid=(rows // tile,),
        in_specs=specs,
        out_specs=[row(hidden), row(width)],
        out_shape=[
            jax.ShapeDtypeStruct((rows, hidden), BF16),
            jax.ShapeDtypeStruct((rows, width), BF16 if base is None else F32),
        ],
        compiler_params=pltpu.CompilerParams(vmem_limit_bytes=48 << 20),
        cost_estimate=pl.CostEstimate(
            flops=4 * rows * width * hidden,
            bytes_accessed=4 * width * hidden + 4 * rows * hidden + 6 * rows * width,
            transcendentals=0,
        ),
    )(*args, *[w_in] * count, *[w_out] * count)


def outer_kernel(count, *refs):
    lefts, rights, out_ref = refs[:count], refs[count : 2 * count], refs[-1]
    total = None
    for a, b in zip(lefts, rights):
        term = dot(a[...], b[...], ((0,), (0,)))
        total = term if total is None else total + term
    out_ref[...] = total.astype(out_ref.dtype)


def outer(lefts, rights, blocks):
    rows = lefts[0].shape[0]
    count = len(lefts)
    left_blocks = blocks if lefts[0].shape[1] > rights[0].shape[1] else 1
    right_blocks = blocks // left_blocks
    left_width = lefts[0].shape[1] // left_blocks
    right_width = rights[0].shape[1] // right_blocks
    tile = min(256, left_width)
    steps = left_width // tile
    if left_blocks > 1:
        left_spec = pl.BlockSpec((rows, tile), lambda j, i: (0, j * steps + i))
        right_spec = pl.BlockSpec((rows, right_width), lambda j, i: (0, 0))
    else:
        left_spec = pl.BlockSpec((rows, tile), lambda j, i: (0, i))
        right_spec = pl.BlockSpec((rows, right_width), lambda j, i: (0, j))
    return pl.pallas_call(
        functools.partial(outer_kernel, count),
        grid=(blocks, steps),
        in_specs=[left_spec] * count + [right_spec] * count,
        out_specs=pl.BlockSpec((None, tile, right_width), lambda j, i: (j, i, 0)),
        out_shape=jax.ShapeDtypeStruct((blocks, left_width, right_width), BF16),
        compiler_params=pltpu.CompilerParams(vmem_limit_bytes=48 << 20),
        cost_estimate=pl.CostEstimate(
            flops=2 * count * blocks * rows * left_width * right_width,
            bytes_accessed=2 * blocks * (count * rows * (left_width + right_width) + left_width * right_width),
            transcendentals=0,
        ),
    )(*lefts, *rights)


class Grid:
    def __init__(self, shards, experts):
        self.size = shards
        self.experts = experts
        self.depth = experts // CORES

    def over_core(self, value):
        return lax.ppermute(value, "dp", [(d, d ^ 1) for d in range(self.experts)])

    def over_tensor(self, value, other):
        return lax.ppermute(value, "tensor", [(t, t ^ other) for t in range(self.size)])

    def sum_tensor(self, value):
        step = 1
        while step < self.size:
            value = value + self.over_tensor(value, step)
            step *= 2
        return value

    def sum_dp(self, value):
        step = 1
        while step < self.experts:
            pairs = [(d, d ^ step) for d in range(self.experts)]
            value = value + lax.ppermute(value, "dp", pairs)
            step *= 2
        return value

    def exchange_depth(self, value):
        groups = [[CORES * z + c for z in range(self.depth)] for c in range(CORES)]
        return lax.all_to_all(
            value, "dp", split_axis=0, concat_axis=0, axis_index_groups=groups, tiled=True
        )


ROWS_OF_CHIPS = [[0, 2], [1, 3]]


def owner_pairs(grid, back=False):
    pairs = []
    for z in range(grid.depth):
        for core in range(CORES):
            for y in range(2):
                for x in range(2):
                    here = (CORES * z + core) * 4 + 2 * y + x
                    there = (CORES * z + 1 - x) * 4 + 2 * y + core
                    pairs.append((there, here) if back else (here, there))
    return pairs


def fetch_near(grid, weight):
    return lax.ppermute(weight, ("dp", "tensor"), owner_pairs(grid)) if grid.size == 4 else weight


def fetch_hidden(grid, weight):
    if grid.size == 4:
        return lax.all_gather(weight, "tensor", axis=0, axis_index_groups=ROWS_OF_CHIPS, tiled=False)
    core = lax.axis_index("dp") % CORES
    every = lax.all_gather(weight, "tensor", axis=0, tiled=False)
    chosen = jnp.where(lax.axis_index("tensor") % 2 == core, every, grid.over_core(every))
    chosen = chosen.reshape(grid.size // 2, 2, *weight.shape)
    return jnp.where(core == 0, chosen[:, 0], chosen[:, 1])


def sum_hidden(grid, pieces):
    if grid.size != 4:
        return pieces
    return lax.psum_scatter(
        pieces, "tensor", scatter_dimension=0, axis_index_groups=ROWS_OF_CHIPS, tiled=False
    )


def return_hidden(grid, pieces):
    if grid.size == 4:
        return lax.ppermute(pieces, ("dp", "tensor"), owner_pairs(grid, True))
    core = lax.axis_index("dp") % CORES
    me = lax.axis_index("tensor")
    zero = jnp.zeros_like(pieces)
    row = jnp.stack([jnp.where(core == c, pieces, zero) for c in range(CORES)], axis=1)
    row = row.reshape(grid.size, *pieces.shape[1:])
    wide = jnp.stack([jnp.where(me % 2 == parity, row, jnp.zeros_like(row)) for parity in range(2)])
    mine = lax.psum_scatter(wide, "tensor", scatter_dimension=1, tiled=False)
    other = grid.over_core(jnp.where(core == 0, mine[1], mine[0]))
    total = jnp.where(core == 0, mine[0], mine[1]).astype(F32) + other.astype(F32)
    return total.astype(BF16)


class Gather:
    def __init__(self, grid, value):
        self.grid = grid
        if grid.size != 4:
            self.pieces = [lax.all_gather(value, "tensor", axis=0, tiled=True)]
            self.devices = [jnp.int32(0)]
            return
        me = lax.axis_index("tensor")
        self.pieces = [value, grid.over_tensor(value, 1), grid.over_tensor(value, 2)]
        self.devices = [jnp.bitwise_xor(me, other) for other in range(4)]

    def ready(self):
        return self.pieces[1:3]

    def joined(self):
        if self.grid.size != 4:
            return self.pieces[0]
        rows, width = self.pieces[0].shape
        out = jnp.zeros((4 * rows, width), self.pieces[0].dtype)
        for piece, device in zip(self.pieces, self.devices):
            out = lax.dynamic_update_slice(out, piece, (device * rows, 0))
        return out

    def finish(self, *others, over=1):
        if self.grid.size == 4:
            self.pieces.append(self.grid.over_tensor(after(self.pieces[3 - over], *others), over))
        return self.pieces


def gather_rows(grid, value):
    if grid.size != 4:
        return lax.all_gather(value, "tensor", axis=0, tiled=True), [], []
    rows, width = value.shape
    half = rows // 2
    first, second = value[:half], value[half:]
    first_x = grid.over_tensor(first, 1)
    second_y = grid.over_tensor(second, 2)
    first_y = grid.over_tensor(first, 2)
    second_x = grid.over_tensor(second, 1)
    first_xy = grid.over_tensor(first_x, 2)
    second_xy = grid.over_tensor(second_y, 1)
    me = lax.axis_index("tensor")
    out = jnp.zeros((4 * rows, width), value.dtype)
    out = lax.dynamic_update_slice(out, value, (me * rows, 0))
    for other, top, bottom in ((1, first_x, second_x), (2, first_y, second_y), (3, first_xy, second_xy)):
        place = jnp.bitwise_xor(me, other) * rows
        out = lax.dynamic_update_slice(out, top, (place, 0))
        out = lax.dynamic_update_slice(out, bottom, (place + half, 0))
    return out, [first_x, second_y], [first_xy, second_xy]


def scatter_rows(grid, term, beside):
    size, rows, width = term.shape
    if size != 4:
        total = lax.psum_scatter(term.astype(BF16), "tensor", scatter_dimension=0, tiled=False)
        return total.astype(F32), [], beside
    me = lax.axis_index("tensor")
    half = width // 2

    def pick(other, low):
        place = jnp.bitwise_xor(me, other)
        return lax.dynamic_slice(term, (place, 0, low), (1, rows, half))[0]

    halves = ((0, 1, 2), (half, 2, 1))
    got_far = [grid.over_tensor(pick(3, low).astype(BF16), near) for low, near, far in halves]
    got_own = [grid.over_tensor(pick(near, low).astype(BF16), near) for low, near, far in halves]
    first, second, *beside = together(*got_far, *beside)
    totals, arrived = [], []
    for (low, near, far), far_term, own_term in zip(halves, (first, second), got_own):
        onward = pick(far, low).astype(F32) + far_term.astype(F32)
        got = grid.over_tensor(onward.astype(BF16), far)
        arrived.append(got)
        totals.append(pick(0, low).astype(F32) + own_term.astype(F32) + got.astype(F32))
    return jnp.concatenate(totals, axis=1), arrived, beside


def body(
    tokens,
    lengths,
    routes,
    fill_order,
    norm_gain,
    norm_bias,
    qkv_weight,
    out_weight,
    centroids,
    expert_in,
    expert_out,
    cotangent,
):
    tok_count, model_width = tokens.shape
    seq_count = lengths.shape[0]
    seq_len = tok_count // seq_count
    heads_here = qkv_weight.shape[1]
    head_size = out_weight.shape[1]
    experts = lax.axis_size("dp")
    shards = lax.axis_size("tensor")
    grid = Grid(shards, experts)
    me = lax.axis_index("tensor")
    parity, part = me % 2, me // 2
    core = lax.axis_index("dp") % CORES
    depth = experts // CORES
    row_parts = shards // 2
    capacity = (9 * tok_count + 8 * experts - 1) // (8 * experts)
    share = 16 * -(-capacity // (16 * row_parts))
    padded = share * row_parts
    own_rows = depth * share
    tok_rows = tok_count // shards

    near = [fetch_near(grid, w[0, k]) for k in range(2) for w in (expert_in, expert_out)]
    out_flat = out_weight.reshape(heads_here * head_size, model_width)
    out_gather = Gather(grid, out_flat)
    out_gather.finish(over=2)
    out_all = out_gather.joined()
    centroid = jnp.where(parity == core, centroids[0], grid.over_core(centroids[0]))

    slots = token_slots(
        routes, fill_order, lengths, seq_len, capacity, padded, experts * padded
    )
    slot = slots.reshape(tok_count, 1)
    rank = slot % padded
    slot_device = (rank // share) * 2 + (slot // padded) % 2
    slot_place = (slot_device * depth + slot // (2 * padded)) * share + rank % share
    place = jnp.where(slot < experts * padded, slot_place, -1)
    own_first = (parity * padded + part * share).astype(jnp.int32).reshape(1)

    def to_experts(rows):
        picked = pick_rows(rows, slots, own_first, depth, share, CORES, padded)
        return grid.exchange_depth(picked.reshape(depth, share, model_width)).reshape(own_rows, model_width)

    def leave_experts(rows):
        return grid.exchange_depth(rows.reshape(depth, share, model_width))

    def row_starts(gathered):
        return jnp.stack([device * own_rows for device in gathered.devices]).astype(jnp.int32)

    grad_ret = to_experts(cotangent).astype(F32)
    heads = heads_here + heads_here % 2
    fused = qkv_weight.reshape(model_width, heads_here, 3, head_size)
    fused = jnp.swapaxes(fused, 1, 2)
    fused = jnp.pad(fused, ((0, 0), (0, 0), (0, heads - heads_here), (0, 0)))
    fused = fused.reshape(model_width, 3 * heads * head_size)
    inner = heads_here * head_size
    ln_in, projected = norm_project(tokens, norm_gain, norm_bias, fused)
    near[0] = after(near[0], projected)
    attended, log_total = attend(projected, lengths, seq_count, heads, head_size)
    near[1:] = [after(piece, attended) for piece in near[1:]]
    win, wout = [fetch_hidden(grid, w) for w in near[::2]], [fetch_hidden(grid, w) for w in near[1::2]]
    if shards == 4:
        gathered = Gather(grid, attended)
        pieces = gathered.finish()
        first = jnp.stack(gathered.devices).astype(jnp.int32)
    else:
        every = lax.all_gather(attended[:, :inner], "tensor", axis=1, tiled=True)
        pieces, first = [every], jnp.zeros((1,), jnp.int32)
    sent = out_project(pieces, first, out_all, tokens)

    expert_rows = to_experts(sent)
    gate = jax.nn.sigmoid(jnp.dot(expert_rows, centroid, preferred_element_type=F32))[:, None]
    current = expert_rows.astype(F32)
    saved = []
    for k in range(2):
        here = current.astype(BF16)
        there = grid.over_core(here)
        act, slope, total = expert_forward(here, win[k], wout[k], current)
        act_there, slope_there, part = expert_forward(there, win[k], wout[k])
        current = total + grid.over_core(part).astype(F32)
        saved.append(([here, there], [act, act_there], [slope, slope_there]))
    returned = leave_experts((gate * current).astype(BF16))

    grad_gate = jnp.sum(grad_ret * current, axis=1, keepdims=True)
    grad_logit = grad_gate * gate * (1.0 - gate)
    grad_current = gate * grad_ret
    branches = [None, None]
    for k in (1, 0):
        slopes = saved[k][2]
        here = grad_current.astype(BF16)
        there = grid.over_core(here)
        grad_pre_there, part = expert_backward(there, slopes[1], win[k], wout[k])
        grad_pre, total = expert_backward(here, slopes[0], win[k], wout[k], grad_current)
        grad_current = total + grid.over_core(part).astype(F32)
        branches[k] = ([here, there], [grad_pre, grad_pre_there])
    grad_rows = (grad_current + grad_logit * centroid.astype(F32)[None, :]).astype(BF16)
    centroid_part = jnp.sum(grad_logit * expert_rows.astype(F32), axis=0, keepdims=True)
    centroid_parts = grid.sum_tensor(
        jnp.concatenate([jnp.where(parity == p, centroid_part, 0.0) for p in range(2)], axis=0)
    )
    centroid_other = grid.over_core(centroid_parts)
    grad_centroid = lax.dynamic_slice_in_dim(centroid_parts + centroid_other, core, 1, 0)

    moved = leave_experts(grad_rows)
    outers = []
    for k in (1, 0):
        rows_in, acts, unused = saved[k]
        branch, grad_pres = branches[k]
        blocks = win[k].shape[0]
        outers += [outer(rows_in, grad_pres, blocks), outer(acts, branch, blocks)]
    sums_in2, sums_back2 = [sum_hidden(grid, pieces) for pieces in outers[:2]]
    moved = after(moved, *outers, centroid_other)
    grad_gather = Gather(grid, moved.reshape(own_rows, model_width))
    sums_in1, sums_back1 = [
        sum_hidden(grid, after(pieces, *grad_gather.ready())) for pieces in outers[2:]
    ]
    pieces = grad_gather.finish()
    first = row_starts(grad_gather)
    out_padded = jnp.pad(out_flat, ((0, heads * head_size - inner), (0, 0)))
    grad_mixed, grad_attended = combine(pieces, first, place, cotangent, out_padded)
    back_in2 = return_hidden(grid, after(sums_in2, *pieces[1:]))
    back_out2 = return_hidden(grid, after(sums_back2, *pieces[1:]))
    out_gather = Gather(grid, after(returned, *pieces[1:]).reshape(own_rows, model_width))
    grad_projected = attend_back(
        projected,
        attended,
        grad_attended,
        log_total,
        lengths,
        seq_count,
        heads,
        head_size,
    )
    grad_ln_part = dot(grad_projected, fused, ((1,), (1,))).astype(BF16)
    grad_ln_part, grad_mixed, grad_projected = together(
        grad_ln_part, grad_mixed, grad_projected, back_in2, back_out2, sums_in1, sums_back1, *out_gather.ready()
    )[:3]
    grad_out_local = dot(attended[:, :inner], grad_mixed, ((0,), (0,))).reshape(
        heads_here, head_size, model_width
    )
    grad_qkv_local = dot(ln_in, grad_projected, ((0,), (0,)))
    grad_sums = (grad_qkv_local.astype(BF16), grad_out_local.astype(BF16))
    grad_ln, scattered, grad_sums = scatter_rows(
        grid, grad_ln_part.reshape(shards, tok_rows, model_width), grad_sums
    )
    grad_sums = lax.psum(grad_sums, "dp")
    scattered = scattered + [grad_projected]
    out_pieces = out_gather.finish(*scattered, over=2)

    def own(rows):
        return lax.dynamic_slice_in_dim(rows, me * tok_rows, tok_rows, 0)

    own_tokens = own(tokens).astype(F32)
    centre = own_tokens - jnp.mean(own_tokens, axis=1, keepdims=True)
    own_scale = lax.rsqrt(jnp.mean(centre * centre, axis=1, keepdims=True) + EPSILON)
    own_normed = centre * own_scale
    grad_normed = grad_ln * norm_gain
    mean_plain = jnp.mean(grad_normed, axis=1, keepdims=True)
    mean_cross = jnp.mean(grad_normed * own_normed, axis=1, keepdims=True)
    grad_input = own(grad_mixed).astype(F32) + own_scale * (
        grad_normed - mean_plain - own_normed * mean_cross
    )
    grad_tokens, halfway, gathered = gather_rows(grid, grad_input.astype(BF16))
    output = combine(out_pieces, first, place, after(sent, *scattered))[0]
    norm_total = jnp.stack([jnp.sum(grad_ln * own_normed, axis=0), jnp.sum(grad_ln, axis=0)])
    norm_total = grid.sum_tensor(after(norm_total, *halfway))
    back_in1 = return_hidden(grid, after(sums_in1, *halfway))
    back_out1 = return_hidden(grid, after(sums_back1, *halfway))
    norm_total = grid.sum_dp(after(norm_total, output))
    norm_total = lax.dynamic_slice_in_dim(
        norm_total, me * (model_width // shards), model_width // shards, 1
    )
    grad_qkv, grad_out_weight = [after(total, *gathered) for total in grad_sums]
    grad_qkv = grad_qkv.astype(F32).reshape(model_width, 3, heads, head_size)[:, :, :heads_here]
    grad_qkv_weight = jnp.swapaxes(grad_qkv, 1, 2).reshape(model_width, heads_here, 3 * head_size)
    return (
        output,
        grad_tokens,
        norm_total[0],
        norm_total[1],
        grad_qkv_weight,
        grad_out_weight.astype(F32),
        grad_centroid,
        jnp.stack([back_in1, back_in2])[None].astype(F32),
        jnp.stack([back_out1, back_out2])[None].astype(F32),
    )


def solution(mesh):
    return jax.shard_map(
        body,
        mesh=mesh,
        in_specs=(
            P("dp", None),
            P("dp"),
            P("dp", None),
            P("dp", None),
            P(),
            P(),
            P(None, "tensor", None),
            P("tensor", None, None),
            P("dp", None),
            P("dp", None, None, "tensor"),
            P("dp", None, "tensor", None),
            P("dp", None),
        ),
        out_specs=(
            P("dp", None),
            P("dp", None),
            P("tensor"),
            P("tensor"),
            P(None, "tensor", None),
            P("tensor", None, None),
            P("dp", None),
            P("dp", None, None, "tensor"),
            P("dp", None, "tensor", None),
        ),
        check_vma=False,
    )
```
